32 devices in a mesh: dp: 8 (over y, x, core), sp: 4 (over z).
Axes of the slice: x: 2, y: 2, z: 4, core: 2. Of those that a mesh axis runs over, the one named last changes fastest.
Arguments:
- hidden_in: bfloat16 [32, 1024, 768], P('dp', 'sp'), may hold values from -6 to 6
- time_embed: bfloat16 [32, 128], P('dp'), may hold values from -6 to 6
- ada_weight: bfloat16 [128, 4608], replicated, may hold values from -0.25 to 0.25
- ada_bias: bfloat16 [4608], replicated, may hold values from -1.5 to 1.5
- attn_gain: bfloat16 [768], replicated, may hold values from 0.25 to 1.75
- query_key_value_matrix: bfloat16 [768, 2304], replicated, may hold values from -0.21875 to 0.21875
- attention_output_matrix: bfloat16 [768, 768], replicated, may hold values from -1.75 to 1.75
- mlp_gain: bfloat16 [768], replicated, may hold values from 0.25 to 1.75
- up_projection_matrix: bfloat16 [768, 3072], replicated, may hold values from -0.21875 to 0.21875
- up_bias: bfloat16 [3072], replicated, may hold values from -3 to 3
- down_projection_matrix: bfloat16 [3072, 768], replicated, may hold values from -0.109375 to 0.109375
- down_bias: bfloat16 [768], replicated, may hold values from -3 to 3
- out_cotangent: bfloat16 [32, 1024, 768], P('dp', 'sp'), may hold values from -6 to 6
Outputs:
- output: bfloat16 [32, 1024, 768], P('dp', 'sp')
- hidden_grad: float32 [32, 1024, 768], P('dp', 'sp')
- time_grad: float32 [32, 128], P('dp')
- ada_weight_grad: float32 [128, 4608], P('sp')
- ada_bias_grad: float32 [4608], P('sp')
- attn_gain_grad: float32 [768], P('sp')
- qkv_weight_grad: float32 [768, 2304], P('sp')
- proj_weight_grad: float32 [768, 768], P('sp')
- mlp_gain_grad: float32 [768], P('sp')
- up_weight_grad: float32 [768, 3072], P('sp')
- up_bias_grad: float32 [3072], P('sp')
- down_weight_grad: float32 [3072, 768], P('sp')
- down_bias_grad: float32 [768], P('sp')
The draws below stay inside these ranges and needn't reach their ends.
All inputs are finite; a program needn't handle non-finite values.
Results may differ from the reference program's by a relative error of at most 0.012.
The reference program's roundings to bfloat16 on the way count: a program that leaves them out, or rounds other values in their place, can miss the bound.
Values may be sent and summed in bfloat16 or wider, within the bound.
No kernel may reach another device: no remote copies, remote signals or barrier semaphores. Data moves between devices by JAX's collectives and lax.ppermute only.
A program may use at most 192 MiB of HBM per device.

```python
import math
import jax
import jax.numpy as jnp
from jax import lax

D = 768
HEADS = 12
HEAD_DIM = 64
FF = 3072
COND = 128
SEQ_LEN = 1024
BATCH = 32


def block_levels(own_key, extent, pieces, least, largest):
    gain = 1.0
    for dim, parts in pieces:
        heights = jax.random.uniform(jax.random.fold_in(jax.random.fold_in(own_key, 6), dim), (parts,), jnp.float32, least / len(pieces), largest / len(pieces))
        gain = gain * jnp.repeat(jnp.exp(heights), extent[dim] // parts).reshape((-1,) + (1,) * (len(extent) - 1 - dim))
    return gain


def bell_draw(own_key, shape, scale, most, cuts=(), held_as=jnp.bfloat16):
    array = scale * jax.random.normal(own_key, shape, jnp.float32)
    if cuts:
        array = array * block_levels(own_key, shape, cuts, -0.22, 0.18)
    return jnp.clip(array, -most, most).astype(held_as)


def setup_inputs(seed: int = 0) -> dict:
    splits = jax.random.split(jax.random.key(seed), 14)
    return {
        "hidden_in": bell_draw(splits[0], (BATCH, SEQ_LEN, D), 1.0, 6.0, ((0, 8), (1, 4))),
        "time_embed": bell_draw(splits[1], (BATCH, COND), 1.0, 6.0, ((0, 8),)),
        "ada_weight": bell_draw(splits[2], (COND, 6 * D), (4 * COND) ** -0.5, 0.25),
        "ada_bias": bell_draw(splits[3], (6 * D,), 0.25, 1.5),
        "attn_gain": jnp.clip(1.0 + 0.15 * jax.random.normal(splits[4], (D,), jnp.float32), 0.25, 1.75).astype(jnp.bfloat16),
        "query_key_value_matrix": bell_draw(splits[5], (D, 3 * D), D ** -0.5, 0.21875),
        "attention_output_matrix": bell_draw(splits[6], (D, D), (D // 64) ** -0.5, 1.75),
        "mlp_gain": jnp.clip(1.0 + 0.15 * jax.random.normal(splits[7], (D,), jnp.float32), 0.25, 1.75).astype(jnp.bfloat16),
        "up_projection_matrix": bell_draw(splits[8], (D, FF), D ** -0.5, 0.21875),
        "up_bias": bell_draw(splits[9], (FF,), 0.5, 3.0),
        "down_projection_matrix": bell_draw(splits[10], (FF, D), FF ** -0.5, 0.109375),
        "down_bias": bell_draw(splits[11], (D,), 0.5, 3.0),
        "out_cotangent": bell_draw(splits[12], (BATCH, SEQ_LEN, D), 1.0, 6.0, ((0, 8), (1, 4))),
    }


highest = lax.Precision.HIGHEST
epsilon = 1e-05

@jax.custom_vjp
def low(v):
    return lax.optimization_barrier(v.astype(jnp.bfloat16)).astype(jnp.float32)

@jax.custom_vjp
def low_back(v):
    return v

def low_keep(v):
    return (low(v), None)

def low_pass(kept, grad):
    return (grad,)

def back_keep(v):
    return (v, None)

def back_low(kept, grad):
    return (low(grad),)
low.defvjp(low_keep, low_pass)
low_back.defvjp(back_keep, back_low)

def rope_tables(length, columns):
    half_width = columns // 2
    frequency = 10000.0 ** (-(jnp.arange(half_width, dtype=jnp.float32) * 2.0 / columns))
    angles = jnp.arange(length, dtype=jnp.float32)[:, None] * frequency[None, :]
    cos_table = jnp.cos(angles)
    sin_table = jnp.sin(angles)
    return (jnp.concatenate([cos_table, cos_table], axis=-1), jnp.concatenate([sin_table, sin_table], axis=-1))

def rotary(values, cos_table, sin_table):
    half_width = values.shape[-1] // 2
    turned = jnp.concatenate([-values[..., half_width:], values[..., :half_width]], axis=-1)
    return values * cos_table + turned * sin_table

def layer_norm(values):
    center = values - lax.optimization_barrier(jnp.mean(values, axis=-1, keepdims=True))
    inverse = lax.rsqrt(lax.optimization_barrier(jnp.mean(center * center, axis=-1, keepdims=True)) + epsilon)
    return center * inverse

def one_head(operands):
    queries, rotated_keys, values = operands
    scores = low_back(jnp.einsum('gqd,gkd->gqk', queries, rotated_keys, precision=highest) * HEAD_DIM ** (-0.5))
    probabilities = low(jax.nn.softmax(scores, axis=-1))
    return jnp.einsum('gqk,gkd->gqd', probabilities, values, precision=highest)

def forward_block(hidden, timing, ada_weight, ada_bias, attn_gain, query_key_value_matrix, attention_output_matrix, mlp_gain, up_projection_matrix, up_bias, down_projection_matrix, down_bias):
    group_size, length, width = hidden.shape
    modulation = jnp.dot(timing, ada_weight, precision=highest) + ada_bias
    shift_attn, scale_attn, gate_attn, shift_mlp, scale_mlp, gate_mlp = jnp.split(modulation[:, None, :], 6, axis=-1)
    attention_modulated_input = low(layer_norm(hidden) * attn_gain * (1.0 + scale_attn) + shift_attn)
    qkv = low(low_back(jnp.einsum('gld,de->gle', attention_modulated_input, query_key_value_matrix, precision=highest)))
    qkv = qkv.reshape(group_size, length, 3, HEADS, HEAD_DIM)
    cos_table, sin_table = rope_tables(length, HEAD_DIM)
    cos_table = cos_table[:, None, :]
    sin_table = sin_table[:, None, :]
    queries = low(rotary(qkv[:, :, 0], cos_table, sin_table))
    rotated_keys = low(rotary(qkv[:, :, 1], cos_table, sin_table))
    values = qkv[:, :, 2]
    heads_first = (jnp.moveaxis(queries, 2, 0), jnp.moveaxis(rotated_keys, 2, 0), jnp.moveaxis(values, 2, 0))
    mixed = lax.map(jax.checkpoint(one_head), heads_first)
    mixed = jnp.moveaxis(mixed, 0, 2).reshape(group_size, length, width)
    mixed = low(low_back(mixed))
    projected = low_back(jnp.einsum('gld,de->gle', mixed, attention_output_matrix, precision=highest))
    middle = hidden + gate_attn * projected
    feedforward_modulated_input = low(layer_norm(middle) * mlp_gain * (1.0 + scale_mlp) + shift_mlp)
    pre_act = low_back(jnp.einsum('gld,df->glf', feedforward_modulated_input, up_projection_matrix, precision=highest) + up_bias)
    gelu_activation = low(jax.nn.gelu(pre_act, approximate=True))
    down_out = low_back(jnp.einsum('glf,fd->gld', gelu_activation, down_projection_matrix, precision=highest) + down_bias)
    return middle + gate_mlp * down_out

def reference(hidden_in, time_embed, ada_weight, ada_bias, attn_gain, query_key_value_matrix, attention_output_matrix, mlp_gain, up_projection_matrix, up_bias, down_projection_matrix, down_bias, out_cotangent):
    group_size = math.gcd(BATCH, 4)
    blocks = BATCH // group_size
    hidden = hidden_in.astype(jnp.float32).reshape(blocks, group_size, SEQ_LEN, D)
    timing = time_embed.astype(jnp.float32).reshape(blocks, group_size, COND)
    cotangent = out_cotangent.astype(jnp.float32).reshape(blocks, group_size, SEQ_LEN, D)
    weights = (ada_weight.astype(jnp.float32), ada_bias.astype(jnp.float32), attn_gain.astype(jnp.float32), query_key_value_matrix.astype(jnp.float32), attention_output_matrix.astype(jnp.float32), mlp_gain.astype(jnp.float32), up_projection_matrix.astype(jnp.float32), up_bias.astype(jnp.float32), down_projection_matrix.astype(jnp.float32), down_bias.astype(jnp.float32))

    def block_step(totals, block_in):
        hidden_part, timing_part, cotangent_part = block_in
        result, pullback = jax.vjp(forward_block, hidden_part, timing_part, *weights)
        gradients = pullback(cotangent_part)
        totals = tuple((total + grad_part for total, grad_part in zip(totals, gradients[2:])))
        return (totals, (result, gradients[0], gradients[1]))
    zeros_init = tuple((jnp.zeros_like(weight_one) for weight_one in weights))
    totals, (results, hidden_grads, time_grads) = lax.scan(block_step, zeros_init, (hidden, timing, cotangent))
    return (results.reshape(BATCH, SEQ_LEN, D).astype(jnp.bfloat16), hidden_grads.reshape(BATCH, SEQ_LEN, D), time_grads.reshape(BATCH, COND), totals[0], totals[1], totals[2], totals[3], totals[4], totals[5], totals[6], totals[7], totals[8], totals[9])
```

```python
import functools

import jax
import jax.numpy as jnp
from jax import lax
from jax.experimental import pallas as pl
from jax.experimental.pallas import tpu as pltpu
from jax.sharding import PartitionSpec as P

HEAD_DIM = 64
HALF = HEAD_DIM // 2
LANES = 128
EPSILON = 1e-05
LOG2E = 1.4426950408889634
SCALE = HEAD_DIM ** (-0.5)
f32 = jnp.float32
bf16 = jnp.bfloat16


def dot_nn(a, b):
    return lax.dot_general(a, b, (((1,), (0,)), ((), ())), preferred_element_type=f32)


def dot_nt(a, b):
    return lax.dot_general(a, b, (((1,), (1,)), ((), ())), preferred_element_type=f32)


def dot_tn(a, b):
    return lax.dot_general(a, b, (((0,), (0,)), ((), ())), preferred_element_type=f32)


def column_sum(values):
    return jnp.sum(values, axis=0, keepdims=True)


def norm_forward(values):
    center = values - jnp.mean(values, axis=-1, keepdims=True)
    inverse = lax.rsqrt(jnp.mean(center * center, axis=-1, keepdims=True) + EPSILON)
    return center * inverse, inverse


def norm_backward(grad, normed, inverse):
    first = jnp.mean(grad, axis=-1, keepdims=True)
    second = jnp.mean(grad * normed, axis=-1, keepdims=True)
    return inverse * (grad - first - normed * second)


def swap_halves(values):
    lane = lax.broadcasted_iota(jnp.int32, (1, LANES), 1)
    lower = (lane & (HEAD_DIM - 1)) < HALF
    up = pltpu.roll(values, LANES - HALF, 1)
    down = pltpu.roll(values, HALF, 1)
    return lower, up, down


def rotary(values, cos, sin):
    lower, up, down = swap_halves(values)
    return values * cos + jnp.where(lower, -up, down) * sin


def unrotary(values, cos, sin):
    lower, up, down = swap_halves(values * sin)
    return values * cos + jnp.where(lower, up, -down)


def qkv_kernel(x_ref, mod_ref, w_ref, cos_ref, sin_ref, xm_ref, q_ref, k_ref, v_ref):
    width = x_ref.shape[1]
    normed, _ = norm_forward(x_ref[...].astype(f32))
    xm = (normed * mod_ref[0:1, :] + mod_ref[1:2, :]).astype(bf16)
    xm_ref[...] = xm
    cos, sin = cos_ref[...], sin_ref[...]
    for part, ref in enumerate((q_ref, k_ref, v_ref)):
        whole = dot_nn(xm, w_ref[:, part * width : (part + 1) * width]).astype(bf16)
        if part == 2:
            ref[...] = whole
            continue
        for lane in range(0, width, LANES):
            piece = whole[:, lane : lane + LANES].astype(f32)
            ref[:, lane : lane + LANES] = rotary(piece, cos, sin).astype(bf16)


def project_qkv(x, mods, weight, cos, sin, rows=256):
    length, width = x.shape
    block = pl.BlockSpec((rows, width), lambda i: (i, 0))
    table = pl.BlockSpec((rows, LANES), lambda i: (i, 0))
    shape = jax.ShapeDtypeStruct((length, width), bf16)
    return pl.pallas_call(
        qkv_kernel,
        grid=(length // rows,),
        in_specs=[
            block,
            pl.BlockSpec(mods.shape, lambda i: (0, 0)),
            pl.BlockSpec(weight.shape, lambda i: (0, 0)),
            table,
            table,
        ],
        out_specs=[block] * 4,
        out_shape=[shape] * 4,
        cost_estimate=pl.CostEstimate(
            flops=6 * length * width * width, bytes_accessed=16_000_000, transcendentals=0
        ),
        name="project_qkv",
    )(x, mods, weight, cos, sin)


def attention_forward_kernel(q_ref, k_ref, v_ref, o_ref, lse_ref):
    q, k, v = q_ref[...], k_ref[...], v_ref[...]
    first = lax.broadcasted_iota(jnp.int32, (1, LANES), 1) < HEAD_DIM
    c = LOG2E * SCALE
    outs = []
    for h in range(2):
        mine = first if h == 0 else ~first
        kh = jnp.where(mine, k, jnp.zeros_like(k))
        st = dot_nt(kh, q)
        top = jnp.max(st, axis=0, keepdims=True) * c
        p = jnp.exp2(st * c - top).astype(bf16)
        ot = dot_tn(jnp.where(mine, v, jnp.ones_like(v)), p)
        own, ones = (ot[:HEAD_DIM], ot[HEAD_DIM:]) if h == 0 else (ot[HEAD_DIM:], ot[:HEAD_DIM])
        total = ones[0:1]
        outs.append(own * (1.0 / total))
        lse_ref[0, h : h + 1, :] = top + jnp.log2(total)
    o_ref[...] = jnp.concatenate(outs, axis=0).T.astype(bf16)


def attention_forward(q, k, v):
    length, width = q.shape
    pairs = width // LANES
    block = pl.BlockSpec((length, LANES), lambda i: (0, i))
    return pl.pallas_call(
        attention_forward_kernel,
        grid=(pairs,),
        in_specs=[block] * 3,
        out_specs=[block, pl.BlockSpec((1, 2, length), lambda i: (i, 0, 0))],
        out_shape=[
            jax.ShapeDtypeStruct((length, width), bf16),
            jax.ShapeDtypeStruct((pairs, 2, length), f32),
        ],
        cost_estimate=pl.CostEstimate(
            flops=16 * length * length * width,
            bytes_accessed=8 * length * width,
            transcendentals=length * length * width // HEAD_DIM,
        ),
        name="attention_forward",
    )(q, k, v)


def attention_backward_kernel(
    q_ref, k_ref, v_ref, do_ref, o_ref, lse_ref, cos_ref, sin_ref, dq_ref, dk_ref, dv_ref
):
    first = lax.broadcasted_iota(jnp.int32, (1, LANES), 1) < HEAD_DIM
    upper = lax.broadcasted_iota(jnp.int32, (LANES, 1), 0) < HEAD_DIM
    c = LOG2E * SCALE
    q, k, v, do = q_ref[...], k_ref[...], v_ref[...], do_ref[...]
    prod = (do.astype(f32) * o_ref[...].astype(f32)).T
    kt = k.T
    zero = jnp.zeros_like(k)
    dq = dk = dv = None
    for h in range(2):
        mine = first if h == 0 else ~first
        row = column_sum(prod[h * HEAD_DIM : (h + 1) * HEAD_DIM])
        st = dot_nt(jnp.where(mine, k, zero), q)
        p = jnp.exp2(st * c - lse_ref[0, h : h + 1, :])
        dp = dot_nt(jnp.where(mine, v, zero), do)
        ds = (p * (dp - row)).astype(bf16)
        dvh = dot_nn(p.astype(bf16), jnp.where(mine, do, zero))
        dkh = dot_nn(ds, jnp.where(mine, q, zero))
        dqh = dot_nn(jnp.where(upper if h == 0 else ~upper, kt, jnp.zeros_like(kt)), ds)
        dq, dk, dv = (dqh, dkh, dvh) if h == 0 else (dq + dqh, dk + dkh, dv + dvh)
    cos, sin = cos_ref[...], sin_ref[...]
    dv_ref[...] = dv.astype(bf16)
    dk_ref[...] = unrotary(dk * SCALE, cos, sin).astype(bf16)
    dq_ref[...] = unrotary(dq.T * SCALE, cos, sin).astype(bf16)


def attention_backward(q, k, v, do, o, lse, cos, sin):
    length, width = q.shape
    pairs = width // LANES
    block = pl.BlockSpec((length, LANES), lambda i: (0, i))
    table = pl.BlockSpec((length, LANES), lambda i: (0, 0))
    return pl.pallas_call(
        attention_backward_kernel,
        grid=(pairs,),
        in_specs=[block] * 5
        + [pl.BlockSpec((1, 2, length), lambda i: (i, 0, 0)), table, table],
        out_specs=[block] * 3,
        out_shape=[jax.ShapeDtypeStruct((length, width), bf16)] * 3,
        cost_estimate=pl.CostEstimate(
            flops=40 * length * length * width,
            bytes_accessed=16 * length * width,
            transcendentals=length * length * width // HEAD_DIM,
        ),
        name="attention_backward",
    )(q, k, v, do, o, lse, cos, sin)


def mlp_kernel(
    x_ref, mixed_ref, cot_ref, mod_ref, bias_ref, wo_ref, wu_ref, wd_ref,
    out_ref, xm_ref, act_ref, gd_ref, gp_ref, gm_ref, gpj_ref, gmix_ref, sum_ref, up_sum_ref,
    *, chunk,
):
    ff = wu_ref.shape[1]
    gate_attn, scaled, shift = mod_ref[0:1, :], mod_ref[1:2, :], mod_ref[2:3, :]
    gate_mlp, down_bias = mod_ref[3:4, :], mod_ref[4:5, :]
    cot = cot_ref[...].astype(f32)
    projected = dot_nn(mixed_ref[...], wo_ref[...])
    middle = x_ref[...].astype(f32) + gate_attn * projected
    normed, inverse = norm_forward(middle)
    xm = (normed * scaled + shift).astype(bf16)
    xm_ref[...] = xm
    gd = (gate_mlp * cot).astype(bf16)
    gd_ref[...] = gd
    down = grad_mod = None
    c0 = 0.7978845608028654
    c1 = c0 * 0.044715
    up_sums = []
    for at in range(0, ff, chunk):
        cols = slice(at, at + chunk)
        pre = dot_nn(xm, wu_ref[:, cols]) + bias_ref[:, cols]
        square = pre * pre
        t = jnp.tanh(pre * (c0 + c1 * square))
        half = 0.5 + 0.5 * t
        act = (pre * half).astype(bf16)
        act_ref[:, cols] = act
        slope = half + (0.5 * pre) * (1.0 - t * t) * (c0 + (3.0 * c1) * square)
        gp = (slope * dot_nt(gd, wd_ref[cols, :])).astype(bf16)
        gp_ref[:, cols] = gp
        up_sums.append(column_sum(gp.astype(f32)))
        d = dot_nn(act, wd_ref[cols, :])
        g = dot_nt(gp, wu_ref[:, cols])
        down, grad_mod = (d, g) if down is None else (down + d, grad_mod + g)
    down = down + down_bias
    out_ref[...] = (middle + gate_mlp * down).astype(bf16)
    gm = cot + norm_backward(grad_mod * scaled, normed, inverse)
    gm_ref[...] = gm
    gpj = (gate_attn * gm).astype(bf16)
    gpj_ref[...] = gpj
    gmix_ref[...] = dot_nt(gpj, wo_ref[...]).astype(bf16)
    sums = jnp.concatenate(
        [
            column_sum(cot * down),
            column_sum(gd.astype(f32)),
            column_sum(grad_mod),
            column_sum(grad_mod * normed),
            column_sum(gm * projected),
            jnp.zeros((3, cot.shape[1]), f32),
        ],
        axis=0,
    )
    up_sum = jnp.concatenate(up_sums, axis=1)

    @pl.when(pl.program_id(0) == 0)
    def _():
        sum_ref[...] = sums
        up_sum_ref[...] = up_sum

    @pl.when(pl.program_id(0) > 0)
    def _():
        sum_ref[...] += sums
        up_sum_ref[...] += up_sum


def feed_forward(x, mixed, cot, mods, up_bias, wo, wu, wd, rows=256, chunk=768):
    length, width = x.shape
    ff = wu.shape[1]
    block = pl.BlockSpec((rows, width), lambda i: (i, 0))
    wide = pl.BlockSpec((rows, ff), lambda i: (i, 0))

    def whole(a):
        return pl.BlockSpec(a.shape, lambda i: (0, 0), pipeline_mode=pl.Buffered(1))

    narrow = jax.ShapeDtypeStruct((length, width), bf16)
    broad = jax.ShapeDtypeStruct((length, ff), bf16)
    return pl.pallas_call(
        functools.partial(mlp_kernel, chunk=chunk),
        grid=(length // rows,),
        in_specs=[block, block, block] + [whole(a) for a in (mods, up_bias, wo, wu, wd)],
        out_specs=[block, block, wide, block, wide, block, block, block]
        + [pl.BlockSpec((8, width), lambda i: (0, 0)), pl.BlockSpec((1, ff), lambda i: (0, 0))],
        out_shape=[
            narrow, narrow, broad, narrow, broad,
            jax.ShapeDtypeStruct((length, width), f32), narrow, narrow,
            jax.ShapeDtypeStruct((8, width), f32), jax.ShapeDtypeStruct((1, ff), f32),
        ],
        cost_estimate=pl.CostEstimate(
            flops=8 * length * width * ff + 4 * length * width * width,
            bytes_accessed=40_000_000,
            transcendentals=length * ff,
        ),
        name="feed_forward",
    )(x, mixed, cot, mods, up_bias, wo, wu, wd)


def input_grad_kernel(x_ref, gq_ref, gk_ref, gv_ref, gm_ref, mod_ref, w_ref, hg_ref, sum_ref):
    width = x_ref.shape[1]
    normed, inverse = norm_forward(x_ref[...].astype(f32))
    grad = None
    for part, ref in enumerate((gq_ref, gk_ref, gv_ref)):
        g = dot_nt(ref[...], w_ref[:, part * width : (part + 1) * width])
        grad = g if grad is None else grad + g
    hg_ref[...] = (
        gm_ref[...] + norm_backward(grad * mod_ref[0:1, :], normed, inverse)
    ).astype(bf16)
    sums = jnp.concatenate(
        [column_sum(grad), column_sum(grad * normed), jnp.zeros((6, width), f32)], axis=0
    )

    @pl.when(pl.program_id(0) == 0)
    def _():
        sum_ref[...] = sums

    @pl.when(pl.program_id(0) > 0)
    def _():
        sum_ref[...] += sums


def input_grad(x, gq, gk, gv, gm, mods, weight, rows=256):
    length, width = x.shape
    block = pl.BlockSpec((rows, width), lambda i: (i, 0))
    return pl.pallas_call(
        input_grad_kernel,
        grid=(length // rows,),
        in_specs=[block] * 5
        + [
            pl.BlockSpec(mods.shape, lambda i: (0, 0)),
            pl.BlockSpec(weight.shape, lambda i: (0, 0), pipeline_mode=pl.Buffered(1)),
        ],
        out_specs=[block, pl.BlockSpec((8, width), lambda i: (0, 0))],
        out_shape=[
            jax.ShapeDtypeStruct((length, width), bf16),
            jax.ShapeDtypeStruct((8, width), f32),
        ],
        cost_estimate=pl.CostEstimate(
            flops=6 * length * width * width, bytes_accessed=16_000_000, transcendentals=0
        ),
        name="input_grad",
    )(x, gq, gk, gv, gm, mods, weight)


def shift_permute(value, axis, by):
    n = lax.axis_size(axis)
    return lax.ppermute(value, axis, [(i, (i + by) % n) for i in range(n)])


def pair_permute(value, axis, bit):
    n = lax.axis_size(axis)
    return lax.ppermute(value, axis, [(i, i ^ bit) for i in range(n)])


def pick(values, index, axis=0):
    return lax.dynamic_index_in_dim(values, index, axis, keepdims=False)


def to_sequences(values):
    n, me = lax.axis_size("sp"), lax.axis_index("sp")
    blocks = [pick(values, me)]
    for d in range(1, n):
        blocks.append(shift_permute(pick(values, (me + d) % n), "sp", d))
    return jnp.concatenate(blocks, axis=0)


def from_sequences(values, length):
    n, me = lax.axis_size("sp"), lax.axis_index("sp")
    result = jnp.zeros((n, length, values.shape[1]), values.dtype)
    for d in range(n):
        block = values[d * length : (d + 1) * length]
        if d:
            block = shift_permute(block, "sp", -d)
        result = lax.dynamic_update_index_in_dim(result, block, (me + d) % n, 0)
    return result


def dp_bits(order):
    n = lax.axis_size("dp")
    bits = [1 << b for b in range(n.bit_length() - 1)]
    first, rest = bits[:1], bits[1:]
    return first + (rest[::-1] if order else rest)


def reduce_weight(grad, order):
    rows, columns = grad.shape
    sp, me = lax.axis_size("sp"), lax.axis_index("sp")
    dp, here = lax.axis_size("dp"), lax.axis_index("dp")
    bits = dp_bits(order)
    piece = rows // (sp * dp)
    current = grad.reshape((sp,) + (2,) * len(bits) + (piece, columns))
    for bit in bits:
        mine = (here // bit) % 2
        other = pair_permute(pick(current, 1 - mine, 1), "dp", bit)
        current = (pick(current, mine, 1).astype(f32) + other.astype(f32)).astype(bf16)
    total = pick(current, me).astype(f32)
    for d in range(1, sp):
        total = total + shift_permute(pick(current, (me + d) % sp), "sp", d).astype(f32)
    gathered = total.astype(bf16)[None]
    for bit in bits[::-1]:
        gathered = jnp.concatenate([gathered, pair_permute(gathered, "dp", bit)], axis=0)
    result = []
    for at in range(dp):
        index = 0
        for place, bit in enumerate(bits[::-1]):
            wanted = (at >> place) & 1
            index = index + ((wanted ^ ((here // bit) % 2)) << place)
        result.append(pick(gathered, index))
    return jnp.concatenate(result, axis=0).astype(f32)


def body(
    hidden_in,
    time_embed,
    ada_weight,
    ada_bias,
    attn_gain,
    query_key_value_matrix,
    attention_output_matrix,
    mlp_gain,
    up_projection_matrix,
    up_bias,
    down_projection_matrix,
    down_bias,
    out_cotangent,
):
    sequences, local_len, width = hidden_in.shape
    sp, me = lax.axis_size("sp"), lax.axis_index("sp")
    assert sequences == sp
    x = to_sequences(hidden_in)
    cot = to_sequences(out_cotangent)

    timing = lax.dynamic_slice_in_dim(time_embed, me, 1, 0)
    modulation = dot_nn(timing, ada_weight) + ada_bias.astype(f32)[None]
    shift_attn, scale_attn, gate_attn, shift_mlp, scale_mlp, gate_mlp = jnp.split(
        modulation, 6, axis=-1
    )
    gain_attn = attn_gain.astype(f32)[None]
    gain_mlp = mlp_gain.astype(f32)[None]
    zero = jnp.zeros_like(shift_attn)
    attn_mods = jnp.concatenate(
        [gain_attn * (1.0 + scale_attn), shift_attn] + [zero] * 6, axis=0
    )
    mlp_mods = jnp.concatenate(
        [gate_attn, gain_mlp * (1.0 + scale_mlp), shift_mlp, gate_mlp, down_bias.astype(f32)[None]]
        + [zero] * 3,
        axis=0,
    )
    lane = lax.broadcasted_iota(jnp.int32, (1, LANES), 1)
    frequency = 10000.0 ** (-((lane % HALF).astype(f32) * 2.0 / HEAD_DIM))
    row = lax.broadcasted_iota(jnp.int32, (sp * local_len, 1), 0)
    position = ((me - row // local_len + sp) % sp) * local_len + row % local_len
    angles = position.astype(f32) * frequency
    cos, sin = jnp.cos(angles), jnp.sin(angles)

    xm_attn, q, k, v = project_qkv(x, attn_mods, query_key_value_matrix, cos, sin)
    mixed, lse = attention_forward(q, k, v)
    out, xm_mlp, act, gd, gp, gm, gpj, gmix, sums, up_sum = feed_forward(
        x,
        mixed,
        cot,
        mlp_mods,
        up_bias.astype(f32)[None],
        attention_output_matrix,
        up_projection_matrix,
        down_projection_matrix,
    )
    output = from_sequences(out, local_len)
    down_grad = reduce_weight(dot_tn(act, gd).astype(bf16), 0)
    up_grad = reduce_weight(dot_tn(xm_mlp, gp).astype(bf16), 1)
    proj_grad = reduce_weight(dot_tn(mixed, gpj).astype(bf16), 0)
    gq, gk, gv = attention_backward(q, k, v, gmix, mixed, lse, cos, sin)
    grad_qkv = jnp.concatenate([gq, gk, gv], axis=1)
    qkv_grad = reduce_weight(dot_tn(xm_attn, grad_qkv).astype(bf16), 1)
    hg, attn_sums = input_grad(x, gq, gk, gv, gm, attn_mods, query_key_value_matrix)
    hidden_grad = from_sequences(hg, local_len).astype(f32)

    grad_modulation = jnp.concatenate(
        [
            attn_sums[0:1],
            attn_sums[1:2] * gain_attn,
            sums[4:5],
            sums[2:3],
            sums[3:4] * gain_mlp,
            sums[0:1],
        ],
        axis=1,
    )
    others = jnp.concatenate(
        [
            attn_sums[1:2] * (1.0 + scale_attn),
            sums[3:4] * (1.0 + scale_mlp),
            up_sum,
            sums[1:2],
        ],
        axis=1,
    )
    cond = timing.shape[1]
    packed = jnp.concatenate(
        [timing, grad_modulation.astype(bf16), others.astype(bf16)], axis=1
    )
    rows_sp = jnp.concatenate(
        [packed] + [shift_permute(packed, "sp", d) for d in range(1, sp)], axis=0
    )
    six = grad_modulation.shape[1]
    time_rows = dot_nt(rows_sp[:, cond : cond + six], ada_weight)
    time_grad = jnp.concatenate([pick(time_rows, (me - s + sp) % sp)[None] for s in range(sp)], axis=0)
    rows_all = rows_sp
    for bit in dp_bits(0):
        rows_all = jnp.concatenate([rows_all, pair_permute(rows_all, "dp", bit)], axis=0)
    cond_here = cond // sp
    own_timing = lax.dynamic_slice_in_dim(rows_all, me * cond_here, cond_here, 1)
    ada_weight_grad = dot_tn(own_timing, rows_all[:, cond : cond + six])
    totals = jnp.sum(rows_all[:, cond:].astype(f32), axis=0)

    def own(start, size):
        return lax.dynamic_slice_in_dim(totals[start : start + size], me * (size // sp), size // sp, 0)

    ff = up_bias.shape[0]
    ada_bias_grad = own(0, six)
    attn_gain_grad = own(six, width)
    mlp_gain_grad = own(six + width, width)
    up_bias_grad = own(six + 2 * width, ff)
    down_bias_grad = own(six + 2 * width + ff, width)
    return (
        output,
        hidden_grad,
        time_grad,
        ada_weight_grad,
        ada_bias_grad,
        attn_gain_grad,
        qkv_grad,
        proj_grad,
        mlp_gain_grad,
        up_grad,
        up_bias_grad,
        down_grad,
        down_bias_grad,
    )


def solution(mesh):
    return jax.shard_map(
        body,
        mesh=mesh,
        in_specs=(P("dp", "sp", None), P("dp", None)) + (P(),) * 10 + (P("dp", "sp", None),),
        out_specs=(
            P("dp", "sp", None),
            P("dp", "sp", None),
            P("dp", None),
            P("sp", None),
            P("sp"),
            P("sp"),
            P("sp", None),
            P("sp", None),
            P("sp"),
            P("sp", None),
            P("sp"),
            P("sp", None),
            P("sp"),
        ),
        check_vma=False,
    )
```

```python
import functools

import jax
import jax.numpy as jnp
from jax import lax
from jax.experimental import pallas as pl
from jax.experimental.pallas import tpu as pltpu
from jax.sharding import PartitionSpec as P

HEAD_DIM = 64
HALF = HEAD_DIM // 2
LANES = 128
EPSILON = 1e-05
LOG2E = 1.4426950408889634
SCALE = HEAD_DIM ** (-0.5)
f32 = jnp.float32
bf16 = jnp.bfloat16


def dot_nn(a, b):
    return lax.dot_general(a, b, (((1,), (0,)), ((), ())), preferred_element_type=f32)


def dot_nt(a, b):
    return lax.dot_general(a, b, (((1,), (1,)), ((), ())), preferred_element_type=f32)


def dot_tn(a, b):
    return lax.dot_general(a, b, (((0,), (0,)), ((), ())), preferred_element_type=f32)


def column_sum(values):
    return jnp.sum(values, axis=0, keepdims=True)


def norm_forward(values):
    center = values - jnp.mean(values, axis=-1, keepdims=True)
    inverse = lax.rsqrt(jnp.mean(center * center, axis=-1, keepdims=True) + EPSILON)
    return center * inverse, inverse


def norm_backward(grad, normed, inverse):
    first = jnp.mean(grad, axis=-1, keepdims=True)
    second = jnp.mean(grad * normed, axis=-1, keepdims=True)
    return inverse * (grad - first - normed * second)


def swap_halves(values):
    lane = lax.broadcasted_iota(jnp.int32, (1, LANES), 1)
    lower = (lane & (HEAD_DIM - 1)) < HALF
    up = pltpu.roll(values, LANES - HALF, 1)
    down = pltpu.roll(values, HALF, 1)
    return lower, up, down


def rotary(values, cos, sin):
    lower, up, down = swap_halves(values)
    return values * cos + jnp.where(lower, -up, down) * sin


def unrotary(values, cos, sin):
    lower, up, down = swap_halves(values * sin)
    return values * cos + jnp.where(lower, up, -down)


def qkv_kernel(x_ref, mod_ref, w_ref, cos_ref, sin_ref, xm_ref, q_ref, k_ref, v_ref):
    width = x_ref.shape[1]
    normed, _ = norm_forward(x_ref[...].astype(f32))
    xm = (normed * mod_ref[0:1, :] + mod_ref[1:2, :]).astype(bf16)
    xm_ref[...] = xm
    cos, sin = cos_ref[...], sin_ref[...]
    for part, ref in enumerate((q_ref, k_ref, v_ref)):
        whole = dot_nn(xm, w_ref[:, part * width : (part + 1) * width]).astype(bf16)
        if part == 2:
            ref[...] = whole
            continue
        for lane in range(0, width, LANES):
            piece = whole[:, lane : lane + LANES].astype(f32)
            ref[:, lane : lane + LANES] = rotary(piece, cos, sin).astype(bf16)


def project_qkv(x, mods, weight, cos, sin, rows=256):
    length, width = x.shape
    block = pl.BlockSpec((rows, width), lambda i: (i, 0))
    table = pl.BlockSpec((rows, LANES), lambda i: (i, 0))
    shape = jax.ShapeDtypeStruct((length, width), bf16)
    return pl.pallas_call(
        qkv_kernel,
        grid=(length // rows,),
        in_specs=[
            block,
            pl.BlockSpec(mods.shape, lambda i: (0, 0)),
            pl.BlockSpec(weight.shape, lambda i: (0, 0)),
            table,
            table,
        ],
        out_specs=[block] * 4,
        out_shape=[shape] * 4,
        cost_estimate=pl.CostEstimate(
            flops=6 * length * width * width, bytes_accessed=16_000_000, transcendentals=0
        ),
        name="project_qkv",
    )(x, mods, weight, cos, sin)


def attention_forward_kernel(q_ref, k_ref, v_ref, o_ref, lse_ref):
    q, k, v = q_ref[...], k_ref[...], v_ref[...]
    first = lax.broadcasted_iota(jnp.int32, (1, LANES), 1) < HEAD_DIM
    c = LOG2E * SCALE
    outs = []
    for h in range(2):
        mine = first if h == 0 else ~first
        kh = jnp.where(mine, k, jnp.zeros_like(k))
        st = dot_nt(kh, q)
        top = jnp.max(st, axis=0, keepdims=True) * c
        p = jnp.exp2(st * c - top).astype(bf16)
        ot = dot_tn(jnp.where(mine, v, jnp.ones_like(v)), p)
        own, ones = (ot[:HEAD_DIM], ot[HEAD_DIM:]) if h == 0 else (ot[HEAD_DIM:], ot[:HEAD_DIM])
        total = ones[0:1]
        outs.append(own * (1.0 / total))
        lse_ref[0, h : h + 1, :] = top + jnp.log2(total)
    o_ref[...] = jnp.concatenate(outs, axis=0).T.astype(bf16)


def attention_forward(q, k, v):
    length, width = q.shape
    pairs = width // LANES
    block = pl.BlockSpec((length, LANES), lambda i: (0, i))
    return pl.pallas_call(
        attention_forward_kernel,
        grid=(pairs,),
        in_specs=[block] * 3,
        out_specs=[block, pl.BlockSpec((1, 2, length), lambda i: (i, 0, 0))],
        out_shape=[
            jax.ShapeDtypeStruct((length, width), bf16),
            jax.ShapeDtypeStruct((pairs, 2, length), f32),
        ],
        cost_estimate=pl.CostEstimate(
            flops=16 * length * length * width,
            bytes_accessed=8 * length * width,
            transcendentals=length * length * width // HEAD_DIM,
        ),
        name="attention_forward",
    )(q, k, v)


def attention_backward_kernel(
    q_ref, k_ref, v_ref, do_ref, o_ref, lse_ref, cos_ref, sin_ref, *rest
):
    g_ref = rest[-1]
    first = lax.broadcasted_iota(jnp.int32, (1, LANES), 1) < HEAD_DIM
    upper = lax.broadcasted_iota(jnp.int32, (LANES, 1), 0) < HEAD_DIM
    c = LOG2E * SCALE
    q, k, v, do = q_ref[...], k_ref[...], v_ref[...], do_ref[...]
    prod = (do.astype(f32) * o_ref[...].astype(f32)).T
    kt = k.T
    zero = jnp.zeros_like(k)
    dq = dk = dv = None
    for h in range(2):
        mine = first if h == 0 else ~first
        row = column_sum(prod[h * HEAD_DIM : (h + 1) * HEAD_DIM])
        st = dot_nt(jnp.where(mine, k, zero), q)
        p = jnp.exp2(st * c - lse_ref[0, h : h + 1, :])
        dp = dot_nt(jnp.where(mine, v, zero), do)
        ds = (p * (dp - row)).astype(bf16)
        dvh = dot_nn(p.astype(bf16), jnp.where(mine, do, zero))
        dkh = dot_nn(ds, jnp.where(mine, q, zero))
        dqh = dot_nn(jnp.where(upper if h == 0 else ~upper, kt, jnp.zeros_like(kt)), ds)
        dq, dk, dv = (dqh, dkh, dvh) if h == 0 else (dq + dqh, dk + dkh, dv + dvh)
    cos, sin = cos_ref[...], sin_ref[...]
    g_ref[0] = unrotary(dq.T * SCALE, cos, sin).astype(bf16)
    g_ref[1] = unrotary(dk * SCALE, cos, sin).astype(bf16)
    g_ref[2] = dv.astype(bf16)


def attention_backward(q, k, v, do, o, lse, cos, sin, start, count, into=None):
    length, width = q.shape
    block = pl.BlockSpec((length, LANES), lambda i: (0, start + i))
    table = pl.BlockSpec((length, LANES), lambda i: (0, 0))
    extra = [] if into is None else [into]
    return pl.pallas_call(
        attention_backward_kernel,
        grid=(count,),
        in_specs=[block] * 5
        + [pl.BlockSpec((1, 2, length), lambda i: (start + i, 0, 0)), table, table]
        + [pl.BlockSpec(memory_space=pl.ANY)] * len(extra),
        out_specs=pl.BlockSpec((3, length, LANES), lambda i: (0, 0, start + i)),
        out_shape=jax.ShapeDtypeStruct((3, length, width), bf16),
        input_output_aliases={8: 0} if extra else {},
        cost_estimate=pl.CostEstimate(
            flops=40 * length * length * LANES * count,
            bytes_accessed=16 * length * LANES * count,
            transcendentals=2 * length * length * count,
        ),
        name="attention_backward",
    )(q, k, v, do, o, lse, cos, sin, *extra)


def store_block(value, refs):
    for d, ref in enumerate(refs):

        @pl.when(pl.program_id(0) == d)
        def _(ref=ref):
            ref[...] = value


def mlp_kernel(
    x_ref, mixed_ref, cot_ref, mod_ref, bias_ref, wo_ref, wu_ref, wd_ref,
    xm_ref, act_ref, gd_ref, gp_ref, gm_ref, gmix_ref, sum_ref, up_sum_ref, *out_refs,
):
    chunk, ff = wu_ref.shape
    gate_attn, scaled, shift = mod_ref[0:1, :], mod_ref[1:2, :], mod_ref[2:3, :]
    gate_mlp, down_bias = mod_ref[3:4, :], mod_ref[4:5, :]
    cot = cot_ref[...].astype(f32)
    projected = dot_nn(mixed_ref[...], wo_ref[...])
    middle = x_ref[...].astype(f32) + gate_attn * projected
    normed, inverse = norm_forward(middle)
    xm = (normed * scaled + shift).astype(bf16)
    xm_ref[0] = xm
    xm_ref[1] = mixed_ref[...]
    gd = (gate_mlp * cot).astype(bf16)
    gd_ref[...] = gd
    down = grad_mod = None
    c0 = 0.7978845608028654
    c1 = c0 * 0.044715
    up_sums = []
    for at in range(0, ff, chunk):
        cols = slice(at, at + chunk)
        pre = dot_nn(xm, wu_ref[:, cols]) + bias_ref[:, cols]
        square = pre * pre
        t = jnp.tanh(pre * (c0 + c1 * square))
        half = 0.5 + 0.5 * t
        act = (pre * half).astype(bf16)
        act_ref[:, cols] = act
        slope = half + (0.5 * pre) * (1.0 - t * t) * (c0 + (3.0 * c1) * square)
        gp = (slope * dot_nt(gd, wd_ref[cols, :])).astype(bf16)
        gp_ref[at // chunk] = gp
        up_sums.append(column_sum(gp.astype(f32)))
        d = dot_nn(act, wd_ref[cols, :])
        g = dot_nt(gp, wu_ref[:, cols])
        down, grad_mod = (d, g) if down is None else (down + d, grad_mod + g)
    down = down + down_bias
    store_block((middle + gate_mlp * down).astype(bf16), out_refs)
    gm = cot + norm_backward(grad_mod * scaled, normed, inverse)
    gm_ref[...] = gm
    gpj = (gate_attn * gm).astype(bf16)
    gp_ref[ff // chunk] = gpj
    gmix_ref[...] = dot_nt(gpj, wo_ref[...]).astype(bf16)
    sums = jnp.concatenate(
        [
            column_sum(cot * down),
            column_sum(gd.astype(f32)),
            column_sum(grad_mod),
            column_sum(grad_mod * normed),
            column_sum(gm * projected),
            jnp.zeros((3, cot.shape[1]), f32),
        ],
        axis=0,
    )
    up_sum = jnp.concatenate(up_sums, axis=1)

    @pl.when(pl.program_id(0) == 0)
    def _():
        sum_ref[...] = sums
        up_sum_ref[...] = up_sum

    @pl.when(pl.program_id(0) > 0)
    def _():
        sum_ref[...] += sums
        up_sum_ref[...] += up_sum


def feed_forward(x, mixed, cot, mods, up_bias, wo, wu, wd, rows):
    length, width = x.shape
    steps = length // rows
    ff = wu.shape[1]
    block = pl.BlockSpec((rows, width), lambda i: (i, 0))
    wide = pl.BlockSpec((rows, ff), lambda i: (i, 0))

    def whole(a):
        return pl.BlockSpec(a.shape, lambda i: (0, 0), pipeline_mode=pl.Buffered(1))

    narrow = jax.ShapeDtypeStruct((length, width), bf16)
    broad = jax.ShapeDtypeStruct((length, ff), bf16)
    return pl.pallas_call(
        mlp_kernel,
        grid=(length // rows,),
        in_specs=[block, block, block] + [whole(a) for a in (mods, up_bias, wo, wu, wd)],
        out_specs=[
            pl.BlockSpec((2, rows, width), lambda i: (0, i, 0)),
            wide,
            block,
            pl.BlockSpec((ff // width + 1, rows, width), lambda i: (0, i, 0)),
            block,
            block,
            pl.BlockSpec((8, width), lambda i: (0, 0)),
            pl.BlockSpec((1, ff), lambda i: (0, 0)),
        ]
        + [pl.BlockSpec((rows, width), lambda i: (0, 0))] * steps,
        out_shape=[
            jax.ShapeDtypeStruct((2, length, width), bf16), broad, narrow,
            jax.ShapeDtypeStruct((ff // width + 1, length, width), bf16),
            jax.ShapeDtypeStruct((length, width), f32), narrow,
            jax.ShapeDtypeStruct((8, width), f32), jax.ShapeDtypeStruct((1, ff), f32),
        ]
        + [jax.ShapeDtypeStruct((rows, width), bf16)] * steps,
        cost_estimate=pl.CostEstimate(
            flops=8 * length * width * ff + 4 * length * width * width,
            bytes_accessed=40_000_000,
            transcendentals=length * ff,
        ),
        name="feed_forward",
    )(x, mixed, cot, mods, up_bias, wo, wu, wd)


def input_grad_kernel(x_ref, g_ref, gm_ref, mod_ref, w_ref, sum_ref, *hg_refs):
    width = x_ref.shape[1]
    normed, inverse = norm_forward(x_ref[...].astype(f32))
    grad = None
    for part in range(3):
        g = dot_nt(g_ref[part], w_ref[:, part * width : (part + 1) * width])
        grad = g if grad is None else grad + g
    hg = gm_ref[...] + norm_backward(grad * mod_ref[0:1, :], normed, inverse)
    store_block(hg.astype(bf16), hg_refs)
    sums = jnp.concatenate(
        [column_sum(grad), column_sum(grad * normed), jnp.zeros((6, width), f32)], axis=0
    )

    @pl.when(pl.program_id(0) == 0)
    def _():
        sum_ref[...] = sums

    @pl.when(pl.program_id(0) > 0)
    def _():
        sum_ref[...] += sums


def input_grad(x, grads, gm, mods, weight, rows):
    length, width = x.shape
    steps = length // rows
    block = pl.BlockSpec((rows, width), lambda i: (i, 0))
    return pl.pallas_call(
        input_grad_kernel,
        grid=(length // rows,),
        in_specs=[block, pl.BlockSpec((3, rows, width), lambda i: (0, i, 0)), block]
        + [
            pl.BlockSpec(mods.shape, lambda i: (0, 0)),
            pl.BlockSpec(weight.shape, lambda i: (0, 0), pipeline_mode=pl.Buffered(1)),
        ],
        out_specs=[pl.BlockSpec((8, width), lambda i: (0, 0))]
        + [pl.BlockSpec((rows, width), lambda i: (0, 0))] * steps,
        out_shape=[jax.ShapeDtypeStruct((8, width), f32)]
        + [jax.ShapeDtypeStruct((rows, width), bf16)] * steps,
        cost_estimate=pl.CostEstimate(
            flops=6 * length * width * width, bytes_accessed=16_000_000, transcendentals=0
        ),
        name="input_grad",
    )(x, grads, gm, mods, weight)


def split_halves(product, half, this_core):
    pieces = []
    for at in range(0, product.shape[0], 2 * half):
        low = product[at : at + half].astype(bf16)
        high = product[at + half : at + 2 * half].astype(bf16)
        pieces.append((jnp.where(this_core, high, low), jnp.where(this_core, low, high)))
    return pieces


def row_grad_kernel(core_ref, a_ref, b_ref, send_ref, keep_ref, *, half):
    product = dot_tn(a_ref[...], b_ref[...])
    for i, (send, keep) in enumerate(split_halves(product, half, core_ref[0] == 0)):
        send_ref[0, i * half : (i + 1) * half] = send
        keep_ref[0, i * half : (i + 1) * half] = keep


def row_grad(core, a, b, sp):
    length, width = b.shape
    out = jax.ShapeDtypeStruct((sp, width // 2, width), bf16)
    block = pl.BlockSpec((1, width // 2, width), lambda j, c: (j, 0, 0))
    return pl.pallas_call(
        functools.partial(row_grad_kernel, half=width // sp // 2),
        grid_spec=pltpu.PrefetchScalarGridSpec(
            num_scalar_prefetch=1,
            grid=(sp,),
            in_specs=[
                pl.BlockSpec((length, width), lambda j, c: (0, j)),
                pl.BlockSpec((length, width), lambda j, c: (0, 0)),
            ],
            out_specs=[block, block],
        ),
        out_shape=[out, out],
        cost_estimate=pl.CostEstimate(
            flops=2 * length * width * width * sp, bytes_accessed=16_000_000, transcendentals=0
        ),
        name="row_grad",
    )(core, a, b)


def column_grad_kernel(core_ref, a_ref, b_ref, send_ref, keep_ref, turned_ref):
    @pl.when((pl.program_id(0) == 0) | (pl.program_id(0) == core_ref[1]))
    def _():
        turned_ref[...] = a_ref[0].T

    product = dot_nn(turned_ref[...], b_ref[0])
    for i, (send, keep) in enumerate(split_halves(product, send_ref.shape[1], core_ref[0] == 0)):
        send_ref[i] = send
        keep_ref[i] = keep


def column_grad(core, a, b, sp, blocks, second):
    _, length, width = a.shape
    n = b.shape[0]
    half = width // sp // 2
    out = jax.ShapeDtypeStruct((sp, blocks * half, width), bf16)
    block = pl.BlockSpec((sp, half, width), lambda j, c: (0, j, 0))
    return pl.pallas_call(
        column_grad_kernel,
        grid_spec=pltpu.PrefetchScalarGridSpec(
            num_scalar_prefetch=1,
            grid=(n,),
            in_specs=[
                pl.BlockSpec((1, length, width), lambda j, c: (j // second, 0, 0)),
                pl.BlockSpec((1, length, width), lambda j, c: (j, 0, 0)),
            ],
            out_specs=[block, block],
            scratch_shapes=[pltpu.VMEM((width, length), bf16)],
        ),
        out_shape=[out, out],
        cost_estimate=pl.CostEstimate(
            flops=2 * length * width * width * n, bytes_accessed=16_000_000, transcendentals=0
        ),
        name="column_grad",
    )(jnp.concatenate([core, jnp.full((1,), second, jnp.int32)]), a, b)


def vector_grad_kernel(core_ref, timing_ref, parts_ref, sums_ref, _, __, send_ref, keep_ref):
    sp, half, width = send_ref.shape
    parts = parts_ref.shape[0] // 2
    count = timing_ref.shape[0] // sp
    filled = parts * count
    rest = half - filled - sums_ref.shape[2]
    for ref, side in ((send_ref, 1 - core_ref[0]), (keep_ref, core_ref[0])):
        for s in range(sp):
            for p in range(parts):
                part = jnp.where(side == 0, parts_ref[p : p + 1, :], parts_ref[parts + p : parts + p + 1, :])
                column = timing_ref[s * count : (s + 1) * count, :]
                ref[s, p * count : (p + 1) * count] = (column * part).astype(bf16)
            ref[s, filled : filled + sums_ref.shape[2]] = jnp.where(
                side == 0, sums_ref[0, s], sums_ref[1, s]
            ).astype(bf16)
            if rest:
                ref[s, half - rest : half] = jnp.zeros((rest, width), bf16)


def vector_grad(core, timing, parts, sums, send, keep, rows):
    sp, total, width = send.shape
    block = pl.BlockSpec((sp, rows, width), lambda i, c: (0, total // rows - 1, 0))
    return pl.pallas_call(
        vector_grad_kernel,
        grid_spec=pltpu.PrefetchScalarGridSpec(
            num_scalar_prefetch=1,
            grid=(1,),
            in_specs=[
                pl.BlockSpec(timing.shape, lambda i, c: (0, 0)),
                pl.BlockSpec(parts.shape, lambda i, c: (0, 0)),
                pl.BlockSpec(sums.shape, lambda i, c: (0, 0, 0, 0)),
                pl.BlockSpec(memory_space=pl.ANY),
                pl.BlockSpec(memory_space=pl.ANY),
            ],
            out_specs=[block, block],
        ),
        out_shape=[jax.ShapeDtypeStruct(send.shape, bf16)] * 2,
        input_output_aliases={4: 0, 5: 1},
        cost_estimate=pl.CostEstimate(flops=1000, bytes_accessed=1000, transcendentals=0),
        name="vector_grad",
    )(core, timing, parts, sums, send, keep)


def shift_permute(value, axis, by):
    n = lax.axis_size(axis)
    return lax.ppermute(value, axis, [(i, (i + by) % n) for i in range(n)])


def pair_permute(value, bit, axis="dp"):
    n = lax.axis_size(axis)
    return lax.ppermute(value, axis, [(i, i ^ bit) for i in range(n)])


def pick(values, index, axis=0):
    return lax.dynamic_index_in_dim(values, index, axis, keepdims=False)


def after(values, *others):
    return lax.optimization_barrier((values, others))[0]


def to_sequences(values):
    n, me = lax.axis_size("sp"), lax.axis_index("sp")
    blocks = [pick(values, me)]
    for d in range(1, n):
        blocks.append(shift_permute(pick(values, (me + d) % n), "sp", d))
    return blocks


def from_sequences(blocks):
    return [shift_permute(block, "sp", -d) if d else block for d, block in enumerate(blocks)]


VMEM = pl.BlockSpec(memory_space=pltpu.VMEM)
SMEM = pl.BlockSpec(memory_space=pltpu.SMEM)
ANY = pl.BlockSpec(memory_space=pl.ANY)
SMALL = pl.CostEstimate(flops=1000, bytes_accessed=1000, transcendentals=0)


def place_kernel(at_ref, *refs, n):
    blocks, out_ref, held_ref, sem = refs[:n], refs[n], refs[n + 1], refs[n + 2]
    copies = []
    for d, block in enumerate(blocks):
        held_ref[d] = block[...].astype(out_ref.dtype)
        copies.append(
            pltpu.make_async_copy(
                held_ref.at[d], out_ref.at[lax.rem(at_ref[2] + d, n)], sem.at[d]
            )
        )
        copies[-1].start()
    for copy in copies:
        copy.wait()


def place(at, blocks, dtype):
    n = len(blocks)
    shape = (n,) + blocks[0].shape
    return pl.pallas_call(
        functools.partial(place_kernel, n=n),
        in_specs=[SMEM] + [VMEM] * n,
        out_specs=ANY,
        out_shape=jax.ShapeDtypeStruct(shape, dtype),
        scratch_shapes=[pltpu.VMEM(shape, dtype), pltpu.SemaphoreType.DMA((n,))],
        cost_estimate=SMALL,
        name="place",
    )(at, *blocks)


def bit_of(index, bit):
    return (index // bit) % 2


def add(a, b):
    return (a.astype(f32) + b.astype(f32)).astype(bf16)


CORE, FIRST, SECOND = 1, 2, 4


def first_halves_kernel(at_ref, row_keep, row_got, col_keep, col_got, *outs):
    columns = outs[0].shape[2]
    start = 0
    for keep, got in ((row_keep, row_got), (col_keep, col_got)):
        total = add(keep[0], got[0])
        n = total.shape[0] // 2
        low, high = total[:n], total[n:]
        for side in range(2):
            cols = slice(side * columns, (side + 1) * columns)
            mine = at_ref[side] == 0
            outs[2 * side][0, start : start + n] = jnp.where(mine, high, low)[:, cols]
            outs[2 * side + 1][0, start : start + n] = jnp.where(mine, low, high)[:, cols]
        start += n


def first_halves(at, row_keep, row_got, col_keep, col_got):
    sp, rows, width = row_keep.shape
    cols = col_keep.shape[1]

    def spec(a):
        return pl.BlockSpec((1,) + a.shape[1:], lambda s, t: (s, 0, 0))

    out = jax.ShapeDtypeStruct((sp, (rows + cols) // 2, width // 2), bf16)
    return pl.pallas_call(
        first_halves_kernel,
        grid_spec=pltpu.PrefetchScalarGridSpec(
            num_scalar_prefetch=1,
            grid=(sp,),
            in_specs=[spec(a) for a in (row_keep, row_got, col_keep, col_got)],
            out_specs=[spec(out)] * 4,
        ),
        out_shape=[out] * 4,
        cost_estimate=pl.CostEstimate(flops=1000, bytes_accessed=1000, transcendentals=0),
        name="first_halves",
    )(at, row_keep, row_got, col_keep, col_got)


def second_halves_kernel(at_ref, *refs):
    for side in range(2):
        mine = at_ref[1 - side]
        keep, got = refs[2 * side : 2 * side + 2]
        for s in range(keep.shape[0]):
            refs[4 + 2 * side][s] = add(keep[s, 1 - mine], got[s, 1 - mine])
            refs[5 + 2 * side][s] = add(keep[s, mine], got[s, mine])


def second_halves(at, *arrays):
    sp, rows, columns = arrays[0].shape
    out = jax.ShapeDtypeStruct((sp, rows // 2, columns), bf16)
    return pl.pallas_call(
        second_halves_kernel,
        in_specs=[SMEM] + [VMEM] * 4,
        out_specs=[VMEM] * 4,
        out_shape=[out] * 4,
        cost_estimate=SMALL,
        name="second_halves",
    )(at, *[a.reshape(sp, 2, rows // 2, columns) for a in arrays])


def near_halves_kernel(at_ref, *refs, terms, sides):
    ins, outs = refs[:-2], refs[-2:]
    mine = lax.rem(at_ref[2], 2)
    for out, bit in zip(outs, (1 - mine, mine)):
        for s in range(out.shape[0]):
            at = 0
            for side in range(sides):
                total = None
                for ref in ins[side * terms : (side + 1) * terms]:
                    value = ref[2 * s + bit].astype(f32)
                    total = value if total is None else total + value
                out[s, :, at : at + total.shape[1]] = total.astype(bf16)
                at += total.shape[1]


def near_halves(at, sides):
    terms = len(sides[0])
    flat = [a for side in sides for a in side]
    sp, rows, _ = flat[0].shape
    width = sum(side[0].shape[2] for side in sides)
    out = jax.ShapeDtypeStruct((sp // 2, rows, width), bf16)
    return pl.pallas_call(
        functools.partial(near_halves_kernel, terms=terms, sides=len(sides)),
        in_specs=[SMEM] + [VMEM] * len(flat),
        out_specs=[VMEM] * 2,
        out_shape=[out] * 2,
        cost_estimate=SMALL,
        name="near_halves",
    )(at, *flat)


def far_halves_kernel(at_ref, keep, got, send_ref, keep_ref):
    mine = lax.div(at_ref[2], 2)
    send_ref[...] = add(keep[1 - mine], got[1 - mine])
    keep_ref[...] = add(keep[mine], got[mine])


def far_halves(at, keep, got):
    out = jax.ShapeDtypeStruct(keep.shape[1:], bf16)
    return pl.pallas_call(
        far_halves_kernel,
        in_specs=[SMEM] + [VMEM] * 2,
        out_specs=[VMEM] * 2,
        out_shape=[out] * 2,
        cost_estimate=SMALL,
        name="far_halves",
    )(at, keep, got)


def own_kernel(keep_ref, got_ref, out_ref):
    out_ref[...] = add(keep_ref[...], got_ref[...])


def own_sum(keep, got):
    return pl.pallas_call(
        own_kernel,
        in_specs=[VMEM] * 2,
        out_specs=VMEM,
        out_shape=jax.ShapeDtypeStruct(keep.shape, bf16),
        cost_estimate=SMALL,
        name="own_sum",
    )(keep, got)


def quarters_kernel(at_ref, keep_ref, got_ref, *outs):
    for i, out in enumerate(outs):
        index = 2 * (at_ref[0] ^ (i // 2)) + (at_ref[1] ^ (i % 2))
        for s in range(keep_ref.shape[0]):
            out[s] = add(keep_ref[s, index], got_ref[s, index])


def quarters(at, keep, got):
    sp, rows, width = keep.shape
    out = jax.ShapeDtypeStruct((sp, rows // 4, width), bf16)
    return pl.pallas_call(
        quarters_kernel,
        in_specs=[SMEM] + [VMEM] * 2,
        out_specs=[VMEM] * 4,
        out_shape=[out] * 4,
        cost_estimate=SMALL,
        name="quarters",
    )(at, keep.reshape(sp, 4, rows // 4, width), got.reshape(sp, 4, rows // 4, width))


def four_chips_kernel(at_ref, *refs, crossed):
    pieces, out_ref = refs[:4], refs[4]
    columns = out_ref.shape[2] // 2
    for i, piece in enumerate(pieces):
        x, y = at_ref[0] ^ (i // 2), at_ref[1] ^ (i % 2)
        out_ref[2 * x + y, :, :columns] = piece[:, :columns]
        out_ref[2 * y + x if crossed else 2 * x + y, :, columns:] = piece[:, columns:]


def four_chips(at, pieces, crossed):
    rows, width = pieces[0].shape
    return pl.pallas_call(
        functools.partial(four_chips_kernel, crossed=crossed),
        in_specs=[SMEM] + [VMEM] * 4,
        out_specs=VMEM,
        out_shape=jax.ShapeDtypeStruct((4, rows, width), bf16),
        cost_estimate=SMALL,
        name="four_chips",
    )(at, *pieces).reshape(4 * rows, width)


def spread(own):
    return [own] + [pair_permute(own, bit) for bit in (SECOND, FIRST, FIRST + SECOND)]


def finish_kernel(core_ref, mine_ref, other_ref, *outs, half, layout):
    first = core_ref[0] == 0
    width = mine_ref.shape[1]
    for out, (_, across, starts) in zip(outs, layout):
        for n, at in enumerate(starts):
            cols = slice(n % across * width, (n % across + 1) * width)
            mine = mine_ref[at : at + half].astype(f32)
            other = other_ref[at : at + half].astype(f32)
            to = n // across * 2 * half
            out[to : to + half, cols] = jnp.where(first, mine, other)
            out[to + half : to + 2 * half, cols] = jnp.where(first, other, mine)


def finish(core, mine, other, half, layout):
    width = mine.shape[1]
    shapes = [(2 * half * down, width * across) for down, across, _ in layout]
    return pl.pallas_call(
        functools.partial(finish_kernel, half=half, layout=layout),
        grid=(1,),
        in_specs=[SMEM] + [VMEM] * 2,
        out_specs=[pl.BlockSpec(s, lambda i: (0, 0)) for s in shapes],
        out_shape=[jax.ShapeDtypeStruct(s, f32) for s in shapes],
        cost_estimate=SMALL,
        name="finish",
    )(core, mine, other)


def late_row_kernel(sums_ref, parts_ref, mod_ref, ada_ref, row_ref):
    width = sums_ref.shape[1]
    shift, scaled = sums_ref[0:1, :], sums_ref[1:2, :]
    scale = scaled * mod_ref[0:1, :]
    row = jnp.concatenate([shift, scale] + [parts_ref[i : i + 1, :] for i in range(4)], axis=1)
    high = row.astype(bf16)
    low = (row - high.astype(f32)).astype(bf16)
    time = dot_nt(high, ada_ref[...]) + dot_nt(low, ada_ref[...])
    row_ref[:, :width] = shift.astype(bf16)
    row_ref[:, width : 2 * width] = scale.astype(bf16)
    row_ref[:, 2 * width : 3 * width] = (scaled * mod_ref[1:2, :]).astype(bf16)
    row_ref[:, 3 * width :] = time.astype(bf16)


def late_row(sums, parts, mods, ada):
    return pl.pallas_call(
        late_row_kernel,
        in_specs=[VMEM] * 4,
        out_specs=VMEM,
        out_shape=jax.ShapeDtypeStruct((1, 3 * sums.shape[1] + ada.shape[0]), bf16),
        cost_estimate=SMALL,
        name="late_row",
    )(sums, parts, mods, ada)


def ada_grad_kernel(timings_ref, rows_ref, vector_ref, out_ref, total_ref, *, half):
    count, width = out_ref.shape[0], vector_ref.shape[1]
    out_ref[:, : 2 * width] = dot_nn(timings_ref[...], rows_ref[:, : 2 * width])
    for p in range(4):
        start = p // 2 * half + p % 2 * count
        out_ref[:, (2 + p) * width : (3 + p) * width] = vector_ref[start : start + count, :]
    total_ref[...] = column_sum(rows_ref[:, : 3 * width].astype(f32))


def ada_grad(timings, rows, vectors, half):
    width = vectors.shape[1]
    shapes = [(timings.shape[0], 6 * width), (1, 3 * width)]
    return pl.pallas_call(
        functools.partial(ada_grad_kernel, half=half),
        grid=(1,),
        in_specs=[VMEM] * 3,
        out_specs=[pl.BlockSpec(s, lambda i: (0, 0)) for s in shapes],
        out_shape=[jax.ShapeDtypeStruct(s, f32) for s in shapes],
        cost_estimate=SMALL,
        name="ada_grad",
    )(timings, rows, vectors)


def sum_over_rest(total):
    bit = 2 * SECOND
    while bit < lax.axis_size("dp"):
        total = add(total, pair_permute(total, bit))
        bit *= 2
    return total


def double(rows, bit, axis):
    return jnp.concatenate([rows, pair_permute(rows, bit, axis)], axis=0)


def bits(axis):
    n, bit = lax.axis_size(axis), 1
    while bit < n:
        yield bit
        bit *= 2


def body(
    hidden_in,
    time_embed,
    ada_weight,
    ada_bias,
    attn_gain,
    query_key_value_matrix,
    attention_output_matrix,
    mlp_gain,
    up_projection_matrix,
    up_bias,
    down_projection_matrix,
    down_bias,
    out_cotangent,
):
    sequences, local_len, width = hidden_in.shape
    sp, me = lax.axis_size("sp"), lax.axis_index("sp")
    assert sequences == sp
    x_blocks = to_sequences(hidden_in)
    x = jnp.concatenate(x_blocks, axis=0)
    cot = jnp.concatenate(to_sequences(after(out_cotangent, x)), axis=0)
    here = lax.axis_index("dp")
    core = bit_of(here, CORE).reshape(1)
    at = jnp.stack([bit_of(here, FIRST), bit_of(here, SECOND), me])

    timing = lax.dynamic_slice_in_dim(time_embed, me, 1, 0)
    timings = timing
    for bit in bits("sp"):
        timings = double(timings, bit, "sp")
    for bit in bits("dp"):
        timings = double(timings, bit, "dp")
    modulation = dot_nn(timing, ada_weight) + ada_bias.astype(f32)[None]
    shift_attn, scale_attn, gate_attn, shift_mlp, scale_mlp, gate_mlp = jnp.split(
        modulation, 6, axis=-1
    )
    gain_attn = attn_gain.astype(f32)[None]
    gain_mlp = mlp_gain.astype(f32)[None]
    zero = jnp.zeros_like(shift_attn)
    attn_mods = jnp.concatenate(
        [gain_attn * (1.0 + scale_attn), shift_attn] + [zero] * 6, axis=0
    )
    mlp_mods = jnp.concatenate(
        [gate_attn, gain_mlp * (1.0 + scale_mlp), shift_mlp, gate_mlp, down_bias.astype(f32)[None]]
        + [zero] * 3,
        axis=0,
    )
    lane = lax.broadcasted_iota(jnp.int32, (1, LANES), 1)
    frequency = 10000.0 ** (-((lane % HALF).astype(f32) * 2.0 / HEAD_DIM))
    row = lax.broadcasted_iota(jnp.int32, (sp * local_len, 1), 0)
    position = ((me - row // local_len + sp) % sp) * local_len + row % local_len
    angles = position.astype(f32) * frequency
    cos, sin = jnp.cos(angles), jnp.sin(angles)

    xm_attn, q, k, v = project_qkv(x, attn_mods, query_key_value_matrix, cos, sin)
    mixed, lse = attention_forward(q, k, v)
    both_in, act, gd, both_grad, gm, gmix, sums, up_sum, *outs = feed_forward(
        x,
        mixed,
        cot,
        mlp_mods,
        up_bias.astype(f32)[None],
        attention_output_matrix,
        up_projection_matrix,
        down_projection_matrix,
        local_len,
    )
    ff = up_bias.shape[0]
    assert ff == sp * width
    n_up = ff // width
    half = width // sp // 2
    quarter = width // sp
    cond = timing.shape[1]
    column = timing.astype(f32).reshape(cond, 1)

    def shards(row):
        return row.reshape(sp, -1)

    def sum_rows(rows):
        filled = [
            jnp.stack([jnp.pad(r, ((0, 0), (0, width - r.shape[1]))) for r in side], axis=1)
            for side in rows
        ]
        return jnp.stack([jnp.pad(f, ((0, 0), (0, 16 - f.shape[1]), (0, 0))) for f in filled])

    row_send, row_keep = row_grad(core, act, gd, sp)
    out_blocks = from_sequences(outs)
    row_got = pair_permute(row_send, CORE)
    both_in, both_grad = after((both_in, both_grad), row_keep)
    col_send, col_keep = column_grad(core, both_in, both_grad, sp, n_up + 2, n_up)
    early_parts = jnp.concatenate([sums[4:5], sums[2:3], sums[3:4] * gain_mlp, sums[0:1]], axis=0)
    six = 6 * width
    early_bias = jnp.concatenate([jnp.zeros((2 * width,), f32), early_parts.reshape(-1)])
    early_bias = shards(early_bias)
    early_sums = sum_rows(
        [
            [shards(up_sum), early_bias[:, :width]],
            [
                jnp.concatenate(
                    [shards(sums[3:4] * (1.0 + scale_mlp)), shards(sums[1:2])], axis=1
                ),
                early_bias[:, width:],
            ],
        ]
    )
    col_send, col_keep = vector_grad(core, column, early_parts, early_sums, col_send, col_keep, half)
    col_got = pair_permute(col_send, CORE)

    pairs = width // LANES

    def backward(start, stop, into=None):
        return attention_backward(
            q, k, v, gmix, mixed, lse, cos, sin, start, stop - start, into
        )

    gmix = after(gmix, col_keep)
    grads = backward(0, 1)
    row_got, col_got = after((row_got, col_got), grads)
    left_send, left, right_send, right = first_halves(at, row_keep, row_got, col_keep, col_got)
    left_got, right_got = pair_permute(left_send, FIRST), pair_permute(right_send, SECOND)
    grads = after(grads, left, right)
    grads = backward(1, pairs, grads)
    left_got, right_got, out_blocks = after((left_got, right_got, out_blocks), grads)
    left_send, left, right_send, right = second_halves(at, left, left_got, right, right_got)
    left_got, right_got = pair_permute(left_send, SECOND), pair_permute(right_send, FIRST)
    grads = after(grads, left, right)

    late_send, late_keep = column_grad(core, xm_attn[None], grads, sp, 3, 3)
    late_got = pair_permute(late_send, CORE)
    left_got, right_got = after((left_got, right_got), late_keep)
    if lax.axis_size("dp") > 2 * SECOND:
        left, right = sum_over_rest(add(left, left_got)), sum_over_rest(add(right, right_got))
        sides = [(left,), (right,)]
    else:
        sides = [(left, left_got), (right, right_got)]
    near_send, near = near_halves(at, sides)
    near_got = pair_permute(near_send, 1, "sp")
    grads = after(grads, near)
    attn_sums, *hgs = input_grad(x, grads, gm, attn_mods, query_key_value_matrix, local_len)
    hidden_blocks = from_sequences(hgs)
    late_got = after(late_got, hgs[0])
    own_quarter, *other_quarters = quarters(at, late_keep, late_got)
    quarter_parts = [own_quarter] + [
        pair_permute(p, bit)
        for p, bit in zip(other_quarters, (SECOND, FIRST, FIRST + SECOND))
    ]
    near_got = after(near_got, own_quarter)
    far_send, far = far_halves(at, near, near_got)
    far_got = pair_permute(far_send, 2, "sp")
    row_mods = jnp.concatenate([gain_attn, 1.0 + scale_attn] + [zero] * 6, axis=0)
    rows = late_row(after(attn_sums, far), early_parts, row_mods, ada_weight)

    hidden_blocks, quarter_parts, far_got, rows = lax.optimization_barrier(
        (hidden_blocks, quarter_parts, far_got, rows)
    )
    if lax.axis_size("dp") > 2 * SECOND:
        total = sum(p.astype(f32) for p in quarter_parts).astype(bf16)
        quarter_parts = [sum_over_rest(total)]
    near_send, near = near_halves(at, [quarter_parts])
    near_got = pair_permute(near_send, 1, "sp")
    rows_got = pair_permute(after(rows, near), 1, "sp")
    early_own = own_sum(after(far, near), far_got)
    early_four = spread(early_own)
    hidden_grad = place(at, after(hidden_blocks, early_own), f32)
    near_got, rows_got = after((near_got, rows_got), hidden_grad)
    far_send, far = far_halves(at, near, near_got)
    far_got = pair_permute(far_send, 2, "sp")
    rows = jnp.concatenate([rows, rows_got], axis=0)
    rows = double(after(rows, far), 2, "sp")
    time_grad = jnp.concatenate(
        [pick(rows[:, 3 * width :], me ^ s)[None] for s in range(sp)], axis=0
    ).astype(f32)
    late_own = own_sum(far, far_got)
    late_four = spread(late_own)
    rows = after(rows, late_own)
    for bit in bits("dp"):
        rows = double(rows, bit, "dp")
    early_half = four_chips(at, after(early_four, late_own), True)
    early_other = pair_permute(early_half, CORE)
    late_half = four_chips(at, after(late_four, early_half), False)
    late_other = pair_permute(late_half, CORE)
    n_row, n_col = row_keep.shape[1] // 2, col_keep.shape[1] // 2
    row_starts = [x * (n_row + n_col) + i for x in range(2) for i in range(0, n_row, half)]
    col_starts = [x * (n_row + n_col) + n_row + i for x in range(2) for i in range(0, n_col, half)]
    down_grad, up_grad, proj_grad, vectors = finish(
        core,
        early_half,
        after(early_other, late_half),
        half,
        (
            (sp, 1, row_starts),
            (1, n_up, col_starts[:n_up]),
            (1, 1, col_starts[n_up : n_up + 1]),
            (1, 1, col_starts[n_up + 1 :]),
        ),
    )
    output = place(at, out_blocks, bf16)
    (qkv_grad,) = finish(
        core, late_half, after(late_other, down_grad), half, ((1, 3, [0, half, 2 * half]),)
    )

    cond_here = cond // sp
    count = 2 * cond_here
    own_timing = lax.dynamic_slice_in_dim(timings, me * cond_here, cond_here, 1).T
    ada_weight_grad, totals = ada_grad(own_timing, rows, vectors, half)
    totals = totals[0]
    late_bias = jnp.concatenate([totals[: 2 * width], jnp.zeros((4 * width,), f32)])
    ada_bias_grad = lax.dynamic_slice_in_dim(late_bias, me * (six // sp), six // sp, 0)
    ada_bias_grad = ada_bias_grad + jnp.concatenate(
        [vectors[count + 1], vectors[half + count + 1, : six // sp - width]]
    )
    attn_gain_grad = lax.dynamic_slice_in_dim(totals[2 * width :], me * quarter, quarter, 0)
    up_bias_grad = vectors[count]
    mlp_gain_grad = vectors[half + count, :quarter]
    down_bias_grad = vectors[half + count, quarter : 2 * quarter]
    return (
        output,
        hidden_grad,
        time_grad,
        ada_weight_grad,
        ada_bias_grad,
        attn_gain_grad,
        qkv_grad,
        proj_grad,
        mlp_gain_grad,
        up_grad,
        up_bias_grad,
        down_grad,
        down_bias_grad,
    )


def solution(mesh):
    return jax.shard_map(
        body,
        mesh=mesh,
        in_specs=(P("dp", "sp", None), P("dp", None)) + (P(),) * 10 + (P("dp", "sp", None),),
        out_specs=(
            P("dp", "sp", None),
            P("dp", "sp", None),
            P("dp", None),
            P("sp", None),
            P("sp"),
            P("sp"),
            P("sp", None),
            P("sp", None),
            P("sp"),
            P("sp", None),
            P("sp"),
            P("sp", None),
            P("sp"),
        ),
        check_vma=False,
    )
```

```python
import functools

import jax
import jax.numpy as jnp
from jax import lax
from jax.experimental import pallas as pl
from jax.experimental.pallas import tpu as pltpu
from jax.sharding import PartitionSpec as P

HEAD_DIM = 64
HALF = HEAD_DIM // 2
LANES = 128
EPSILON = 1e-05
LOG2E = 1.4426950408889634
SCALE = HEAD_DIM ** (-0.5)
f32 = jnp.float32
COVER = pl.CostEstimate(flops=40_000_000_000, bytes_accessed=100_000_000, transcendentals=0)
bf16 = jnp.bfloat16


def dot_nn(a, b):
    return lax.dot_general(a, b, (((1,), (0,)), ((), ())), preferred_element_type=f32)


def dot_nt(a, b):
    return lax.dot_general(a, b, (((1,), (1,)), ((), ())), preferred_element_type=f32)


def dot_tn(a, b):
    return lax.dot_general(a, b, (((0,), (0,)), ((), ())), preferred_element_type=f32)


def column_sum(values):
    return jnp.sum(values, axis=0, keepdims=True)


def norm_forward(values):
    center = values - jnp.mean(values, axis=-1, keepdims=True)
    inverse = lax.rsqrt(jnp.mean(center * center, axis=-1, keepdims=True) + EPSILON)
    return center * inverse, inverse


def norm_backward(grad, normed, inverse):
    first = jnp.mean(grad, axis=-1, keepdims=True)
    second = jnp.mean(grad * normed, axis=-1, keepdims=True)
    return inverse * (grad - first - normed * second)


def swap_halves(values):
    lane = lax.broadcasted_iota(jnp.int32, (1, LANES), 1)
    lower = (lane & (HEAD_DIM - 1)) < HALF
    up = pltpu.roll(values, LANES - HALF, 1)
    down = pltpu.roll(values, HALF, 1)
    return lower, up, down


def rotary(values, cos, sin):
    lower, up, down = swap_halves(values)
    return values * cos + jnp.where(lower, -up, down) * sin


def unrotary(values, cos, sin):
    lower, up, down = swap_halves(values * sin)
    return values * cos + jnp.where(lower, up, -down)


def qkv_kernel(x_ref, mod_ref, w_ref, cos_ref, sin_ref, xm_ref, q_ref, k_ref, v_ref):
    width = x_ref.shape[1]
    normed, _ = norm_forward(x_ref[...].astype(f32))
    xm = (normed * mod_ref[0:1, :] + mod_ref[1:2, :]).astype(bf16)
    xm_ref[...] = xm
    cos, sin = cos_ref[...], sin_ref[...]
    for part, ref in enumerate((q_ref, k_ref, v_ref)):
        whole = dot_nn(xm, w_ref[:, part * width : (part + 1) * width]).astype(bf16)
        if part == 2:
            ref[...] = whole
            continue
        for lane in range(0, width, LANES):
            piece = whole[:, lane : lane + LANES].astype(f32)
            ref[:, lane : lane + LANES] = rotary(piece, cos, sin).astype(bf16)


def project_qkv(x, mods, weight, cos, sin, rows=256):
    length, width = x.shape
    block = pl.BlockSpec((rows, width), lambda i: (i, 0))
    table = pl.BlockSpec((rows, LANES), lambda i: (i, 0))
    shape = jax.ShapeDtypeStruct((length, width), bf16)
    return pl.pallas_call(
        qkv_kernel,
        grid=(length // rows,),
        in_specs=[
            block,
            pl.BlockSpec(mods.shape, lambda i: (0, 0)),
            pl.BlockSpec(weight.shape, lambda i: (0, 0)),
            table,
            table,
        ],
        out_specs=[block] * 4,
        out_shape=[shape] * 4,
        cost_estimate=COVER,
        name="project_qkv",
    )(x, mods, weight, cos, sin)


def attention_forward_kernel(q_ref, k_ref, v_ref, o_ref, lse_ref):
    q, k, v = q_ref[...], k_ref[...], v_ref[...]
    first = lax.broadcasted_iota(jnp.int32, (1, LANES), 1) < HEAD_DIM
    c = LOG2E * SCALE
    outs = []
    for h in range(2):
        mine = first if h == 0 else ~first
        kh = jnp.where(mine, k, jnp.zeros_like(k))
        st = dot_nt(kh, q)
        top = jnp.max(st, axis=0, keepdims=True) * c
        p = jnp.exp2(st * c - top).astype(bf16)
        ot = dot_tn(jnp.where(mine, v, jnp.ones_like(v)), p)
        own, ones = (ot[:HEAD_DIM], ot[HEAD_DIM:]) if h == 0 else (ot[HEAD_DIM:], ot[:HEAD_DIM])
        total = ones[0:1]
        outs.append(own * (1.0 / total))
        lse_ref[0, h : h + 1, :] = top + jnp.log2(total)
    o_ref[...] = jnp.concatenate(outs, axis=0).T.astype(bf16)


def attention_forward(q, k, v):
    length, width = q.shape
    pairs = width // LANES
    block = pl.BlockSpec((length, LANES), lambda i: (0, i))
    return pl.pallas_call(
        attention_forward_kernel,
        grid=(pairs,),
        in_specs=[block] * 3,
        out_specs=[block, pl.BlockSpec((1, 2, length), lambda i: (i, 0, 0))],
        out_shape=[
            jax.ShapeDtypeStruct((length, width), bf16),
            jax.ShapeDtypeStruct((pairs, 2, length), f32),
        ],
        cost_estimate=COVER,
        name="attention_forward",
    )(q, k, v)


def attention_backward_kernel(
    q_ref, k_ref, v_ref, do_ref, o_ref, lse_ref, cos_ref, sin_ref, *rest
):
    g_ref = rest[-1]
    first = lax.broadcasted_iota(jnp.int32, (1, LANES), 1) < HEAD_DIM
    upper = lax.broadcasted_iota(jnp.int32, (LANES, 1), 0) < HEAD_DIM
    c = LOG2E * SCALE
    q, k, v, do = q_ref[...], k_ref[...], v_ref[...], do_ref[...]
    prod = (do.astype(f32) * o_ref[...].astype(f32)).T
    kt = k.T
    zero = jnp.zeros_like(k)
    dq = dk = dv = None
    for h in range(2):
        mine = first if h == 0 else ~first
        row = column_sum(prod[h * HEAD_DIM : (h + 1) * HEAD_DIM])
        st = dot_nt(jnp.where(mine, k, zero), q)
        p = jnp.exp2(st * c - lse_ref[0, h : h + 1, :])
        dp = dot_nt(jnp.where(mine, v, zero), do)
        ds = (p * (dp - row)).astype(bf16)
        dvh = dot_nn(p.astype(bf16), jnp.where(mine, do, zero))
        dkh = dot_nn(ds, jnp.where(mine, q, zero))
        dqh = dot_nn(jnp.where(upper if h == 0 else ~upper, kt, jnp.zeros_like(kt)), ds)
        dq, dk, dv = (dqh, dkh, dvh) if h == 0 else (dq + dqh, dk + dkh, dv + dvh)
    cos, sin = cos_ref[...], sin_ref[...]
    g_ref[0] = unrotary(dq.T * SCALE, cos, sin).astype(bf16)
    g_ref[1] = unrotary(dk * SCALE, cos, sin).astype(bf16)
    g_ref[2] = dv.astype(bf16)


def attention_backward(q, k, v, do, o, lse, cos, sin, start, count, into=None):
    length, width = q.shape
    block = pl.BlockSpec((length, LANES), lambda i: (0, start + i))
    table = pl.BlockSpec((length, LANES), lambda i: (0, 0))
    extra = [] if into is None else [into]
    return pl.pallas_call(
        attention_backward_kernel,
        grid=(count,),
        in_specs=[block] * 5
        + [pl.BlockSpec((1, 2, length), lambda i: (start + i, 0, 0)), table, table]
        + [pl.BlockSpec(memory_space=pl.ANY)] * len(extra),
        out_specs=pl.BlockSpec((3, length, LANES), lambda i: (0, 0, start + i)),
        out_shape=jax.ShapeDtypeStruct((3, length, width), bf16),
        input_output_aliases={8: 0} if extra else {},
        cost_estimate=COVER,
        name="attention_backward",
    )(q, k, v, do, o, lse, cos, sin, *extra)


def mlp_kernel(
    x_ref, mixed_ref, cot_ref, mod_ref, bias_ref, wo_ref, wu_ref, wd_ref,
    xm_ref, act_ref, gd_ref, gp_ref, gm_ref, gmix_ref, sum_ref, up_sum_ref, out_ref,
):
    chunk, ff = wu_ref.shape
    gate_attn, scaled, shift = mod_ref[0:1, :], mod_ref[1:2, :], mod_ref[2:3, :]
    gate_mlp, down_bias = mod_ref[3:4, :], mod_ref[4:5, :]
    cot = cot_ref[...].astype(f32)
    projected = dot_nn(mixed_ref[...], wo_ref[...])
    middle = x_ref[...].astype(f32) + gate_attn * projected
    normed, inverse = norm_forward(middle)
    xm = (normed * scaled + shift).astype(bf16)
    xm_ref[0] = xm
    xm_ref[1] = mixed_ref[...]
    gd = (gate_mlp * cot).astype(bf16)
    gd_ref[...] = gd
    down = grad_mod = None
    c0 = 0.7978845608028654
    c1 = c0 * 0.044715
    up_sums = []
    for at in range(0, ff, chunk):
        cols = slice(at, at + chunk)
        pre = dot_nn(xm, wu_ref[:, cols]) + bias_ref[:, cols]
        square = pre * pre
        t = jnp.tanh(pre * (c0 + c1 * square))
        half = 0.5 + 0.5 * t
        act = (pre * half).astype(bf16)
        act_ref[:, cols] = act
        slope = half + (0.5 * pre) * (1.0 - t * t) * (c0 + (3.0 * c1) * square)
        gp = (slope * dot_nt(gd, wd_ref[cols, :])).astype(bf16)
        gp_ref[at // chunk] = gp
        up_sums.append(column_sum(gp.astype(f32)))
        d = dot_nn(act, wd_ref[cols, :])
        g = dot_nt(gp, wu_ref[:, cols])
        down, grad_mod = (d, g) if down is None else (down + d, grad_mod + g)
    down = down + down_bias
    out_ref[...] = (middle + gate_mlp * down).astype(bf16)
    gm = cot + norm_backward(grad_mod * scaled, normed, inverse)
    gm_ref[...] = gm
    gpj = (gate_attn * gm).astype(bf16)
    gp_ref[ff // chunk] = gpj
    gmix_ref[...] = dot_nt(gpj, wo_ref[...]).astype(bf16)
    sums = jnp.concatenate(
        [
            column_sum(cot * down),
            column_sum(gd.astype(f32)),
            column_sum(grad_mod),
            column_sum(grad_mod * normed),
            column_sum(gm * projected),
            jnp.zeros((3, cot.shape[1]), f32),
        ],
        axis=0,
    )
    up_sum = jnp.concatenate(up_sums, axis=1)

    @pl.when(pl.program_id(0) == 0)
    def _():
        sum_ref[...] = sums
        up_sum_ref[...] = up_sum

    @pl.when(pl.program_id(0) > 0)
    def _():
        sum_ref[...] += sums
        up_sum_ref[...] += up_sum


def feed_forward(x, mixed, cot, mods, up_bias, wo, wu, wd, rows):
    length, width = x.shape
    ff = wu.shape[1]
    block = pl.BlockSpec((rows, width), lambda i: (i, 0))
    wide = pl.BlockSpec((rows, ff), lambda i: (i, 0))

    def whole(a):
        return pl.BlockSpec(a.shape, lambda i: (0, 0), pipeline_mode=pl.Buffered(1))

    narrow = jax.ShapeDtypeStruct((length, width), bf16)
    broad = jax.ShapeDtypeStruct((length, ff), bf16)
    return pl.pallas_call(
        mlp_kernel,
        grid=(length // rows,),
        in_specs=[block, block, block] + [whole(a) for a in (mods, up_bias, wo, wu, wd)],
        out_specs=[
            pl.BlockSpec((2, rows, width), lambda i: (0, i, 0)),
            wide,
            block,
            pl.BlockSpec((ff // width + 1, rows, width), lambda i: (0, i, 0)),
            block,
            block,
            pl.BlockSpec((8, width), lambda i: (0, 0)),
            pl.BlockSpec((1, ff), lambda i: (0, 0)),
        ]
        + [block],
        out_shape=[
            jax.ShapeDtypeStruct((2, length, width), bf16), broad, narrow,
            jax.ShapeDtypeStruct((ff // width + 1, length, width), bf16),
            jax.ShapeDtypeStruct((length, width), f32), narrow,
            jax.ShapeDtypeStruct((8, width), f32), jax.ShapeDtypeStruct((1, ff), f32),
        ]
        + [narrow],
        cost_estimate=COVER,
        name="feed_forward",
    )(x, mixed, cot, mods, up_bias, wo, wu, wd)


def late_grads_kernel(
    core_ref, x_ref, tile_ref, gm_ref, mod_ref, w_ref, xm_ref, block_ref,
    sum_ref, hg_ref, send_ref, keep_ref, turned_ref, *, tiles,
):
    step = pl.program_id(0)
    width = x_ref.shape[1]

    @pl.when(step < tiles)
    def _():
        normed, inverse = norm_forward(x_ref[...].astype(f32))
        grad = None
        for part in range(3):
            g = dot_nt(tile_ref[part], w_ref[:, part * width : (part + 1) * width])
            grad = g if grad is None else grad + g
        hg = gm_ref[...] + norm_backward(grad * mod_ref[0:1, :], normed, inverse)
        hg_ref[...] = hg.astype(bf16)
        sums = jnp.concatenate(
            [column_sum(grad), column_sum(grad * normed), jnp.zeros((6, width), f32)], axis=0
        )

        @pl.when(step == 0)
        def _():
            sum_ref[...] = sums

        @pl.when(step > 0)
        def _():
            sum_ref[...] += sums

    @pl.when(step == tiles)
    def _():
        turned_ref[...] = xm_ref[...].T

    @pl.when(step >= tiles)
    def _():
        product = dot_nn(turned_ref[...], block_ref[0])
        half = send_ref.shape[1]
        for i, (send, keep) in enumerate(split_halves(product, half, core_ref[0] == 0)):
            send_ref[i] = send
            keep_ref[i] = keep


def late_grads(core, x, grads, gm, mods, weight, xm, sp, rows):
    length, width = x.shape
    tiles = length // rows
    n = grads.shape[0]
    half = width // sp // 2

    def tile(i, c):
        return (jnp.minimum(i, tiles - 1), 0)

    def part(i):
        return jnp.maximum(i - tiles, 0)

    block = pl.BlockSpec((rows, width), tile)

    def whole(a):
        return pl.BlockSpec(a.shape, lambda i, c: (0, 0), pipeline_mode=pl.Buffered(1))

    out = pl.BlockSpec((sp, half, width), lambda i, c: (0, part(i), 0))
    shape = jax.ShapeDtypeStruct((sp, n * half, width), bf16)
    return pl.pallas_call(
        functools.partial(late_grads_kernel, tiles=tiles),
        grid_spec=pltpu.PrefetchScalarGridSpec(
            num_scalar_prefetch=1,
            grid=(tiles + n,),
            in_specs=[
                block,
                pl.BlockSpec((n, rows, width), lambda i, c: (0, jnp.minimum(i, tiles - 1), 0)),
                block,
                whole(mods),
                whole(weight),
                whole(xm),
                pl.BlockSpec((1, length, width), lambda i, c: (part(i), 0, 0)),
            ],
            out_specs=[pl.BlockSpec((8, width), lambda i, c: (0, 0)), block, out, out],
            scratch_shapes=[pltpu.VMEM((width, length), bf16)],
        ),
        out_shape=[
            jax.ShapeDtypeStruct((8, width), f32),
            jax.ShapeDtypeStruct((length, width), bf16),
            shape,
            shape,
        ],
        cost_estimate=COVER,
        name="late_grads",
    )(core, x, grads, gm, mods, weight, xm, grads)


def split_halves(product, half, this_core):
    pieces = []
    for at in range(0, product.shape[0], 2 * half):
        low = product[at : at + half].astype(bf16)
        high = product[at + half : at + 2 * half].astype(bf16)
        pieces.append((jnp.where(this_core, high, low), jnp.where(this_core, low, high)))
    return pieces


def row_grad_kernel(core_ref, a_ref, b_ref, send_ref, keep_ref, *, half):
    product = dot_tn(a_ref[...], b_ref[...])
    for i, (send, keep) in enumerate(split_halves(product, half, core_ref[0] == 0)):
        send_ref[0, i * half : (i + 1) * half] = send
        keep_ref[0, i * half : (i + 1) * half] = keep


def row_grad(core, a, b, sp):
    length, width = b.shape
    out = jax.ShapeDtypeStruct((sp, width // 2, width), bf16)
    block = pl.BlockSpec((1, width // 2, width), lambda j, c: (j, 0, 0))
    return pl.pallas_call(
        functools.partial(row_grad_kernel, half=width // sp // 2),
        grid_spec=pltpu.PrefetchScalarGridSpec(
            num_scalar_prefetch=1,
            grid=(sp,),
            in_specs=[
                pl.BlockSpec((length, width), lambda j, c: (0, j)),
                pl.BlockSpec((length, width), lambda j, c: (0, 0)),
            ],
            out_specs=[block, block],
        ),
        out_shape=[out, out],
        cost_estimate=COVER,
        name="row_grad",
    )(core, a, b)


def column_grad_kernel(core_ref, a_ref, b_ref, send_ref, keep_ref, turned_ref):
    @pl.when((pl.program_id(0) == 0) | (pl.program_id(0) == core_ref[1]))
    def _():
        turned_ref[...] = a_ref[0].T

    product = dot_nn(turned_ref[...], b_ref[0])
    for i, (send, keep) in enumerate(split_halves(product, send_ref.shape[1], core_ref[0] == 0)):
        send_ref[i] = send
        keep_ref[i] = keep


def column_grad(core, a, b, sp, blocks, second):
    _, length, width = a.shape
    n = b.shape[0]
    half = width // sp // 2
    out = jax.ShapeDtypeStruct((sp, blocks * half, width), bf16)
    block = pl.BlockSpec((sp, half, width), lambda j, c: (0, j, 0))
    return pl.pallas_call(
        column_grad_kernel,
        grid_spec=pltpu.PrefetchScalarGridSpec(
            num_scalar_prefetch=1,
            grid=(n,),
            in_specs=[
                pl.BlockSpec((1, length, width), lambda j, c: (j // second, 0, 0)),
                pl.BlockSpec((1, length, width), lambda j, c: (j, 0, 0)),
            ],
            out_specs=[block, block],
            scratch_shapes=[pltpu.VMEM((width, length), bf16)],
        ),
        out_shape=[out, out],
        cost_estimate=COVER,
        name="column_grad",
    )(jnp.concatenate([core, jnp.full((1,), second, jnp.int32)]), a, b)


def vector_grad_kernel(core_ref, timing_ref, parts_ref, sums_ref, _, __, send_ref, keep_ref):
    sp, half, width = send_ref.shape
    parts = parts_ref.shape[0] // 2
    count = timing_ref.shape[0] // sp
    filled = parts * count
    rest = half - filled - sums_ref.shape[2]
    for ref, side in ((send_ref, 1 - core_ref[0]), (keep_ref, core_ref[0])):
        for s in range(sp):
            for p in range(parts):
                part = jnp.where(side == 0, parts_ref[p : p + 1, :], parts_ref[parts + p : parts + p + 1, :])
                column = timing_ref[s * count : (s + 1) * count, :]
                ref[s, p * count : (p + 1) * count] = (column * part).astype(bf16)
            ref[s, filled : filled + sums_ref.shape[2]] = jnp.where(
                side == 0, sums_ref[0, s], sums_ref[1, s]
            ).astype(bf16)
            if rest:
                ref[s, half - rest : half] = jnp.zeros((rest, width), bf16)


def vector_grad(core, timing, parts, sums, send, keep, rows):
    sp, total, width = send.shape
    block = pl.BlockSpec((sp, rows, width), lambda i, c: (0, total // rows - 1, 0))
    return pl.pallas_call(
        vector_grad_kernel,
        grid_spec=pltpu.PrefetchScalarGridSpec(
            num_scalar_prefetch=1,
            grid=(1,),
            in_specs=[
                pl.BlockSpec(timing.shape, lambda i, c: (0, 0)),
                pl.BlockSpec(parts.shape, lambda i, c: (0, 0)),
                pl.BlockSpec(sums.shape, lambda i, c: (0, 0, 0, 0)),
                pl.BlockSpec(memory_space=pl.ANY),
                pl.BlockSpec(memory_space=pl.ANY),
            ],
            out_specs=[block, block],
        ),
        out_shape=[jax.ShapeDtypeStruct(send.shape, bf16)] * 2,
        input_output_aliases={4: 0, 5: 1},
        cost_estimate=COVER,
        name="vector_grad",
    )(core, timing, parts, sums, send, keep)


def shift_permute(value, axis, by):
    n = lax.axis_size(axis)
    return lax.ppermute(value, axis, [(i, (i + by) % n) for i in range(n)])


def pair_permute(value, bit, axis="dp"):
    n = lax.axis_size(axis)
    return lax.ppermute(value, axis, [(i, i ^ bit) for i in range(n)])


def pick(values, index, axis=0):
    return lax.dynamic_index_in_dim(values, index, axis, keepdims=False)


def after(values, *others):
    return lax.optimization_barrier((values, others))[0]


VMEM = pl.BlockSpec(memory_space=pltpu.VMEM)
SMEM = pl.BlockSpec(memory_space=pltpu.SMEM)


def bit_of(index, bit):
    return (index // bit) % 2


def add(a, b):
    return (a.astype(f32) + b.astype(f32)).astype(bf16)


CORE, FIRST, SECOND = 1, 2, 4


def first_halves_kernel(at_ref, row_keep, row_got, col_keep, col_got, *outs):
    columns = outs[0].shape[2]
    start = 0
    for keep, got in ((row_keep, row_got), (col_keep, col_got)):
        total = add(keep[0], got[0])
        n = total.shape[0] // 2
        low, high = total[:n], total[n:]
        for side in range(2):
            cols = slice(side * columns, (side + 1) * columns)
            mine = at_ref[side] == 0
            outs[2 * side][0, start : start + n] = jnp.where(mine, high, low)[:, cols]
            outs[2 * side + 1][0, start : start + n] = jnp.where(mine, low, high)[:, cols]
        start += n


def first_halves(at, row_keep, row_got, col_keep, col_got):
    sp, rows, width = row_keep.shape
    cols = col_keep.shape[1]

    def spec(a):
        return pl.BlockSpec((1,) + a.shape[1:], lambda s, t: (s, 0, 0))

    out = jax.ShapeDtypeStruct((sp, (rows + cols) // 2, width // 2), bf16)
    return pl.pallas_call(
        first_halves_kernel,
        grid_spec=pltpu.PrefetchScalarGridSpec(
            num_scalar_prefetch=1,
            grid=(sp,),
            in_specs=[spec(a) for a in (row_keep, row_got, col_keep, col_got)],
            out_specs=[spec(out)] * 4,
        ),
        out_shape=[out] * 4,
        cost_estimate=COVER,
        name="first_halves",
    )(at, row_keep, row_got, col_keep, col_got)


def second_halves_kernel(at_ref, *refs):
    for side in range(2):
        mine = at_ref[1 - side]
        keep, got = refs[2 * side : 2 * side + 2]
        for s in range(keep.shape[0]):
            refs[4 + 2 * side][s] = add(keep[s, 1 - mine], got[s, 1 - mine])
            refs[5 + 2 * side][s] = add(keep[s, mine], got[s, mine])


def second_halves(at, *arrays):
    sp, rows, columns = arrays[0].shape
    out = jax.ShapeDtypeStruct((sp, rows // 2, columns), bf16)
    return pl.pallas_call(
        second_halves_kernel,
        in_specs=[SMEM] + [VMEM] * 4,
        out_specs=[VMEM] * 4,
        out_shape=[out] * 4,
        cost_estimate=COVER,
        name="second_halves",
    )(at, *[a.reshape(sp, 2, rows // 2, columns) for a in arrays])


def near_halves_kernel(at_ref, *refs, terms, sides):
    ins, outs = refs[:-2], refs[-2:]
    mine = lax.rem(at_ref[2], 2)
    for out, bit in zip(outs, (1 - mine, mine)):
        for s in range(out.shape[0]):
            at = 0
            for side in range(sides):
                total = None
                for ref in ins[side * terms : (side + 1) * terms]:
                    value = ref[2 * s + bit].astype(f32)
                    total = value if total is None else total + value
                out[s, :, at : at + total.shape[1]] = total.astype(bf16)
                at += total.shape[1]


def near_halves(at, sides):
    terms = len(sides[0])
    flat = [a for side in sides for a in side]
    sp, rows, _ = flat[0].shape
    width = sum(side[0].shape[2] for side in sides)
    out = jax.ShapeDtypeStruct((sp // 2, rows, width), bf16)
    return pl.pallas_call(
        functools.partial(near_halves_kernel, terms=terms, sides=len(sides)),
        in_specs=[SMEM] + [VMEM] * len(flat),
        out_specs=[VMEM] * 2,
        out_shape=[out] * 2,
        cost_estimate=COVER,
        name="near_halves",
    )(at, *flat)


def far_halves_kernel(at_ref, keep, got, send_ref, keep_ref):
    mine = lax.div(at_ref[2], 2)
    send_ref[...] = add(keep[1 - mine], got[1 - mine])
    keep_ref[...] = add(keep[mine], got[mine])


def far_halves(at, keep, got):
    out = jax.ShapeDtypeStruct(keep.shape[1:], bf16)
    return pl.pallas_call(
        far_halves_kernel,
        in_specs=[SMEM] + [VMEM] * 2,
        out_specs=[VMEM] * 2,
        out_shape=[out] * 2,
        cost_estimate=COVER,
        name="far_halves",
    )(at, keep, got)


def hand_over_kernel(in_ref, out_ref):
    out_ref[...] = in_ref[...].astype(out_ref.dtype)


def widen(value):
    return hand_over(value, f32)


def hand_over(value, dtype=bf16):
    block = pl.BlockSpec((1,) + value.shape[1:], lambda i: (i, 0, 0))
    return pl.pallas_call(
        hand_over_kernel,
        grid=(value.shape[0],),
        in_specs=[block],
        out_specs=block,
        out_shape=jax.ShapeDtypeStruct(value.shape, dtype),
        cost_estimate=COVER,
        name="hand_over",
    )(value)


def own_kernel(keep_ref, got_ref, out_ref):
    out_ref[...] = add(keep_ref[...], got_ref[...])


def own_sum(keep, got):
    return pl.pallas_call(
        own_kernel,
        in_specs=[VMEM] * 2,
        out_specs=VMEM,
        out_shape=jax.ShapeDtypeStruct(keep.shape, bf16),
        cost_estimate=COVER,
        name="own_sum",
    )(keep, got)


def quarters_kernel(at_ref, keep_ref, got_ref, *outs):
    for i, out in enumerate(outs):
        index = 2 * (at_ref[0] ^ (i // 2)) + (at_ref[1] ^ (i % 2))
        for s in range(keep_ref.shape[0]):
            out[s] = add(keep_ref[s, index], got_ref[s, index])


def quarters(at, keep, got):
    sp, rows, width = keep.shape
    out = jax.ShapeDtypeStruct((sp, rows // 4, width), bf16)
    return pl.pallas_call(
        quarters_kernel,
        in_specs=[SMEM] + [VMEM] * 2,
        out_specs=[VMEM] * 4,
        out_shape=[out] * 4,
        cost_estimate=COVER,
        name="quarters",
    )(at, keep.reshape(sp, 4, rows // 4, width), got.reshape(sp, 4, rows // 4, width))


def four_chips_kernel(at_ref, *refs, crossed):
    pieces, out_ref = refs[:4], refs[4]
    columns = out_ref.shape[2] // 2
    for i, piece in enumerate(pieces):
        x, y = at_ref[0] ^ (i // 2), at_ref[1] ^ (i % 2)
        out_ref[2 * x + y, :, :columns] = piece[:, :columns]
        out_ref[2 * y + x if crossed else 2 * x + y, :, columns:] = piece[:, columns:]


def four_chips(at, pieces, crossed):
    rows, width = pieces[0].shape
    return pl.pallas_call(
        functools.partial(four_chips_kernel, crossed=crossed),
        in_specs=[SMEM] + [VMEM] * 4,
        out_specs=VMEM,
        out_shape=jax.ShapeDtypeStruct((4, rows, width), bf16),
        cost_estimate=COVER,
        name="four_chips",
    )(at, *pieces).reshape(4 * rows, width)


def spread(own):
    return [own] + [pair_permute(own, bit) for bit in (SECOND, FIRST, FIRST + SECOND)]


def finish_kernel(core_ref, mine_ref, other_ref, *outs, half, layout):
    first = core_ref[0] == 0
    width = mine_ref.shape[1]
    for out, (_, across, starts) in zip(outs, layout):
        for n, at in enumerate(starts):
            cols = slice(n % across * width, (n % across + 1) * width)
            mine = mine_ref[at : at + half].astype(f32)
            other = other_ref[at : at + half].astype(f32)
            to = n // across * 2 * half
            out[to : to + half, cols] = jnp.where(first, mine, other)
            out[to + half : to + 2 * half, cols] = jnp.where(first, other, mine)


def finish(core, mine, other, half, layout):
    width = mine.shape[1]
    shapes = [(2 * half * down, width * across) for down, across, _ in layout]
    return pl.pallas_call(
        functools.partial(finish_kernel, half=half, layout=layout),
        grid=(1,),
        in_specs=[SMEM] + [VMEM] * 2,
        out_specs=[pl.BlockSpec(s, lambda i: (0, 0)) for s in shapes],
        out_shape=[jax.ShapeDtypeStruct(s, f32) for s in shapes],
        cost_estimate=COVER,
        name="finish",
    )(core, mine, other)


def late_row_kernel(sums_ref, parts_ref, mod_ref, ada_ref, timing_ref, row_ref):
    width = sums_ref.shape[1]
    cond = timing_ref.shape[1]
    shift, scaled = sums_ref[0:1, :], sums_ref[1:2, :]
    scale = scaled * mod_ref[0:1, :]
    row = jnp.concatenate([shift, scale] + [parts_ref[i : i + 1, :] for i in range(4)], axis=1)
    high = row.astype(bf16)
    low = (row - high.astype(f32)).astype(bf16)
    time = dot_nt(high, ada_ref[...]) + dot_nt(low, ada_ref[...])
    row_ref[:, :width] = shift.astype(bf16)
    row_ref[:, width : 2 * width] = scale.astype(bf16)
    row_ref[:, 2 * width : 3 * width] = (scaled * mod_ref[1:2, :]).astype(bf16)
    row_ref[:, 3 * width : 3 * width + cond] = time.astype(bf16)
    row_ref[:, 3 * width + cond :] = timing_ref[...]


def late_row(sums, parts, mods, ada, timing):
    columns = 3 * sums.shape[1] + 2 * timing.shape[1]
    return pl.pallas_call(
        late_row_kernel,
        in_specs=[VMEM] * 5,
        out_specs=VMEM,
        out_shape=jax.ShapeDtypeStruct((1, columns), bf16),
        cost_estimate=COVER,
        name="late_row",
    )(sums, parts, mods, ada, timing)


def vector_outputs_kernel(
    at_ref, rows_ref, vector_ref, ada_ref, bias_ref, attn_gain_ref, mlp_gain_ref, up_ref, down_ref,
    grad_ref, *, half, sp,
):
    count, width = ada_ref.shape[0], vector_ref.shape[1]
    quarter = width // sp
    me = at_ref[2]
    grad_ref[...] = dot_tn(
        rows_ref[:, 3 * width + grad_ref.shape[0] :], rows_ref[:, : 2 * width]
    ).reshape(grad_ref.shape)
    ada_ref[:, : 2 * width] = grad_ref[pl.ds(pl.multiple_of(me * count, count), count), :]
    for p in range(4):
        start = p // 2 * half + p % 2 * count
        ada_ref[:, (2 + p) * width : (3 + p) * width] = vector_ref[start : start + count, :]
    totals = column_sum(rows_ref[:, : 3 * width].astype(f32))
    row = 2 * count
    own = bias_ref.shape[1]
    late_bias = jnp.concatenate([totals[:, : 2 * width], jnp.zeros((1, 4 * width), f32)], axis=1)
    bias, gain = late_bias[:, :own], totals[:, 2 * width : 2 * width + quarter]
    for s in range(1, sp):
        bias = jnp.where(me == s, late_bias[:, s * own : (s + 1) * own], bias)
        at = 2 * width + s * quarter
        gain = jnp.where(me == s, totals[:, at : at + quarter], gain)
    bias_ref[:, :width] = bias[:, :width] + vector_ref[row + 1 : row + 2, :]
    bias_ref[:, width:] = bias[:, width:] + vector_ref[half + row + 1 : half + row + 2, : own - width]
    attn_gain_ref[...] = gain
    up_ref[...] = vector_ref[row : row + 1, :]
    mlp_gain_ref[...] = vector_ref[half + row : half + row + 1, :quarter]
    down_ref[...] = vector_ref[half + row : half + row + 1, quarter : 2 * quarter]


def vector_outputs(at, rows, vectors, half, cond, sp):
    width = vectors.shape[1]
    quarter = width // sp
    shapes = [(cond // sp, 6 * width), (1, 6 * width // sp), (1, quarter), (1, quarter), (1, width), (1, quarter)]
    return pl.pallas_call(
        functools.partial(vector_outputs_kernel, half=half, sp=sp),
        in_specs=[SMEM] + [VMEM] * 2,
        out_specs=[VMEM] * 6,
        out_shape=[jax.ShapeDtypeStruct(s, f32) for s in shapes],
        scratch_shapes=[pltpu.VMEM((cond, 2 * width), f32)],
        cost_estimate=COVER,
        name="vector_outputs",
    )(at, rows, vectors)


def sum_over_rest(total):
    bit = 2 * SECOND
    while bit < lax.axis_size("dp"):
        total = add(total, pair_permute(total, bit))
        bit *= 2
    return total


def double(rows, bit, axis):
    return jnp.concatenate([rows, pair_permute(rows, bit, axis)], axis=0)


def bits(axis):
    n, bit = lax.axis_size(axis), 1
    while bit < n:
        yield bit
        bit *= 2


def body(
    hidden_in,
    time_embed,
    ada_weight,
    ada_bias,
    attn_gain,
    query_key_value_matrix,
    attention_output_matrix,
    mlp_gain,
    up_projection_matrix,
    up_bias,
    down_projection_matrix,
    down_bias,
    out_cotangent,
):
    sequences, local_len, width = hidden_in.shape
    sp, me = lax.axis_size("sp"), lax.axis_index("sp")
    assert sequences == sp
    def exchange(values):
        values = values.reshape(sp, local_len, width)
        return lax.all_to_all(values, "sp", split_axis=0, concat_axis=0, tiled=True)

    x = exchange(hidden_in).reshape(-1, width)
    cot = exchange(after(out_cotangent, x)).reshape(-1, width)
    here = lax.axis_index("dp")
    core = bit_of(here, CORE).reshape(1)
    at = jnp.stack([bit_of(here, FIRST), bit_of(here, SECOND), me])

    timing = lax.dynamic_slice_in_dim(time_embed, me, 1, 0)
    modulation = dot_nn(timing, ada_weight) + ada_bias.astype(f32)[None]
    shift_attn, scale_attn, gate_attn, shift_mlp, scale_mlp, gate_mlp = jnp.split(
        modulation, 6, axis=-1
    )
    gain_attn = attn_gain.astype(f32)[None]
    gain_mlp = mlp_gain.astype(f32)[None]
    zero = jnp.zeros_like(shift_attn)
    attn_mods = jnp.concatenate(
        [gain_attn * (1.0 + scale_attn), shift_attn] + [zero] * 6, axis=0
    )
    mlp_mods = jnp.concatenate(
        [gate_attn, gain_mlp * (1.0 + scale_mlp), shift_mlp, gate_mlp, down_bias.astype(f32)[None]]
        + [zero] * 3,
        axis=0,
    )
    lane = lax.broadcasted_iota(jnp.int32, (1, LANES), 1)
    frequency = 10000.0 ** (-((lane % HALF).astype(f32) * 2.0 / HEAD_DIM))
    row = lax.broadcasted_iota(jnp.int32, (sp * local_len, 1), 0)
    angles = row.astype(f32) * frequency
    cos, sin = jnp.cos(angles), jnp.sin(angles)

    xm_attn, q, k, v = project_qkv(x, attn_mods, query_key_value_matrix, cos, sin)
    mixed, lse = attention_forward(q, k, v)
    both_in, act, gd, both_grad, gm, gmix, sums, up_sum, out = feed_forward(
        x,
        mixed,
        cot,
        mlp_mods,
        up_bias.astype(f32)[None],
        attention_output_matrix,
        up_projection_matrix,
        down_projection_matrix,
        local_len,
    )
    ff = up_bias.shape[0]
    assert ff == sp * width
    n_up = ff // width
    half = width // sp // 2
    quarter = width // sp
    cond = timing.shape[1]
    column = timing.astype(f32).reshape(cond, 1)

    def shards(row):
        return row.reshape(sp, -1)

    def sum_rows(rows):
        filled = [
            jnp.stack([jnp.pad(r, ((0, 0), (0, width - r.shape[1]))) for r in side], axis=1)
            for side in rows
        ]
        return jnp.stack([jnp.pad(f, ((0, 0), (0, 16 - f.shape[1]), (0, 0))) for f in filled])

    output = exchange(out)
    col_send, col_keep = column_grad(core, both_in, both_grad, sp, n_up + 2, n_up)
    early_parts = jnp.concatenate([sums[4:5], sums[2:3], sums[3:4] * gain_mlp, sums[0:1]], axis=0)
    six = 6 * width
    early_bias = jnp.concatenate([jnp.zeros((2 * width,), f32), early_parts.reshape(-1)])
    early_bias = shards(early_bias)
    early_sums = sum_rows(
        [
            [shards(up_sum), early_bias[:, :width]],
            [
                jnp.concatenate(
                    [shards(sums[3:4] * (1.0 + scale_mlp)), shards(sums[1:2])], axis=1
                ),
                early_bias[:, width:],
            ],
        ]
    )
    col_send, col_keep = vector_grad(core, column, early_parts, early_sums, col_send, col_keep, half)
    col_got = pair_permute(col_send, CORE)
    row_send, row_keep = row_grad(core, *after((act, gd), col_keep), sp)
    row_got = pair_permute(row_send, CORE)

    pairs = width // LANES

    def backward(start, stop, into=None):
        return attention_backward(
            q, k, v, gmix, mixed, lse, cos, sin, start, stop - start, into
        )

    left_send, left, right_send, right = first_halves(at, row_keep, row_got, col_keep, col_got)
    left_got, right_got = pair_permute(left_send, FIRST), pair_permute(right_send, SECOND)
    gmix = after(gmix, left, right)
    grads = backward(0, pairs)
    left_got, right_got, output = after((left_got, right_got, output), grads)
    left_send, left, right_send, right = second_halves(at, left, left_got, right, right_got)
    left_got, right_got = pair_permute(left_send, SECOND), pair_permute(right_send, FIRST)
    grads = after(grads, left, right, output)

    attn_sums, hg, late_send, late_keep = late_grads(
        core, x, grads, gm, attn_mods, query_key_value_matrix, xm_attn, sp, local_len
    )
    hidden_grad = exchange(hg)
    row_mods = jnp.concatenate([gain_attn, 1.0 + scale_attn] + [zero] * 6, axis=0)
    late_got = pair_permute(late_send, CORE)
    left_got, right_got = after((left_got, right_got), late_keep)
    if lax.axis_size("dp") > 2 * SECOND:
        left, right = sum_over_rest(add(left, left_got)), sum_over_rest(add(right, right_got))
        sides = [(left,), (right,)]
    else:
        sides = [(left, left_got), (right, right_got)]
    near_send, near = near_halves(at, sides)
    near_got = pair_permute(near_send, 1, "sp")
    rows = late_row(after(attn_sums, near), early_parts, row_mods, ada_weight, timing)
    late_got = after(late_got, rows)
    own_quarter, *other_quarters = quarters(at, late_keep, late_got)
    quarter_parts = [own_quarter] + [
        pair_permute(p, bit)
        for p, bit in zip(other_quarters, (SECOND, FIRST, FIRST + SECOND))
    ]
    rows = after(rows, own_quarter)
    for bit in bits("dp"):
        rows = double(rows, bit, "dp")
    near_got, hidden_grad = after((near_got, hidden_grad), rows)
    far_send, far = far_halves(at, near, after(near_got, hidden_grad))
    far_got = pair_permute(far_send, 2, "sp")
    quarter_parts = after(quarter_parts, far)
    if lax.axis_size("dp") > 2 * SECOND:
        total = sum(p.astype(f32) for p in quarter_parts).astype(bf16)
        quarter_parts = [sum_over_rest(total)]
    late_near_send, late_near = near_halves(at, [quarter_parts])
    late_near_got = pair_permute(late_near_send, 1, "sp")
    rows = double(after(rows, late_near), 1, "sp")
    output = hand_over(after(output, late_near))
    late_near_got = after(late_near_got, rows, output)
    late_far_send, late_far = far_halves(at, late_near, late_near_got)
    late_far_got = pair_permute(late_far_send, 2, "sp")
    early_own = own_sum(far, after(far_got, late_far))
    early_four = spread(early_own)
    rows = double(after(rows, early_own), 2, "sp")
    late_own = own_sum(late_far, after(late_far_got, rows))
    hidden_grad = widen(after(hidden_grad, late_own))
    early_half = four_chips(at, after(early_four, hidden_grad), True)
    early_other = pair_permute(early_half, CORE)
    late_four = spread(after(late_own, early_half))
    time_rows = rows[:: lax.axis_size("dp"), 3 * width : 3 * width + cond]
    time_grad = jnp.concatenate([pick(time_rows, me ^ s)[None] for s in range(sp)], axis=0)
    n_row, n_col = row_keep.shape[1] // 2, col_keep.shape[1] // 2
    row_starts = [x * (n_row + n_col) + i for x in range(2) for i in range(0, n_row, half)]
    col_starts = [x * (n_row + n_col) + n_row + i for x in range(2) for i in range(0, n_col, half)]
    down_grad, up_grad, proj_grad, vectors = finish(
        core,
        early_half,
        after(early_other, late_four[0]),
        half,
        (
            (sp, 1, row_starts),
            (1, n_up, col_starts[:n_up]),
            (1, 1, col_starts[n_up : n_up + 1]),
            (1, 1, col_starts[n_up + 1 :]),
        ),
    )
    late_half = four_chips(at, after(late_four, down_grad), False)
    late_other = pair_permute(late_half, CORE)
    ada_weight_grad, *small = vector_outputs(at, after(rows, late_half), vectors, half, cond, sp)
    (qkv_grad,) = finish(
        core, late_half, after(late_other, ada_weight_grad), half, ((1, 3, [0, half, 2 * half]),)
    )
    ada_bias_grad, attn_gain_grad, mlp_gain_grad, up_bias_grad, down_bias_grad = (
        v.reshape(-1) for v in small
    )
    time_grad = time_grad.astype(f32)
    return (
        output,
        hidden_grad,
        time_grad,
        ada_weight_grad,
        ada_bias_grad,
        attn_gain_grad,
        qkv_grad,
        proj_grad,
        mlp_gain_grad,
        up_grad,
        up_bias_grad,
        down_grad,
        down_bias_grad,
    )


def solution(mesh):
    return jax.shard_map(
        body,
        mesh=mesh,
        in_specs=(P("dp", "sp", None), P("dp", None)) + (P(),) * 10 + (P("dp", "sp", None),),
        out_specs=(
            P("dp", "sp", None),
            P("dp", "sp", None),
            P("dp", None),
            P("sp", None),
            P("sp"),
            P("sp"),
            P("sp", None),
            P("sp", None),
            P("sp"),
            P("sp", None),
            P("sp"),
            P("sp", None),
            P("sp"),
        ),
        check_vma=False,
    )
```

```python
import functools

import jax
import jax.numpy as jnp
from jax import lax
from jax.experimental import pallas as pl
from jax.experimental.pallas import tpu as pltpu
from jax.sharding import PartitionSpec as P

HEAD_DIM = 64
VMEM = pl.BlockSpec(memory_space=pltpu.VMEM)
SMEM = pl.BlockSpec(memory_space=pltpu.SMEM)
HALF = HEAD_DIM // 2
LANES = 128
EPSILON = 1e-05
LOG2E = 1.4426950408889634
SCALE = HEAD_DIM ** (-0.5)
f32 = jnp.float32
COVER = pl.CostEstimate(flops=40_000_000_000, bytes_accessed=100_000_000, transcendentals=0)
bf16 = jnp.bfloat16


def dot_nn(a, b):
    return lax.dot_general(a, b, (((1,), (0,)), ((), ())), preferred_element_type=f32)


def dot_nt(a, b):
    return lax.dot_general(a, b, (((1,), (1,)), ((), ())), preferred_element_type=f32)


def dot_tn(a, b):
    return lax.dot_general(a, b, (((0,), (0,)), ((), ())), preferred_element_type=f32)


def column_sum(values):
    return jnp.sum(values, axis=0, keepdims=True)


def norm_forward(values):
    center = values - jnp.mean(values, axis=-1, keepdims=True)
    inverse = lax.rsqrt(jnp.mean(center * center, axis=-1, keepdims=True) + EPSILON)
    return center * inverse, inverse


def norm_backward(grad, normed, inverse):
    first = jnp.mean(grad, axis=-1, keepdims=True)
    second = jnp.mean(grad * normed, axis=-1, keepdims=True)
    return inverse * (grad - first - normed * second)


def swap_halves(values):
    lane = lax.broadcasted_iota(jnp.int32, (1, LANES), 1)
    lower = (lane & (HEAD_DIM - 1)) < HALF
    up = pltpu.roll(values, LANES - HALF, 1)
    down = pltpu.roll(values, HALF, 1)
    return lower, up, down


def rotary(values, cos, sin):
    lower, up, down = swap_halves(values)
    return values * cos + jnp.where(lower, -up, down) * sin


def unrotary(values, cos, sin):
    lower, up, down = swap_halves(values * sin)
    return values * cos + jnp.where(lower, up, -down)


def qkv_kernel(x_ref, mod_ref, w_ref, cos_ref, sin_ref, xm_ref, q_ref, k_ref, v_ref):
    width = x_ref.shape[1]
    normed, _ = norm_forward(x_ref[...].astype(f32))
    xm = (normed * mod_ref[0:1, :] + mod_ref[1:2, :]).astype(bf16)
    xm_ref[...] = xm
    cos, sin = cos_ref[...], sin_ref[...]
    for part, ref in enumerate((q_ref, k_ref, v_ref)):
        whole = dot_nn(xm, w_ref[:, part * width : (part + 1) * width]).astype(bf16)
        if part == 2:
            ref[...] = whole
            continue
        for lane in range(0, width, LANES):
            piece = whole[:, lane : lane + LANES].astype(f32)
            ref[:, lane : lane + LANES] = rotary(piece, cos, sin).astype(bf16)


def project_qkv(x, mods, weight, cos, sin, rows=256):
    length, width = x.shape
    block = pl.BlockSpec((rows, width), lambda i: (i, 0))
    table = pl.BlockSpec((rows, LANES), lambda i: (i, 0))
    shape = jax.ShapeDtypeStruct((length, width), bf16)
    return pl.pallas_call(
        qkv_kernel,
        grid=(length // rows,),
        in_specs=[
            block,
            VMEM,
            VMEM,
            table,
            table,
        ],
        out_specs=[block] * 4,
        out_shape=[shape] * 4,
        cost_estimate=COVER,
        name="project_qkv",
    )(x, mods, weight, cos, sin)


def attention_forward_kernel(q_ref, k_ref, v_ref, o_ref, lse_ref, *, chunk, ahead):
    k, v = k_ref[...], v_ref[...]
    first = lax.broadcasted_iota(jnp.int32, (1, LANES), 1) < HEAD_DIM
    c = LOG2E * SCALE
    masks = (first, ~first)
    keys = [jnp.where(m, k, jnp.zeros_like(k)) for m in masks]
    values = [jnp.where(m, v, jnp.ones_like(v)) for m in masks]
    items = [(h, start) for start in range(0, q_ref.shape[0], chunk) for h in range(2)]

    def scores(h, start):
        return dot_nt(keys[h], q_ref[start : start + chunk, :])

    waiting = [scores(*item) for item in items[:ahead]]
    outs = {}
    for i, (h, start) in enumerate(items):
        st = waiting.pop(0)
        if i + ahead < len(items):
            waiting.append(scores(*items[i + ahead]))
        rows = slice(start, start + chunk)
        top = jnp.max(st, axis=0, keepdims=True) * c
        p = jnp.exp2(st * c - top).astype(bf16)
        ot = dot_tn(values[h], p)
        own, ones = (ot[:HEAD_DIM], ot[HEAD_DIM:]) if h == 0 else (ot[HEAD_DIM:], ot[:HEAD_DIM])
        total = ones[0:1]
        outs[h] = own * (1.0 / total)
        lse_ref[0, h : h + 1, rows] = top + jnp.log2(total)
        if h == 1:
            o_ref[rows, :] = jnp.concatenate([outs[0], outs[1]], axis=0).T.astype(bf16)


def attention_forward(q, k, v):
    length, width = q.shape
    pairs = width // LANES
    block = pl.BlockSpec((length, LANES), lambda i: (0, i))
    return pl.pallas_call(
        functools.partial(attention_forward_kernel, chunk=length // 2, ahead=2),
        grid=(pairs,),
        in_specs=[block] * 3,
        out_specs=[block, pl.BlockSpec((1, 2, length), lambda i: (i, 0, 0))],
        out_shape=[
            jax.ShapeDtypeStruct((length, width), bf16),
            jax.ShapeDtypeStruct((pairs, 2, length), f32),
        ],
        cost_estimate=COVER,
        name="attention_forward",
    )(q, k, v)


def attention_backward_kernel(
    q_ref, k_ref, v_ref, do_ref, o_ref, lse_ref, cos_ref, sin_ref, *rest
):
    g_ref = rest[-1]
    first = lax.broadcasted_iota(jnp.int32, (1, LANES), 1) < HEAD_DIM
    upper = lax.broadcasted_iota(jnp.int32, (LANES, 1), 0) < HEAD_DIM
    c = LOG2E * SCALE
    q, k, v, do = q_ref[...], k_ref[...], v_ref[...], do_ref[...]
    prod = (do.astype(f32) * o_ref[...].astype(f32)).T
    kt = k.T
    zero = jnp.zeros_like(k)
    dq = dk = dv = None
    for h in range(2):
        mine = first if h == 0 else ~first
        row = column_sum(prod[h * HEAD_DIM : (h + 1) * HEAD_DIM])
        st = dot_nt(jnp.where(mine, k, zero), q)
        p = jnp.exp2(st * c - lse_ref[0, h : h + 1, :])
        dp = dot_nt(jnp.where(mine, v, zero), do)
        ds = (p * (dp - row)).astype(bf16)
        dvh = dot_nn(p.astype(bf16), jnp.where(mine, do, zero))
        dkh = dot_nn(ds, jnp.where(mine, q, zero))
        dqh = dot_nn(jnp.where(upper if h == 0 else ~upper, kt, jnp.zeros_like(kt)), ds)
        dq, dk, dv = (dqh, dkh, dvh) if h == 0 else (dq + dqh, dk + dkh, dv + dvh)
    cos, sin = cos_ref[...], sin_ref[...]
    g_ref[0] = unrotary(dq.T * SCALE, cos, sin).astype(bf16)
    g_ref[1] = unrotary(dk * SCALE, cos, sin).astype(bf16)
    g_ref[2] = dv.astype(bf16)


def attention_backward(q, k, v, do, o, lse, cos, sin, start, count, into=None):
    length, width = q.shape
    block = pl.BlockSpec((length, LANES), lambda i: (0, start + i))
    table = pl.BlockSpec((length, LANES), lambda i: (0, 0))
    extra = [] if into is None else [into]
    return pl.pallas_call(
        attention_backward_kernel,
        grid=(count,),
        in_specs=[block] * 5
        + [pl.BlockSpec((1, 2, length), lambda i: (start + i, 0, 0)), table, table]
        + [pl.BlockSpec(memory_space=pl.ANY)] * len(extra),
        out_specs=pl.BlockSpec((3, length, LANES), lambda i: (0, 0, start + i)),
        out_shape=jax.ShapeDtypeStruct((3, length, width), bf16),
        input_output_aliases={8: 0} if extra else {},
        cost_estimate=COVER,
        name="attention_backward",
    )(q, k, v, do, o, lse, cos, sin, *extra)


def mlp_kernel(
    x_ref, mixed_ref, cot_ref, mod_ref, bias_ref, wo_ref, wu_ref, wd_ref,
    xm_ref, act_ref, gd_ref, gp_ref, gm_ref, gmix_ref, sum_ref, up_sum_ref, out_ref,
):
    chunk, ff = wu_ref.shape
    gate_attn, scaled, shift = mod_ref[0:1, :], mod_ref[1:2, :], mod_ref[2:3, :]
    gate_mlp, down_bias = mod_ref[3:4, :], mod_ref[4:5, :]
    cot = cot_ref[...].astype(f32)
    projected = dot_nn(mixed_ref[...], wo_ref[...])
    middle = x_ref[...].astype(f32) + gate_attn * projected
    normed, inverse = norm_forward(middle)
    xm = (normed * scaled + shift).astype(bf16)
    xm_ref[0] = xm
    xm_ref[1] = mixed_ref[...]
    gd = (gate_mlp * cot).astype(bf16)
    gd_ref[...] = gd
    down = grad_mod = None
    c0 = 0.7978845608028654
    c1 = c0 * 0.044715
    up_sums = []
    for at in range(0, ff, chunk):
        cols = slice(at, at + chunk)
        pre = dot_nn(xm, wu_ref[:, cols]) + bias_ref[:, cols]
        square = pre * pre
        t = jnp.tanh(pre * (c0 + c1 * square))
        half = 0.5 + 0.5 * t
        wide_act = pre * half
        act = wide_act.astype(bf16)
        act_ref[:, cols] = act
        slope = half + wide_act * (1.0 - half) * (2.0 * c0 + (6.0 * c1) * square)
        wide_gp = slope * dot_nt(gd, wd_ref[cols, :])
        gp = wide_gp.astype(bf16)
        gp_ref[at // chunk] = gp
        up_sums.append(column_sum(wide_gp))
        d = dot_nn(act, wd_ref[cols, :])
        g = dot_nt(gp, wu_ref[:, cols])
        down, grad_mod = (d, g) if down is None else (down + d, grad_mod + g)
    down = down + down_bias
    out_ref[...] = (middle + gate_mlp * down).astype(bf16)
    gm = cot + norm_backward(grad_mod * scaled, normed, inverse)
    gm_ref[...] = gm
    gpj = (gate_attn * gm).astype(bf16)
    gp_ref[ff // chunk] = gpj
    gmix_ref[...] = dot_nt(gpj, wo_ref[...]).astype(bf16)
    sums = jnp.concatenate(
        [
            column_sum(cot * down),
            column_sum(gd.astype(f32)),
            column_sum(grad_mod),
            column_sum(grad_mod * normed),
            column_sum(gm * projected),
            jnp.zeros((3, cot.shape[1]), f32),
        ],
        axis=0,
    )
    up_sum = jnp.concatenate(up_sums, axis=1)

    @pl.when(pl.program_id(0) == 0)
    def _():
        sum_ref[...] = sums
        up_sum_ref[...] = up_sum

    @pl.when(pl.program_id(0) > 0)
    def _():
        sum_ref[...] += sums
        up_sum_ref[...] += up_sum


def feed_forward(x, mixed, cot, mods, up_bias, wo, wu, wd, rows):
    length, width = x.shape
    ff = wu.shape[1]
    block = pl.BlockSpec((rows, width), lambda i: (i, 0))
    wide = pl.BlockSpec((rows, ff), lambda i: (i, 0))

    narrow = jax.ShapeDtypeStruct((length, width), bf16)
    broad = jax.ShapeDtypeStruct((length, ff), bf16)
    return pl.pallas_call(
        mlp_kernel,
        grid=(length // rows,),
        in_specs=[block, block, block] + [VMEM] * 5,
        out_specs=[
            pl.BlockSpec((2, rows, width), lambda i: (0, i, 0)),
            wide,
            block,
            pl.BlockSpec((ff // width + 1, rows, width), lambda i: (0, i, 0)),
            block,
            block,
            pl.BlockSpec((8, width), lambda i: (0, 0)),
            pl.BlockSpec((1, ff), lambda i: (0, 0)),
        ]
        + [block],
        out_shape=[
            jax.ShapeDtypeStruct((2, length, width), bf16), broad, narrow,
            jax.ShapeDtypeStruct((ff // width + 1, length, width), bf16),
            jax.ShapeDtypeStruct((length, width), f32), narrow,
            jax.ShapeDtypeStruct((8, width), f32), jax.ShapeDtypeStruct((1, ff), f32),
        ]
        + [narrow],
        cost_estimate=COVER,
        name="feed_forward",
    )(x, mixed, cot, mods, up_bias, wo, wu, wd)


def late_grads_kernel(
    core_ref, x_ref, tile_ref, gm_ref, mod_ref, w_ref, xm_ref, ada_ref, timing_ref, early_ref, block_ref,
    time_ref, hg_ref, send_ref, keep_ref, turned_ref, sum_ref, *, tiles, parts,
):
    step = pl.program_id(0)
    width = x_ref.shape[1]

    @pl.when(step < tiles)
    def _():
        normed, inverse = norm_forward(x_ref[...].astype(f32))
        grad = None
        for part in range(3):
            g = dot_nt(tile_ref[part], w_ref[:, part * width : (part + 1) * width])
            grad = g if grad is None else grad + g
        hg = gm_ref[...] + norm_backward(grad * mod_ref[0:1, :], normed, inverse)
        hg_ref[...] = hg.astype(bf16)
        sums = jnp.concatenate(
            [column_sum(grad), column_sum(grad * normed), jnp.zeros((6, width), f32)], axis=0
        )

        @pl.when(step == 0)
        def _():
            sum_ref[...] = sums

        @pl.when(step > 0)
        def _():
            sum_ref[...] += sums

    @pl.when(step == tiles)
    def _():
        turned_ref[...] = xm_ref[...].T

    @pl.when((step >= tiles) & (step < tiles + parts))
    def _():
        product = dot_nn(turned_ref[...], block_ref[0])
        half = send_ref.shape[1]
        for i, (send, keep) in enumerate(split_halves(product, half, core_ref[0] == 0)):
            send_ref[i] = send
            keep_ref[i] = keep

    @pl.when(step == tiles + parts)
    def _():
        sp, half, _ = send_ref.shape
        shift, scaled = sum_ref[0:1, :], sum_ref[1:2, :]
        scale = scaled * mod_ref[2:3, :]
        gain = scaled * mod_ref[3:4, :]
        row = jnp.concatenate([shift, scale] + [early_ref[i : i + 1, :] for i in range(4)], axis=1)
        high = row.astype(bf16)
        low = (row - high.astype(f32)).astype(bf16)
        time_ref[...] = (dot_nt(high, ada_ref[...]) + dot_nt(low, ada_ref[...])).astype(bf16)
        bias = jnp.concatenate([shift, scale, jnp.zeros((1, 4 * width), f32)], axis=1)
        count, own, quarter = timing_ref.shape[0] // sp, 6 * width // sp, width // sp
        for ref, first in ((send_ref, core_ref[0] == 1), (keep_ref, core_ref[0] == 0)):
            part = jnp.where(first, shift, scale)
            for i in range(sp):
                ref[i, :count] = (timing_ref[i * count : (i + 1) * count, :] * part).astype(bf16)
                mine = bias[:, i * own : (i + 1) * own]
                rest = jnp.concatenate(
                    [
                        mine[:, width:],
                        gain[:, i * quarter : (i + 1) * quarter],
                        jnp.zeros((1, 2 * width - own - quarter), f32),
                    ],
                    axis=1,
                )
                sums = jnp.concatenate(
                    [jnp.where(first, mine[:, :width], rest), jnp.zeros((half - count - 1, width), f32)], axis=0
                )
                ref[i, count:] = sums.astype(bf16)


def late_grads(core, x, grads, gm, mods, weight, xm, ada, timing, early, sp, rows):
    length, width = x.shape
    tiles = length // rows
    n = grads.shape[0]
    half = width // sp // 2

    def tile(i, c):
        return (jnp.minimum(i, tiles - 1), 0)

    def part(i):
        return jnp.maximum(i - tiles, 0)

    def piece(i, c):
        return (jnp.minimum(part(i), n - 1), 0, 0)

    block = pl.BlockSpec((rows, width), tile)

    out = pl.BlockSpec((sp, half, width), lambda i, c: (0, part(i), 0))
    shape = jax.ShapeDtypeStruct((sp, (n + 1) * half, width), bf16)
    cond = timing.shape[0]
    return pl.pallas_call(
        functools.partial(late_grads_kernel, tiles=tiles, parts=n),
        grid_spec=pltpu.PrefetchScalarGridSpec(
            num_scalar_prefetch=1,
            grid=(tiles + n + 1,),
            in_specs=[
                block,
                pl.BlockSpec((n, rows, width), lambda i, c: (0, jnp.minimum(i, tiles - 1), 0)),
                block,
                VMEM,
                VMEM,
                VMEM,
                VMEM,
                VMEM,
                VMEM,
                pl.BlockSpec((1, length, width), piece),
            ],
            out_specs=[pl.BlockSpec((1, cond), lambda i, c: (0, 0)), block, out, out],
            scratch_shapes=[pltpu.VMEM((width, length), bf16), pltpu.VMEM((8, width), f32)],
        ),
        out_shape=[
            jax.ShapeDtypeStruct((1, cond), bf16),
            jax.ShapeDtypeStruct((length, width), bf16),
            shape,
            shape,
        ],
        cost_estimate=COVER,
        name="late_grads",
    )(core, x, grads, gm, mods, weight, xm, ada, timing, early, grads)


def split_halves(product, half, this_core):
    pieces = []
    for at in range(0, product.shape[0], 2 * half):
        low = product[at : at + half].astype(bf16)
        high = product[at + half : at + 2 * half].astype(bf16)
        pieces.append((jnp.where(this_core, high, low), jnp.where(this_core, low, high)))
    return pieces


def row_grad_kernel(core_ref, a_ref, b_ref, send_ref, keep_ref, *, half):
    product = dot_tn(a_ref[...], b_ref[...])
    for i, (send, keep) in enumerate(split_halves(product, half, core_ref[0] == 0)):
        send_ref[0, i * half : (i + 1) * half] = send
        keep_ref[0, i * half : (i + 1) * half] = keep


def row_grad(core, a, b, sp):
    length, width = b.shape
    out = jax.ShapeDtypeStruct((sp, width // 2, width), bf16)
    block = pl.BlockSpec((1, width // 2, width), lambda j, c: (j, 0, 0))
    return pl.pallas_call(
        functools.partial(row_grad_kernel, half=width // sp // 2),
        grid_spec=pltpu.PrefetchScalarGridSpec(
            num_scalar_prefetch=1,
            grid=(sp,),
            in_specs=[
                pl.BlockSpec((length, width), lambda j, c: (0, j)),
                pl.BlockSpec((length, width), lambda j, c: (0, 0)),
            ],
            out_specs=[block, block],
        ),
        out_shape=[out, out],
        cost_estimate=COVER,
        name="row_grad",
    )(core, a, b)


def column_grad_kernel(
    core_ref, sum_ref, up_sum_ref, mod_ref, timing_ref, a_ref, b_ref, send_ref, keep_ref, parts_ref, *, blocks
):
    step = pl.program_id(0)
    sp, half, width = send_ref.shape

    @pl.when(step < blocks)
    def _():
        product = dot_tn(a_ref[0], b_ref[0])
        for i, (send, keep) in enumerate(split_halves(product, half, core_ref[0] == 0)):
            send_ref[i] = send
            keep_ref[i] = keep

    @pl.when(step == blocks)
    def _():
        scaled = sum_ref[3:4, :]
        parts = [sum_ref[4:5, :], sum_ref[2:3, :], scaled * mod_ref[0:1, :], sum_ref[0:1, :]]
        for i, part in enumerate(parts):
            parts_ref[i : i + 1, :] = part
        gain = scaled * mod_ref[1:2, :]
        bias = jnp.concatenate([jnp.zeros((1, 2 * width), f32)] + parts, axis=1)
        count, own, quarter = timing_ref.shape[0] // sp, 6 * width // sp, width // sp
        for ref, first in ((send_ref, core_ref[0] == 1), (keep_ref, core_ref[0] == 0)):
            for i in range(sp):
                column = timing_ref[i * count : (i + 1) * count, :]
                for p in range(2):
                    part = jnp.where(first, parts[p], parts[p + 2])
                    ref[i, p * count : (p + 1) * count] = (column * part).astype(bf16)
                shard = slice(i * quarter, (i + 1) * quarter)
                mine = bias[:, i * own : (i + 1) * own]
                gains = jnp.concatenate(
                    [gain[:, shard], sum_ref[1:2, shard], jnp.zeros((1, width - 2 * quarter), f32)], axis=1
                )
                rest = jnp.concatenate([mine[:, width:], jnp.zeros((1, 2 * width - own), f32)], axis=1)
                sums = jnp.concatenate(
                    [
                        jnp.where(first, up_sum_ref[:, i * width : (i + 1) * width], gains),
                        jnp.where(first, mine[:, :width], rest),
                        jnp.zeros((half - 2 * count - 2, width), f32),
                    ],
                    axis=0,
                )
                ref[i, 2 * count :] = sums.astype(bf16)


def column_grad(core, sums, up_sum, mods, timing, a, b, sp, second):
    _, length, width = a.shape
    n = b.shape[0]
    half = width // sp // 2
    out = jax.ShapeDtypeStruct((sp, (n + 1) * half, width), bf16)
    block = pl.BlockSpec((sp, half, width), lambda j, c: (0, j, 0))
    return pl.pallas_call(
        functools.partial(column_grad_kernel, blocks=n),
        grid_spec=pltpu.PrefetchScalarGridSpec(
            num_scalar_prefetch=1,
            grid=(n + 1,),
            in_specs=[VMEM] * 4
            + [
                pl.BlockSpec((1, length, width), lambda j, c: (jnp.minimum(j, n - 1) // second, 0, 0)),
                pl.BlockSpec((1, length, width), lambda j, c: (jnp.minimum(j, n - 1), 0, 0)),
            ],
            out_specs=[block, block, pl.BlockSpec((4, width), lambda j, c: (0, 0))],
        ),
        out_shape=[out, out, jax.ShapeDtypeStruct((4, width), f32)],
        cost_estimate=COVER,
        name="column_grad",
    )(core, sums, up_sum, mods, timing, a, b)


def shift_permute(value, axis, by):
    n = lax.axis_size(axis)
    return lax.ppermute(value, axis, [(i, (i + by) % n) for i in range(n)])


def pair_permute(value, bit, axis="dp"):
    n = lax.axis_size(axis)
    return lax.ppermute(value, axis, [(i, i ^ bit) for i in range(n)])


def pick(values, index, axis=0):
    return lax.dynamic_index_in_dim(values, index, axis, keepdims=False)


def after(values, *others):
    return lax.optimization_barrier((values, others))[0]


def bit_of(index, bit):
    return (index // bit) % 2


def add(a, b):
    return (a.astype(f32) + b.astype(f32)).astype(bf16)


CORE, FIRST, SECOND = 1, 2, 4


def first_halves_kernel(at_ref, row_keep, row_got, col_keep, col_got, *outs):
    columns = outs[0].shape[2]
    start = 0
    for keep, got in ((row_keep, row_got), (col_keep, col_got)):
        total = add(keep[0], got[0])
        n = total.shape[0] // 2
        low, high = total[:n], total[n:]
        for side in range(2):
            cols = slice(side * columns, (side + 1) * columns)
            mine = at_ref[side] == 0
            outs[2 * side][0, start : start + n] = jnp.where(mine, high, low)[:, cols]
            outs[2 * side + 1][0, start : start + n] = jnp.where(mine, low, high)[:, cols]
        start += n


def first_halves(at, row_keep, row_got, col_keep, col_got):
    sp, rows, width = row_keep.shape
    cols = col_keep.shape[1]

    def spec(a):
        return pl.BlockSpec((1,) + a.shape[1:], lambda s, t: (s, 0, 0))

    out = jax.ShapeDtypeStruct((sp, (rows + cols) // 2, width // 2), bf16)
    return pl.pallas_call(
        first_halves_kernel,
        grid_spec=pltpu.PrefetchScalarGridSpec(
            num_scalar_prefetch=1,
            grid=(sp,),
            in_specs=[spec(a) for a in (row_keep, row_got, col_keep, col_got)],
            out_specs=[spec(out)] * 4,
        ),
        out_shape=[out] * 4,
        cost_estimate=COVER,
        name="first_halves",
    )(at, row_keep, row_got, col_keep, col_got)


def second_halves_kernel(at_ref, *refs):
    for side in range(2):
        mine = at_ref[1 - side]
        keep, got = refs[2 * side : 2 * side + 2]
        for s in range(keep.shape[0]):
            refs[4 + 2 * side][s] = add(keep[s, 1 - mine], got[s, 1 - mine])
            refs[5 + 2 * side][s] = add(keep[s, mine], got[s, mine])


def second_halves(at, *arrays):
    sp, rows, columns = arrays[0].shape
    out = jax.ShapeDtypeStruct((sp, rows // 2, columns), bf16)
    return pl.pallas_call(
        second_halves_kernel,
        in_specs=[SMEM] + [VMEM] * 4,
        out_specs=[VMEM] * 4,
        out_shape=[out] * 4,
        cost_estimate=COVER,
        name="second_halves",
    )(at, *[a.reshape(sp, 2, rows // 2, columns) for a in arrays])


def near_halves_kernel(at_ref, *refs, terms, sides):
    ins, outs = refs[:-2], refs[-2:]
    mine = lax.rem(at_ref[2], 2)
    for out, bit in zip(outs, (1 - mine, mine)):
        for s in range(out.shape[0]):
            at = 0
            for side in range(sides):
                total = None
                for ref in ins[side * terms : (side + 1) * terms]:
                    value = ref[2 * s + bit].astype(f32)
                    total = value if total is None else total + value
                out[s, :, at : at + total.shape[1]] = total.astype(bf16)
                at += total.shape[1]


def near_halves(at, sides):
    terms = len(sides[0])
    flat = [a for side in sides for a in side]
    sp, rows, _ = flat[0].shape
    width = sum(side[0].shape[2] for side in sides)
    out = jax.ShapeDtypeStruct((sp // 2, rows, width), bf16)
    return pl.pallas_call(
        functools.partial(near_halves_kernel, terms=terms, sides=len(sides)),
        in_specs=[SMEM] + [VMEM] * len(flat),
        out_specs=[VMEM] * 2,
        out_shape=[out] * 2,
        cost_estimate=COVER,
        name="near_halves",
    )(at, *flat)


def far_halves_kernel(at_ref, keep, got, send_ref, keep_ref):
    mine = lax.div(at_ref[2], 2)
    send_ref[...] = add(keep[1 - mine], got[1 - mine])
    keep_ref[...] = add(keep[mine], got[mine])


def far_halves(at, keep, got):
    out = jax.ShapeDtypeStruct(keep.shape[1:], bf16)
    return pl.pallas_call(
        far_halves_kernel,
        in_specs=[SMEM] + [VMEM] * 2,
        out_specs=[VMEM] * 2,
        out_shape=[out] * 2,
        cost_estimate=COVER,
        name="far_halves",
    )(at, keep, got)


def hand_over_kernel(in_ref, out_ref):
    out_ref[...] = in_ref[...].astype(out_ref.dtype)


def widen(value):
    return hand_over(value, f32)


def hand_over(value, dtype=bf16):
    block = pl.BlockSpec((1,) + value.shape[1:], lambda i: (i, 0, 0))
    return pl.pallas_call(
        hand_over_kernel,
        grid=(value.shape[0],),
        in_specs=[block],
        out_specs=block,
        out_shape=jax.ShapeDtypeStruct(value.shape, dtype),
        cost_estimate=COVER,
        name="hand_over",
    )(value)


def own_kernel(keep_ref, got_ref, out_ref):
    out_ref[...] = add(keep_ref[...], got_ref[...])


def own_sum(keep, got):
    return pl.pallas_call(
        own_kernel,
        in_specs=[VMEM] * 2,
        out_specs=VMEM,
        out_shape=jax.ShapeDtypeStruct(keep.shape, bf16),
        cost_estimate=COVER,
        name="own_sum",
    )(keep, got)


def quarters_kernel(at_ref, keep_ref, got_ref, *outs):
    for i, out in enumerate(outs):
        index = 2 * (at_ref[0] ^ (i // 2)) + (at_ref[1] ^ (i % 2))
        for s in range(keep_ref.shape[0]):
            out[s] = add(keep_ref[s, index], got_ref[s, index])


def quarters(at, keep, got):
    sp, rows, width = keep.shape
    out = jax.ShapeDtypeStruct((sp, rows // 4, width), bf16)
    return pl.pallas_call(
        quarters_kernel,
        in_specs=[SMEM] + [VMEM] * 2,
        out_specs=[VMEM] * 4,
        out_shape=[out] * 4,
        cost_estimate=COVER,
        name="quarters",
    )(at, keep.reshape(sp, 4, rows // 4, width), got.reshape(sp, 4, rows // 4, width))


def four_chips_kernel(at_ref, *refs, crossed):
    pieces, out_ref = refs[:4], refs[4]
    columns = out_ref.shape[2] // 2
    for i, piece in enumerate(pieces):
        x, y = at_ref[0] ^ (i // 2), at_ref[1] ^ (i % 2)
        out_ref[2 * x + y, :, :columns] = piece[:, :columns]
        out_ref[2 * y + x if crossed else 2 * x + y, :, columns:] = piece[:, columns:]


def four_chips(at, pieces, crossed):
    rows, width = pieces[0].shape
    return pl.pallas_call(
        functools.partial(four_chips_kernel, crossed=crossed),
        in_specs=[SMEM] + [VMEM] * 4,
        out_specs=VMEM,
        out_shape=jax.ShapeDtypeStruct((4, rows, width), bf16),
        cost_estimate=COVER,
        name="four_chips",
    )(at, *pieces).reshape(4 * rows, width)


def spread(own):
    return [own] + [pair_permute(own, bit) for bit in (SECOND, FIRST, FIRST + SECOND)]


def finish_kernel(core_ref, mine_ref, other_ref, *outs, half, layout):
    first = core_ref[0] == 0
    width = mine_ref.shape[1]
    for out, (_, across, starts) in zip(outs, layout):
        for n, at in enumerate(starts):
            cols = slice(n % across * width, (n % across + 1) * width)
            mine = mine_ref[at : at + half].astype(f32)
            other = other_ref[at : at + half].astype(f32)
            to = n // across * 2 * half
            out[to : to + half, cols] = jnp.where(first, mine, other)
            out[to + half : to + 2 * half, cols] = jnp.where(first, other, mine)


def finish(core, mine, other, half, layout):
    width = mine.shape[1]
    shapes = [(2 * half * down, width * across) for down, across, _ in layout]
    return pl.pallas_call(
        functools.partial(finish_kernel, half=half, layout=layout),
        grid=(1,),
        in_specs=[SMEM] + [VMEM] * 2,
        out_specs=[pl.BlockSpec(s, lambda i: (0, 0)) for s in shapes],
        out_shape=[jax.ShapeDtypeStruct(s, f32) for s in shapes],
        cost_estimate=COVER,
        name="finish",
    )(core, mine, other)


def vector_outputs_kernel(
    early_ref, late_ref, ada_ref, bias_ref, attn_gain_ref, mlp_gain_ref, up_ref, down_ref, *, half
):
    count, width = ada_ref.shape[0], early_ref.shape[1]
    quarter, own = attn_gain_ref.shape[1], bias_ref.size
    for p in range(2):
        ada_ref[:, p * width : (p + 1) * width] = late_ref[p * half : p * half + count, :]
    for p in range(4):
        start = p // 2 * half + p % 2 * count
        ada_ref[:, (2 + p) * width : (3 + p) * width] = early_ref[start : start + count, :]
    row, low = 2 * count, half + count
    rest = own - width
    attn_gain_ref[...] = late_ref[low : low + 1, rest : rest + quarter]
    for lane in range(0, own, LANES):
        i, cols = lane // LANES, slice(lane % width, lane % width + LANES)
        a, b = (row + 1, count) if lane < width else (half + row + 1, low)
        bias_ref[i : i + 1, :] = early_ref[a : a + 1, cols] + late_ref[b : b + 1, cols]
    for lane in range(0, width, LANES):
        i = lane // LANES
        up_ref[i : i + 1, :] = early_ref[row : row + 1, lane : lane + LANES]
    mlp_gain_ref[...] = early_ref[half + row : half + row + 1, :quarter]
    down_ref[...] = early_ref[half + row : half + row + 1, quarter : 2 * quarter]


def vector_outputs(early, late, half, cond, sp):
    width = early.shape[1]
    quarter = width // sp
    one = (1, quarter)
    shapes = [(cond // sp, 6 * width), (6 * width // sp // LANES, LANES), one, one, (width // LANES, LANES), one]
    return pl.pallas_call(
        functools.partial(vector_outputs_kernel, half=half),
        in_specs=[VMEM] * 2,
        out_specs=[VMEM] * 6,
        out_shape=[jax.ShapeDtypeStruct(s, f32) for s in shapes],
        cost_estimate=COVER,
        name="vector_outputs",
    )(early, late)


def sum_over_rest(total):
    bit = 2 * SECOND
    while bit < lax.axis_size("dp"):
        total = add(total, pair_permute(total, bit))
        bit *= 2
    return total


def double(rows, bit, axis):
    return jnp.concatenate([rows, pair_permute(rows, bit, axis)], axis=0)


def bits(axis):
    n, bit = lax.axis_size(axis), 1
    while bit < n:
        yield bit
        bit *= 2


def body(
    hidden_in,
    time_embed,
    ada_weight,
    ada_bias,
    attn_gain,
    query_key_value_matrix,
    attention_output_matrix,
    mlp_gain,
    up_projection_matrix,
    up_bias,
    down_projection_matrix,
    down_bias,
    out_cotangent,
):
    sequences, local_len, width = hidden_in.shape
    sp, me = lax.axis_size("sp"), lax.axis_index("sp")
    assert sequences == sp
    def exchange(values):
        values = values.reshape(sp, local_len, width)
        return lax.all_to_all(values, "sp", split_axis=0, concat_axis=0, tiled=True)

    x = exchange(hidden_in).reshape(-1, width)
    cot = exchange(after(out_cotangent, x)).reshape(-1, width)
    here = lax.axis_index("dp")
    core = bit_of(here, CORE).reshape(1)
    at = jnp.stack([bit_of(here, FIRST), bit_of(here, SECOND), me])

    timing = lax.dynamic_slice_in_dim(time_embed, me, 1, 0)
    modulation = dot_nn(timing, ada_weight) + ada_bias.astype(f32)[None]
    shift_attn, scale_attn, gate_attn, shift_mlp, scale_mlp, gate_mlp = jnp.split(
        modulation, 6, axis=-1
    )
    gain_attn = attn_gain.astype(f32)[None]
    gain_mlp = mlp_gain.astype(f32)[None]
    zero = jnp.zeros_like(shift_attn)
    attn_mods = jnp.concatenate(
        [gain_attn * (1.0 + scale_attn), shift_attn] + [zero] * 6, axis=0
    )
    mlp_mods = jnp.concatenate(
        [gate_attn, gain_mlp * (1.0 + scale_mlp), shift_mlp, gate_mlp, down_bias.astype(f32)[None]]
        + [zero] * 3,
        axis=0,
    )
    late_mods = jnp.concatenate([attn_mods[:2], gain_attn, 1.0 + scale_attn] + [zero] * 4, axis=0)
    mlp_grad_mods = jnp.concatenate([gain_mlp, 1.0 + scale_mlp] + [zero] * 6, axis=0)
    column = timing.astype(f32).reshape(timing.shape[1], 1)
    attn_mods, mlp_mods, late_mods, mlp_grad_mods, column, at, core = lax.optimization_barrier(
        (attn_mods, mlp_mods, late_mods, mlp_grad_mods, column, at, core)
    )
    lane = lax.broadcasted_iota(jnp.int32, (1, LANES), 1)
    frequency = 10000.0 ** (-((lane % HALF).astype(f32) * 2.0 / HEAD_DIM))
    row = lax.broadcasted_iota(jnp.int32, (sp * local_len, 1), 0)
    angles = row.astype(f32) * frequency
    cos, sin = jnp.cos(angles), jnp.sin(angles)

    xm_attn, q, k, v = project_qkv(x, attn_mods, query_key_value_matrix, cos, sin)
    mixed, lse = attention_forward(q, k, v)
    both_in, act, gd, both_grad, gm, gmix, sums, up_sum, out = feed_forward(
        x,
        mixed,
        cot,
        mlp_mods,
        up_bias.astype(f32)[None],
        attention_output_matrix,
        up_projection_matrix,
        down_projection_matrix,
        local_len,
    )
    ff = up_bias.shape[0]
    assert ff == sp * width
    n_up = ff // width
    half = width // sp // 2
    quarter = width // sp
    cond = timing.shape[1]
    output = exchange(out)
    col_send, col_keep, early_parts = column_grad(
        core, sums, up_sum, mlp_grad_mods, column, both_in, both_grad, sp, n_up
    )
    col_got = pair_permute(col_send, CORE)
    row_send, row_keep = row_grad(core, *after((act, gd), col_keep), sp)
    row_got = pair_permute(row_send, CORE)

    pairs = width // LANES

    def backward(start, stop, into=None):
        return attention_backward(
            q, k, v, gmix, mixed, lse, cos, sin, start, stop - start, into
        )

    left_send, left, right_send, right = first_halves(at, row_keep, row_got, col_keep, col_got)
    left_got, right_got = pair_permute(left_send, FIRST), pair_permute(right_send, SECOND)
    gmix = after(gmix, left, right)
    grads = backward(0, pairs)
    left_got, right_got, output = after((left_got, right_got, output), grads)
    left_send, left, right_send, right = second_halves(at, left, left_got, right, right_got)
    left_got, right_got = pair_permute(left_send, SECOND), pair_permute(right_send, FIRST)
    grads = after(grads, left, right, output)

    time_row, hg, late_send, late_keep = late_grads(
        core, x, grads, gm, late_mods, query_key_value_matrix, xm_attn, ada_weight, column, early_parts,
        sp, local_len,
    )
    hidden_grad = exchange(hg)
    late_got = pair_permute(late_send, CORE)
    left_got, right_got = after((left_got, right_got), late_keep)
    if lax.axis_size("dp") > 2 * SECOND:
        left, right = sum_over_rest(add(left, left_got)), sum_over_rest(add(right, right_got))
        sides = [(left,), (right,)]
    else:
        sides = [(left, left_got), (right, right_got)]
    near_send, near = near_halves(at, sides)
    near_got = pair_permute(near_send, 1, "sp")
    late_got = after(late_got, near)
    own_quarter, *other_quarters = quarters(at, late_keep, late_got)
    quarter_parts = [own_quarter] + [
        pair_permute(p, bit)
        for p, bit in zip(other_quarters, (SECOND, FIRST, FIRST + SECOND))
    ]
    output = hand_over(after(output, own_quarter))
    near_got, hidden_grad, quarter_parts = after((near_got, hidden_grad, quarter_parts), output)
    near_got = after(near_got, quarter_parts)
    far_send, far = far_halves(at, near, after(near_got, hidden_grad))
    far_got = pair_permute(far_send, 2, "sp")
    quarter_parts = after(quarter_parts, far)
    if lax.axis_size("dp") > 2 * SECOND:
        total = sum(p.astype(f32) for p in quarter_parts).astype(bf16)
        quarter_parts = [sum_over_rest(total)]
    late_near_send, late_near = near_halves(at, [quarter_parts])
    late_near_got = pair_permute(late_near_send, 1, "sp")
    late_far_send, late_far = far_halves(at, late_near, late_near_got)
    late_far_got = pair_permute(late_far_send, 2, "sp")
    early_own = own_sum(far, after(far_got, late_far))
    early_four = spread(early_own)
    late_own = own_sum(late_far, after(late_far_got, early_own))
    hidden_grad = after(hidden_grad, late_own).astype(f32)
    time_rows = after(time_row, late_own)
    for bit in bits("sp"):
        time_rows = double(time_rows, bit, "sp")
    time_grad = jnp.concatenate([pick(time_rows, me ^ s)[None] for s in range(sp)], axis=0)
    time_grad = time_grad.astype(f32)
    early_half = four_chips(at, after(early_four, late_own, time_rows, hidden_grad), True)
    early_other = pair_permute(early_half, CORE)
    late_four = spread(after(late_own, early_half))
    n_row, n_col = row_keep.shape[1] // 2, col_keep.shape[1] // 2
    row_starts = [x * (n_row + n_col) + i for x in range(2) for i in range(0, n_row, half)]
    col_starts = [x * (n_row + n_col) + n_row + i for x in range(2) for i in range(0, n_col, half)]
    down_grad, up_grad, proj_grad, early_vectors = finish(
        core,
        early_half,
        after(early_other, late_four[0]),
        half,
        (
            (sp, 1, row_starts),
            (1, n_up, col_starts[:n_up]),
            (1, 1, col_starts[n_up : n_up + 1]),
            (1, 1, col_starts[n_up + 1 :]),
        ),
    )
    late_half = four_chips(at, after(late_four, down_grad), False)
    late_other = pair_permute(late_half, CORE)
    qkv_grad, late_vectors = finish(
        core, late_half, late_other, half, ((1, 3, [0, half, 2 * half]), (1, 1, [3 * half]))
    )
    ada_weight_grad, *small = vector_outputs(early_vectors, late_vectors, half, cond, sp)
    ada_bias_grad, attn_gain_grad, mlp_gain_grad, up_bias_grad, down_bias_grad = (
        v.reshape(-1) for v in small
    )
    return (
        output,
        hidden_grad,
        time_grad,
        ada_weight_grad,
        ada_bias_grad,
        attn_gain_grad,
        qkv_grad,
        proj_grad,
        mlp_gain_grad,
        up_grad,
        up_bias_grad,
        down_grad,
        down_bias_grad,
    )


def solution(mesh):
    return jax.shard_map(
        body,
        mesh=mesh,
        in_specs=(P("dp", "sp", None), P("dp", None)) + (P(),) * 10 + (P("dp", "sp", None),),
        out_specs=(
            P("dp", "sp", None),
            P("dp", "sp", None),
            P("dp", None),
            P("sp", None),
            P("sp"),
            P("sp"),
            P("sp", None),
            P("sp", None),
            P("sp"),
            P("sp", None),
            P("sp"),
            P("sp", None),
            P("sp"),
        ),
        check_vma=False,
    )
```

```python
import functools

import jax
import jax.numpy as jnp
from jax import lax
from jax.experimental import pallas as pl
from jax.experimental.pallas import tpu as pltpu
from jax.sharding import PartitionSpec as P

HEAD_DIM = 64
VMEM = pl.BlockSpec(memory_space=pltpu.VMEM)
SMEM = pl.BlockSpec(memory_space=pltpu.SMEM)
HALF = HEAD_DIM // 2
LANES = 128
EPSILON = 1e-05
LOG2E = 1.4426950408889634
SCALE = HEAD_DIM ** (-0.5)
f32 = jnp.float32
COVER = pl.CostEstimate(flops=40_000_000_000, bytes_accessed=100_000_000, transcendentals=0)
bf16 = jnp.bfloat16


def dot_nn(a, b):
    return lax.dot_general(a, b, (((1,), (0,)), ((), ())), preferred_element_type=f32)


def dot_nt(a, b):
    return lax.dot_general(a, b, (((1,), (1,)), ((), ())), preferred_element_type=f32)


def dot_tn(a, b):
    return lax.dot_general(a, b, (((0,), (0,)), ((), ())), preferred_element_type=f32)


def column_sum(values):
    return jnp.sum(values, axis=0, keepdims=True)


def norm_forward(values):
    center = values - jnp.mean(values, axis=-1, keepdims=True)
    inverse = lax.rsqrt(jnp.mean(center * center, axis=-1, keepdims=True) + EPSILON)
    return center * inverse, inverse


def norm_backward(grad, normed, inverse):
    first = jnp.mean(grad, axis=-1, keepdims=True)
    second = jnp.mean(grad * normed, axis=-1, keepdims=True)
    return inverse * (grad - first - normed * second)


def swap_halves(values):
    lane = lax.broadcasted_iota(jnp.int32, (1, LANES), 1)
    lower = (lane & (HEAD_DIM - 1)) < HALF
    up = pltpu.roll(values, LANES - HALF, 1)
    down = pltpu.roll(values, HALF, 1)
    return lower, up, down


def rotary(values, cos, sin):
    lower, up, down = swap_halves(values)
    return values * cos + jnp.where(lower, -up, down) * sin


def unrotary(values, cos, sin):
    lower, up, down = swap_halves(values * sin)
    return values * cos + jnp.where(lower, up, -down)


def qkv_kernel(x_ref, mod_ref, w_ref, cos_ref, sin_ref, xm_ref, q_ref, k_ref, v_ref):
    width = x_ref.shape[1]
    normed, _ = norm_forward(x_ref[...].astype(f32))
    xm = (normed * mod_ref[0:1, :] + mod_ref[1:2, :]).astype(bf16)
    xm_ref[...] = xm
    cos, sin = cos_ref[...], sin_ref[...]
    for part, ref in enumerate((q_ref, k_ref, v_ref)):
        whole = dot_nn(xm, w_ref[:, part * width : (part + 1) * width]).astype(bf16)
        if part == 2:
            ref[...] = whole
            continue
        for lane in range(0, width, LANES):
            piece = whole[:, lane : lane + LANES].astype(f32)
            ref[:, lane : lane + LANES] = rotary(piece, cos, sin).astype(bf16)


def project_qkv(x, mods, weight, cos, sin, rows=256):
    length, width = x.shape
    block = pl.BlockSpec((rows, width), lambda i: (i, 0))
    table = pl.BlockSpec((rows, LANES), lambda i: (i, 0))
    shape = jax.ShapeDtypeStruct((length, width), bf16)
    return pl.pallas_call(
        qkv_kernel,
        grid=(length // rows,),
        in_specs=[
            block,
            VMEM,
            VMEM,
            table,
            table,
        ],
        out_specs=[block] * 4,
        out_shape=[shape] * 4,
        cost_estimate=COVER,
        name="project_qkv",
    )(x, mods, weight, cos, sin)


def attention_forward_kernel(q_ref, k_ref, v_ref, o_ref, lse_ref, *, chunk, ahead):
    k, v = k_ref[...], v_ref[...]
    first = lax.broadcasted_iota(jnp.int32, (1, LANES), 1) < HEAD_DIM
    c = LOG2E * SCALE
    masks = (first, ~first)
    keys = [jnp.where(m, k, jnp.zeros_like(k)) for m in masks]
    values = [jnp.where(m, v, jnp.ones_like(v)) for m in masks]
    items = [(h, start) for start in range(0, q_ref.shape[0], chunk) for h in range(2)]

    def scores(h, start):
        return dot_nt(keys[h], q_ref[start : start + chunk, :])

    waiting = [scores(*item) for item in items[:ahead]]
    outs = {}
    for i, (h, start) in enumerate(items):
        st = waiting.pop(0)
        if i + ahead < len(items):
            waiting.append(scores(*items[i + ahead]))
        rows = slice(start, start + chunk)
        top = jnp.max(st, axis=0, keepdims=True) * c
        p = jnp.exp2(st * c - top).astype(bf16)
        ot = dot_tn(values[h], p)
        own, ones = (ot[:HEAD_DIM], ot[HEAD_DIM:]) if h == 0 else (ot[HEAD_DIM:], ot[:HEAD_DIM])
        total = ones[0:1]
        outs[h] = own * (1.0 / total)
        lse_ref[0, h : h + 1, rows] = top + jnp.log2(total)
        if h == 1:
            o_ref[rows, :] = jnp.concatenate([outs[0], outs[1]], axis=0).T.astype(bf16)


def attention_forward(q, k, v):
    length, width = q.shape
    pairs = width // LANES
    block = pl.BlockSpec((length, LANES), lambda i: (0, i))
    return pl.pallas_call(
        functools.partial(attention_forward_kernel, chunk=length // 2, ahead=2),
        grid=(pairs,),
        in_specs=[block] * 3,
        out_specs=[block, pl.BlockSpec((1, 2, length), lambda i: (i, 0, 0))],
        out_shape=[
            jax.ShapeDtypeStruct((length, width), bf16),
            jax.ShapeDtypeStruct((pairs, 2, length), f32),
        ],
        cost_estimate=COVER,
        name="attention_forward",
    )(q, k, v)


def attention_backward_kernel(
    q_ref, k_ref, v_ref, do_ref, o_ref, lse_ref, cos_ref, sin_ref, x_ref, gm_ref, mod_ref, w_ref,
    g_ref, hg_ref, sum_ref, held_ref, *, pairs,
):
    step = pl.program_id(0)
    width = x_ref.shape[1]

    @pl.when(step < pairs)
    def _():
        first = lax.broadcasted_iota(jnp.int32, (1, LANES), 1) < HEAD_DIM
        upper = lax.broadcasted_iota(jnp.int32, (LANES, 1), 0) < HEAD_DIM
        c = LOG2E * SCALE
        q, k, v, do = q_ref[...], k_ref[...], v_ref[...], do_ref[...]
        prod = (do.astype(f32) * o_ref[...].astype(f32)).T
        kt = k.T
        zero = jnp.zeros_like(k)
        dq = dk = dv = None
        for h in range(2):
            mine = first if h == 0 else ~first
            row = column_sum(prod[h * HEAD_DIM : (h + 1) * HEAD_DIM])
            st = dot_nt(jnp.where(mine, k, zero), q)
            p = jnp.exp2(st * c - lse_ref[0, h : h + 1, :])
            dp = dot_nt(jnp.where(mine, v, zero), do)
            ds = (p * (dp - row)).astype(bf16)
            dvh = dot_nn(p.astype(bf16), jnp.where(mine, do, zero))
            dkh = dot_nn(ds, jnp.where(mine, q, zero))
            dqh = dot_nn(jnp.where(upper if h == 0 else ~upper, kt, jnp.zeros_like(kt)), ds)
            dq, dk, dv = (dqh, dkh, dvh) if h == 0 else (dq + dqh, dk + dkh, dv + dvh)
        cos, sin = cos_ref[...], sin_ref[...]
        lanes = pl.ds(pl.multiple_of(step * LANES, LANES), LANES)
        for part, value in enumerate(
            (unrotary(dq.T * SCALE, cos, sin), unrotary(dk * SCALE, cos, sin), dv)
        ):
            value = value.astype(bf16)
            g_ref[part] = value
            held_ref[part, :, lanes] = value

    @pl.when(step >= pairs)
    def _():
        rows = x_ref.shape[0]
        tile = pl.ds(pl.multiple_of((step - pairs) * rows, rows), rows)
        normed, inverse = norm_forward(x_ref[...].astype(f32))
        grad = None
        for part in range(3):
            g = dot_nt(held_ref[part, tile, :], w_ref[:, part * width : (part + 1) * width])
            grad = g if grad is None else grad + g
        hg = gm_ref[...] + norm_backward(grad * mod_ref[0:1, :], normed, inverse)
        hg_ref[...] = hg.astype(bf16)
        sums = jnp.concatenate(
            [column_sum(grad), column_sum(grad * normed), jnp.zeros((6, width), f32)], axis=0
        )

        @pl.when(step == pairs)
        def _():
            sum_ref[...] = sums

        @pl.when(step > pairs)
        def _():
            sum_ref[...] += sums


def attention_backward(q, k, v, do, o, lse, cos, sin, x, gm, mods, weight, rows):
    length, width = q.shape
    pairs = width // LANES

    def pair(i):
        return jnp.minimum(i, pairs - 1)

    block = pl.BlockSpec((length, LANES), lambda i: (0, pair(i)))
    table = pl.BlockSpec((length, LANES), lambda i: (0, 0))
    tile = pl.BlockSpec((rows, width), lambda i: (jnp.maximum(i - pairs, 0), 0))
    return pl.pallas_call(
        functools.partial(attention_backward_kernel, pairs=pairs),
        grid=(pairs + length // rows,),
        in_specs=[block] * 5
        + [pl.BlockSpec((1, 2, length), lambda i: (pair(i), 0, 0)), table, table, tile, tile, VMEM, VMEM],
        out_specs=[
            pl.BlockSpec((3, length, LANES), lambda i: (0, 0, pair(i))),
            tile,
            pl.BlockSpec((8, width), lambda i: (0, 0)),
        ],
        out_shape=[
            jax.ShapeDtypeStruct((3, length, width), bf16),
            jax.ShapeDtypeStruct((length, width), bf16),
            jax.ShapeDtypeStruct((8, width), f32),
        ],
        scratch_shapes=[pltpu.VMEM((3, length, width), bf16)],
        cost_estimate=COVER,
        name="attention_backward",
    )(q, k, v, do, o, lse, cos, sin, x, gm, mods, weight)


def mlp_kernel(
    x_ref, mixed_ref, cot_ref, mod_ref, bias_ref, wo_ref, wu_ref, wd_ref,
    xm_ref, act_ref, gd_ref, gp_ref, gm_ref, gmix_ref, sum_ref, up_sum_ref, out_ref,
):
    chunk, ff = wu_ref.shape
    gate_attn, scaled, shift = mod_ref[0:1, :], mod_ref[1:2, :], mod_ref[2:3, :]
    gate_mlp, down_bias = mod_ref[3:4, :], mod_ref[4:5, :]
    cot = cot_ref[...].astype(f32)
    projected = dot_nn(mixed_ref[...], wo_ref[...])
    middle = x_ref[...].astype(f32) + gate_attn * projected
    normed, inverse = norm_forward(middle)
    xm = (normed * scaled + shift).astype(bf16)
    xm_ref[0] = xm
    xm_ref[1] = mixed_ref[...]
    gd = (gate_mlp * cot).astype(bf16)
    gd_ref[...] = gd
    down = grad_mod = None
    c0 = 0.7978845608028654
    c1 = c0 * 0.044715
    up_sums = []
    for at in range(0, ff, chunk):
        cols = slice(at, at + chunk)
        pre = dot_nn(xm, wu_ref[:, cols]) + bias_ref[:, cols]
        square = pre * pre
        t = jnp.tanh(pre * (c0 + c1 * square))
        half = 0.5 + 0.5 * t
        wide_act = pre * half
        act = wide_act.astype(bf16)
        act_ref[:, cols] = act
        slope = half + wide_act * (1.0 - half) * (2.0 * c0 + (6.0 * c1) * square)
        wide_gp = slope * dot_nt(gd, wd_ref[cols, :])
        gp = wide_gp.astype(bf16)
        gp_ref[at // chunk] = gp
        up_sums.append(column_sum(wide_gp))
        d = dot_nn(act, wd_ref[cols, :])
        g = dot_nt(gp, wu_ref[:, cols])
        down, grad_mod = (d, g) if down is None else (down + d, grad_mod + g)
    down = down + down_bias
    out_ref[...] = (middle + gate_mlp * down).astype(bf16)
    gm = cot + norm_backward(grad_mod * scaled, normed, inverse)
    gm_ref[...] = gm
    gpj = (gate_attn * gm).astype(bf16)
    gp_ref[ff // chunk] = gpj
    gmix_ref[...] = dot_nt(gpj, wo_ref[...]).astype(bf16)
    sums = jnp.concatenate(
        [
            column_sum(cot * down),
            column_sum(gd.astype(f32)),
            column_sum(grad_mod),
            column_sum(grad_mod * normed),
            column_sum(gm * projected),
            jnp.zeros((3, cot.shape[1]), f32),
        ],
        axis=0,
    )
    up_sum = jnp.concatenate(up_sums, axis=1)

    @pl.when(pl.program_id(0) == 0)
    def _():
        sum_ref[...] = sums
        up_sum_ref[...] = up_sum

    @pl.when(pl.program_id(0) > 0)
    def _():
        sum_ref[...] += sums
        up_sum_ref[...] += up_sum


def feed_forward(x, mixed, cot, mods, up_bias, wo, wu, wd, rows):
    length, width = x.shape
    ff = wu.shape[1]
    block = pl.BlockSpec((rows, width), lambda i: (i, 0))
    wide = pl.BlockSpec((rows, ff), lambda i: (i, 0))

    narrow = jax.ShapeDtypeStruct((length, width), bf16)
    broad = jax.ShapeDtypeStruct((length, ff), bf16)
    return pl.pallas_call(
        mlp_kernel,
        grid=(length // rows,),
        in_specs=[block, block, block] + [VMEM] * 5,
        out_specs=[
            pl.BlockSpec((2, rows, width), lambda i: (0, i, 0)),
            wide,
            block,
            pl.BlockSpec((ff // width + 1, rows, width), lambda i: (0, i, 0)),
            block,
            block,
            pl.BlockSpec((8, width), lambda i: (0, 0)),
            pl.BlockSpec((1, ff), lambda i: (0, 0)),
        ]
        + [block],
        out_shape=[
            jax.ShapeDtypeStruct((2, length, width), bf16), broad, narrow,
            jax.ShapeDtypeStruct((ff // width + 1, length, width), bf16),
            jax.ShapeDtypeStruct((length, width), f32), narrow,
            jax.ShapeDtypeStruct((8, width), f32), jax.ShapeDtypeStruct((1, ff), f32),
        ]
        + [narrow],
        cost_estimate=COVER,
        name="feed_forward",
    )(x, mixed, cot, mods, up_bias, wo, wu, wd)


def late_grads_kernel(
    core_ref, sum_ref, mod_ref, ada_ref, timing_ref, early_ref, xm_ref, block_ref,
    time_ref, send_ref, keep_ref, *, parts,
):
    step = pl.program_id(0)
    width = block_ref.shape[2]

    @pl.when(step < parts)
    def _():
        product = dot_tn(xm_ref[...], block_ref[0])
        half = send_ref.shape[1]
        for i, (send, keep) in enumerate(split_halves(product, half, core_ref[0] == 0)):
            send_ref[i] = send
            keep_ref[i] = keep

    @pl.when(step == parts)
    def _():
        sp, half, _ = send_ref.shape
        shift, scaled = sum_ref[0:1, :], sum_ref[1:2, :]
        scale = scaled * mod_ref[0:1, :]
        gain = scaled * mod_ref[1:2, :]
        row = jnp.concatenate([shift, scale] + [early_ref[i : i + 1, :] for i in range(4)], axis=1)
        high = row.astype(bf16)
        low = (row - high.astype(f32)).astype(bf16)
        time_ref[...] = (dot_nt(high, ada_ref[...]) + dot_nt(low, ada_ref[...])).astype(bf16)
        bias = jnp.concatenate([shift, scale, jnp.zeros((1, 4 * width), f32)], axis=1)
        count, own, quarter = timing_ref.shape[0] // sp, 6 * width // sp, width // sp
        for ref, first in ((send_ref, core_ref[0] == 1), (keep_ref, core_ref[0] == 0)):
            part = jnp.where(first, shift, scale)
            for i in range(sp):
                ref[i, :count] = (timing_ref[i * count : (i + 1) * count, :] * part).astype(bf16)
                mine = bias[:, i * own : (i + 1) * own]
                rest = jnp.concatenate(
                    [
                        mine[:, width:],
                        gain[:, i * quarter : (i + 1) * quarter],
                        jnp.zeros((1, 2 * width - own - quarter), f32),
                    ],
                    axis=1,
                )
                sums = jnp.concatenate(
                    [jnp.where(first, mine[:, :width], rest), jnp.zeros((half - count - 1, width), f32)], axis=0
                )
                ref[i, count:] = sums.astype(bf16)


def late_grads(core, grads, xm, sums, mods, ada, timing, early, sp):
    n, length, width = grads.shape
    half = width // sp // 2
    out = pl.BlockSpec((sp, half, width), lambda i, c: (0, i, 0))
    shape = jax.ShapeDtypeStruct((sp, (n + 1) * half, width), bf16)
    cond = timing.shape[0]
    return pl.pallas_call(
        functools.partial(late_grads_kernel, parts=n),
        grid_spec=pltpu.PrefetchScalarGridSpec(
            num_scalar_prefetch=1,
            grid=(n + 1,),
            in_specs=[VMEM] * 5
            + [
                pl.BlockSpec((length, width), lambda i, c: (0, 0)),
                pl.BlockSpec((1, length, width), lambda i, c: (jnp.minimum(i, n - 1), 0, 0)),
            ],
            out_specs=[pl.BlockSpec((1, cond), lambda i, c: (0, 0)), out, out],
        ),
        out_shape=[jax.ShapeDtypeStruct((1, cond), bf16), shape, shape],
        cost_estimate=COVER,
        name="late_grads",
    )(core, sums, mods, ada, timing, early, xm, grads)


def split_halves(product, half, this_core):
    pieces = []
    for at in range(0, product.shape[0], 2 * half):
        low = product[at : at + half].astype(bf16)
        high = product[at + half : at + 2 * half].astype(bf16)
        pieces.append((jnp.where(this_core, high, low), jnp.where(this_core, low, high)))
    return pieces


def row_grad_kernel(core_ref, a_ref, b_ref, send_ref, keep_ref, *, half):
    product = dot_tn(a_ref[...], b_ref[...])
    for i, (send, keep) in enumerate(split_halves(product, half, core_ref[0] == 0)):
        send_ref[0, i * half : (i + 1) * half] = send
        keep_ref[0, i * half : (i + 1) * half] = keep


def row_grad(core, a, b, sp):
    length, width = b.shape
    out = jax.ShapeDtypeStruct((sp, width // 2, width), bf16)
    block = pl.BlockSpec((1, width // 2, width), lambda j, c: (j, 0, 0))
    return pl.pallas_call(
        functools.partial(row_grad_kernel, half=width // sp // 2),
        grid_spec=pltpu.PrefetchScalarGridSpec(
            num_scalar_prefetch=1,
            grid=(sp,),
            in_specs=[
                pl.BlockSpec((length, width), lambda j, c: (0, j)),
                pl.BlockSpec((length, width), lambda j, c: (0, 0)),
            ],
            out_specs=[block, block],
        ),
        out_shape=[out, out],
        cost_estimate=COVER,
        name="row_grad",
    )(core, a, b)


def column_grad_kernel(
    core_ref, sum_ref, up_sum_ref, mod_ref, timing_ref, a_ref, b_ref, send_ref, keep_ref, parts_ref, *, blocks
):
    step = pl.program_id(0)
    sp, half, width = send_ref.shape

    @pl.when(step < blocks)
    def _():
        product = dot_tn(a_ref[0], b_ref[0])
        for i, (send, keep) in enumerate(split_halves(product, half, core_ref[0] == 0)):
            send_ref[i] = send
            keep_ref[i] = keep

    @pl.when(step == blocks)
    def _():
        scaled = sum_ref[3:4, :]
        parts = [sum_ref[4:5, :], sum_ref[2:3, :], scaled * mod_ref[0:1, :], sum_ref[0:1, :]]
        for i, part in enumerate(parts):
            parts_ref[i : i + 1, :] = part
        gain = scaled * mod_ref[1:2, :]
        bias = jnp.concatenate([jnp.zeros((1, 2 * width), f32)] + parts, axis=1)
        count, own, quarter = timing_ref.shape[0] // sp, 6 * width // sp, width // sp
        for ref, first in ((send_ref, core_ref[0] == 1), (keep_ref, core_ref[0] == 0)):
            for i in range(sp):
                column = timing_ref[i * count : (i + 1) * count, :]
                for p in range(2):
                    part = jnp.where(first, parts[p], parts[p + 2])
                    ref[i, p * count : (p + 1) * count] = (column * part).astype(bf16)
                shard = slice(i * quarter, (i + 1) * quarter)
                mine = bias[:, i * own : (i + 1) * own]
                gains = jnp.concatenate(
                    [gain[:, shard], sum_ref[1:2, shard], jnp.zeros((1, width - 2 * quarter), f32)], axis=1
                )
                rest = jnp.concatenate([mine[:, width:], jnp.zeros((1, 2 * width - own), f32)], axis=1)
                sums = jnp.concatenate(
                    [
                        jnp.where(first, up_sum_ref[:, i * width : (i + 1) * width], gains),
                        jnp.where(first, mine[:, :width], rest),
                        jnp.zeros((half - 2 * count - 2, width), f32),
                    ],
                    axis=0,
                )
                ref[i, 2 * count :] = sums.astype(bf16)


def column_grad(core, sums, up_sum, mods, timing, a, b, sp, second):
    _, length, width = a.shape
    n = b.shape[0]
    half = width // sp // 2
    out = jax.ShapeDtypeStruct((sp, (n + 1) * half, width), bf16)
    block = pl.BlockSpec((sp, half, width), lambda j, c: (0, j, 0))
    return pl.pallas_call(
        functools.partial(column_grad_kernel, blocks=n),
        grid_spec=pltpu.PrefetchScalarGridSpec(
            num_scalar_prefetch=1,
            grid=(n + 1,),
            in_specs=[VMEM] * 4
            + [
                pl.BlockSpec((1, length, width), lambda j, c: (jnp.minimum(j, n - 1) // second, 0, 0)),
                pl.BlockSpec((1, length, width), lambda j, c: (jnp.minimum(j, n - 1), 0, 0)),
            ],
            out_specs=[block, block, pl.BlockSpec((4, width), lambda j, c: (0, 0))],
        ),
        out_shape=[out, out, jax.ShapeDtypeStruct((4, width), f32)],
        cost_estimate=COVER,
        name="column_grad",
    )(core, sums, up_sum, mods, timing, a, b)


def shift_permute(value, axis, by):
    n = lax.axis_size(axis)
    return lax.ppermute(value, axis, [(i, (i + by) % n) for i in range(n)])


def pair_permute(value, bit, axis="dp"):
    n = lax.axis_size(axis)
    return lax.ppermute(value, axis, [(i, i ^ bit) for i in range(n)])


def pick(values, index, axis=0):
    return lax.dynamic_index_in_dim(values, index, axis, keepdims=False)


def after(values, *others):
    return lax.optimization_barrier((values, others))[0]


def bit_of(index, bit):
    return (index // bit) % 2


def add(a, b):
    return (a.astype(f32) + b.astype(f32)).astype(bf16)


CORE, FIRST, SECOND = 1, 2, 4


def first_halves_kernel(at_ref, row_keep, row_got, col_keep, col_got, *outs):
    columns = outs[0].shape[2]
    start = 0
    for keep, got in ((row_keep, row_got), (col_keep, col_got)):
        total = add(keep[0], got[0])
        n = total.shape[0] // 2
        low, high = total[:n], total[n:]
        for side in range(2):
            cols = slice(side * columns, (side + 1) * columns)
            mine = at_ref[side] == 0
            outs[2 * side][0, start : start + n] = jnp.where(mine, high, low)[:, cols]
            outs[2 * side + 1][0, start : start + n] = jnp.where(mine, low, high)[:, cols]
        start += n


def first_halves(at, row_keep, row_got, col_keep, col_got):
    sp, rows, width = row_keep.shape
    cols = col_keep.shape[1]

    def spec(a):
        return pl.BlockSpec((1,) + a.shape[1:], lambda s, t: (s, 0, 0))

    out = jax.ShapeDtypeStruct((sp, (rows + cols) // 2, width // 2), bf16)
    return pl.pallas_call(
        first_halves_kernel,
        grid_spec=pltpu.PrefetchScalarGridSpec(
            num_scalar_prefetch=1,
            grid=(sp,),
            in_specs=[spec(a) for a in (row_keep, row_got, col_keep, col_got)],
            out_specs=[spec(out)] * 4,
        ),
        out_shape=[out] * 4,
        cost_estimate=COVER,
        name="first_halves",
    )(at, row_keep, row_got, col_keep, col_got)


def second_halves_kernel(at_ref, *refs):
    for side in range(2):
        mine = at_ref[1 - side]
        keep, got = refs[2 * side : 2 * side + 2]
        for s in range(keep.shape[0]):
            refs[4 + 2 * side][s] = add(keep[s, 1 - mine], got[s, 1 - mine])
            refs[5 + 2 * side][s] = add(keep[s, mine], got[s, mine])


def second_halves(at, *arrays):
    sp, rows, columns = arrays[0].shape
    out = jax.ShapeDtypeStruct((sp, rows // 2, columns), bf16)
    return pl.pallas_call(
        second_halves_kernel,
        in_specs=[SMEM] + [VMEM] * 4,
        out_specs=[VMEM] * 4,
        out_shape=[out] * 4,
        cost_estimate=COVER,
        name="second_halves",
    )(at, *[a.reshape(sp, 2, rows // 2, columns) for a in arrays])


def near_halves_kernel(at_ref, *refs, terms, sides):
    ins, outs = refs[:-2], refs[-2:]
    mine = lax.rem(at_ref[2], 2)
    for out, bit in zip(outs, (1 - mine, mine)):
        for s in range(out.shape[0]):
            at = 0
            for side in range(sides):
                total = None
                for ref in ins[side * terms : (side + 1) * terms]:
                    value = ref[2 * s + bit].astype(f32)
                    total = value if total is None else total + value
                out[s, :, at : at + total.shape[1]] = total.astype(bf16)
                at += total.shape[1]


def near_halves(at, sides):
    terms = len(sides[0])
    flat = [a for side in sides for a in side]
    sp, rows, _ = flat[0].shape
    width = sum(side[0].shape[2] for side in sides)
    out = jax.ShapeDtypeStruct((sp // 2, rows, width), bf16)
    return pl.pallas_call(
        functools.partial(near_halves_kernel, terms=terms, sides=len(sides)),
        in_specs=[SMEM] + [VMEM] * len(flat),
        out_specs=[VMEM] * 2,
        out_shape=[out] * 2,
        cost_estimate=COVER,
        name="near_halves",
    )(at, *flat)


def far_halves_kernel(at_ref, keep, got, send_ref, keep_ref):
    mine = lax.div(at_ref[2], 2)
    send_ref[...] = add(keep[1 - mine], got[1 - mine])
    keep_ref[...] = add(keep[mine], got[mine])


def far_halves(at, keep, got):
    out = jax.ShapeDtypeStruct(keep.shape[1:], bf16)
    return pl.pallas_call(
        far_halves_kernel,
        in_specs=[SMEM] + [VMEM] * 2,
        out_specs=[VMEM] * 2,
        out_shape=[out] * 2,
        cost_estimate=COVER,
        name="far_halves",
    )(at, keep, got)


def hand_over_kernel(in_ref, out_ref):
    out_ref[...] = in_ref[...].astype(out_ref.dtype)


def widen(value):
    return hand_over(value, f32)


def hand_over(value, dtype=bf16):
    block = pl.BlockSpec((1,) + value.shape[1:], lambda i: (i, 0, 0))
    return pl.pallas_call(
        hand_over_kernel,
        grid=(value.shape[0],),
        in_specs=[block],
        out_specs=block,
        out_shape=jax.ShapeDtypeStruct(value.shape, dtype),
        cost_estimate=COVER,
        name="hand_over",
    )(value)


def own_kernel(keep_ref, got_ref, out_ref):
    out_ref[...] = add(keep_ref[...], got_ref[...])


def own_sum(keep, got):
    return pl.pallas_call(
        own_kernel,
        in_specs=[VMEM] * 2,
        out_specs=VMEM,
        out_shape=jax.ShapeDtypeStruct(keep.shape, bf16),
        cost_estimate=COVER,
        name="own_sum",
    )(keep, got)


def quarters_kernel(at_ref, keep_ref, got_ref, *outs):
    for i, out in enumerate(outs):
        index = 2 * (at_ref[0] ^ (i // 2)) + (at_ref[1] ^ (i % 2))
        for s in range(keep_ref.shape[0]):
            out[s] = add(keep_ref[s, index], got_ref[s, index])


def quarters(at, keep, got):
    sp, rows, width = keep.shape
    out = jax.ShapeDtypeStruct((sp, rows // 4, width), bf16)
    return pl.pallas_call(
        quarters_kernel,
        in_specs=[SMEM] + [VMEM] * 2,
        out_specs=[VMEM] * 4,
        out_shape=[out] * 4,
        cost_estimate=COVER,
        name="quarters",
    )(at, keep.reshape(sp, 4, rows // 4, width), got.reshape(sp, 4, rows // 4, width))


def four_chips_kernel(at_ref, *refs, crossed):
    pieces, out_ref = refs[:4], refs[4]
    columns = out_ref.shape[2] // 2
    for i, piece in enumerate(pieces):
        x, y = at_ref[0] ^ (i // 2), at_ref[1] ^ (i % 2)
        out_ref[2 * x + y, :, :columns] = piece[:, :columns]
        out_ref[2 * y + x if crossed else 2 * x + y, :, columns:] = piece[:, columns:]


def four_chips(at, pieces, crossed):
    rows, width = pieces[0].shape
    return pl.pallas_call(
        functools.partial(four_chips_kernel, crossed=crossed),
        in_specs=[SMEM] + [VMEM] * 4,
        out_specs=VMEM,
        out_shape=jax.ShapeDtypeStruct((4, rows, width), bf16),
        cost_estimate=COVER,
        name="four_chips",
    )(at, *pieces).reshape(4 * rows, width)


def spread(own):
    return [own] + [pair_permute(own, bit) for bit in (SECOND, FIRST, FIRST + SECOND)]


def finish_kernel(core_ref, mine_ref, other_ref, *outs, half, layout):
    first = core_ref[0] == 0
    width = mine_ref.shape[1]
    for out, (_, across, starts) in zip(outs, layout):
        for n, at in enumerate(starts):
            cols = slice(n % across * width, (n % across + 1) * width)
            mine = mine_ref[at : at + half].astype(f32)
            other = other_ref[at : at + half].astype(f32)
            to = n // across * 2 * half
            out[to : to + half, cols] = jnp.where(first, mine, other)
            out[to + half : to + 2 * half, cols] = jnp.where(first, other, mine)


def finish(core, mine, other, half, layout):
    width = mine.shape[1]
    shapes = [(2 * half * down, width * across) for down, across, _ in layout]
    return pl.pallas_call(
        functools.partial(finish_kernel, half=half, layout=layout),
        grid=(1,),
        in_specs=[SMEM] + [VMEM] * 2,
        out_specs=[pl.BlockSpec(s, lambda i: (0, 0)) for s in shapes],
        out_shape=[jax.ShapeDtypeStruct(s, f32) for s in shapes],
        cost_estimate=COVER,
        name="finish",
    )(core, mine, other)


def late_finish_kernel(
    core_ref, mine_ref, other_ref, early_ref, qkv_ref, ada_ref, bias_ref, attn_gain_ref, mlp_gain_ref, up_ref,
    down_ref, *, half,
):
    core_first = core_ref[0] == 0
    width = mine_ref.shape[1]
    for n in range(3):
        cols = slice(n * width, (n + 1) * width)
        mine = mine_ref[n * half : (n + 1) * half].astype(f32)
        other = other_ref[n * half : (n + 1) * half].astype(f32)
        qkv_ref[:half, cols] = jnp.where(core_first, mine, other)
        qkv_ref[half:, cols] = jnp.where(core_first, other, mine)
    mine, other = mine_ref[3 * half :].astype(f32), other_ref[3 * half :].astype(f32)
    late = (jnp.where(core_first, mine, other), jnp.where(core_first, other, mine))
    count = ada_ref.shape[0]
    quarter, own = attn_gain_ref.shape[1], bias_ref.size
    for p in range(2):
        ada_ref[:, p * width : (p + 1) * width] = late[p][:count]
    for p in range(4):
        start = p // 2 * half + p % 2 * count
        ada_ref[:, (2 + p) * width : (3 + p) * width] = early_ref[start : start + count, :]
    row, rest = 2 * count, own - width
    sums = (late[0][count : count + 1], late[1][count : count + 1])
    for lane in range(0, own, LANES):
        i, side = lane // LANES, lane // width
        cols = slice(lane % width, lane % width + LANES)
        at = side * half + row + 1
        bias_ref[i : i + 1, :] = early_ref[at : at + 1, cols] + sums[side][:, cols]
    for lane in range(0, width, LANES):
        i = lane // LANES
        up_ref[i : i + 1, :] = early_ref[row : row + 1, lane : lane + LANES]
    attn_gain_ref[...] = sums[1][:, rest : rest + quarter]
    mlp_gain_ref[...] = early_ref[half + row : half + row + 1, :quarter]
    down_ref[...] = early_ref[half + row : half + row + 1, quarter : 2 * quarter]


def late_finish(core, mine, other, early, half, cond, sp):
    width = early.shape[1]
    one = (1, width // sp)
    shapes = [
        (2 * half, 3 * width), (cond // sp, 6 * width), (6 * width // sp // LANES, LANES),
        one, one, (width // LANES, LANES), one,
    ]
    return pl.pallas_call(
        functools.partial(late_finish_kernel, half=half),
        grid=(1,),
        in_specs=[SMEM] + [VMEM] * 3,
        out_specs=[pl.BlockSpec(s, lambda i: (0, 0)) for s in shapes],
        out_shape=[jax.ShapeDtypeStruct(s, f32) for s in shapes],
        cost_estimate=COVER,
        name="late_finish",
    )(core, mine, other, early)


def sum_over_rest(total):
    bit = 2 * SECOND
    while bit < lax.axis_size("dp"):
        total = add(total, pair_permute(total, bit))
        bit *= 2
    return total


def double(rows, bit, axis):
    return jnp.concatenate([rows, pair_permute(rows, bit, axis)], axis=0)


def bits(axis):
    n, bit = lax.axis_size(axis), 1
    while bit < n:
        yield bit
        bit *= 2


def body(
    hidden_in,
    time_embed,
    ada_weight,
    ada_bias,
    attn_gain,
    query_key_value_matrix,
    attention_output_matrix,
    mlp_gain,
    up_projection_matrix,
    up_bias,
    down_projection_matrix,
    down_bias,
    out_cotangent,
):
    sequences, local_len, width = hidden_in.shape
    sp, me = lax.axis_size("sp"), lax.axis_index("sp")
    assert sequences == sp
    def exchange(values):
        values = values.reshape(sp, local_len, width)
        return lax.all_to_all(values, "sp", split_axis=0, concat_axis=0, tiled=True)

    x = exchange(hidden_in).reshape(-1, width)
    cot = exchange(after(out_cotangent, x)).reshape(-1, width)
    here = lax.axis_index("dp")
    core = bit_of(here, CORE).reshape(1)
    at = jnp.stack([bit_of(here, FIRST), bit_of(here, SECOND), me])

    timing = lax.dynamic_slice_in_dim(time_embed, me, 1, 0)
    modulation = dot_nn(timing, ada_weight) + ada_bias.astype(f32)[None]
    shift_attn, scale_attn, gate_attn, shift_mlp, scale_mlp, gate_mlp = jnp.split(
        modulation, 6, axis=-1
    )
    gain_attn = attn_gain.astype(f32)[None]
    gain_mlp = mlp_gain.astype(f32)[None]
    zero = jnp.zeros_like(shift_attn)
    attn_mods = jnp.concatenate(
        [gain_attn * (1.0 + scale_attn), shift_attn] + [zero] * 6, axis=0
    )
    mlp_mods = jnp.concatenate(
        [gate_attn, gain_mlp * (1.0 + scale_mlp), shift_mlp, gate_mlp, down_bias.astype(f32)[None]]
        + [zero] * 3,
        axis=0,
    )
    late_mods = jnp.concatenate([gain_attn, 1.0 + scale_attn] + [zero] * 6, axis=0)
    mlp_grad_mods = jnp.concatenate([gain_mlp, 1.0 + scale_mlp] + [zero] * 6, axis=0)
    column = timing.astype(f32).reshape(timing.shape[1], 1)
    attn_mods, mlp_mods, late_mods, mlp_grad_mods, column, at, core = lax.optimization_barrier(
        (attn_mods, mlp_mods, late_mods, mlp_grad_mods, column, at, core)
    )
    lane = lax.broadcasted_iota(jnp.int32, (1, LANES), 1)
    frequency = 10000.0 ** (-((lane % HALF).astype(f32) * 2.0 / HEAD_DIM))
    row = lax.broadcasted_iota(jnp.int32, (sp * local_len, 1), 0)
    angles = row.astype(f32) * frequency
    cos, sin = jnp.cos(angles), jnp.sin(angles)

    xm_attn, q, k, v = project_qkv(x, attn_mods, query_key_value_matrix, cos, sin)
    mixed, lse = attention_forward(q, k, v)
    both_in, act, gd, both_grad, gm, gmix, sums, up_sum, out = feed_forward(
        x,
        mixed,
        cot,
        mlp_mods,
        up_bias.astype(f32)[None],
        attention_output_matrix,
        up_projection_matrix,
        down_projection_matrix,
        local_len,
    )
    ff = up_bias.shape[0]
    assert ff == sp * width
    n_up = ff // width
    half = width // sp // 2
    quarter = width // sp
    cond = timing.shape[1]
    output = exchange(out)
    col_send, col_keep, early_parts = column_grad(
        core, sums, up_sum, mlp_grad_mods, column, both_in, both_grad, sp, n_up
    )
    col_got = pair_permute(col_send, CORE)
    row_send, row_keep = row_grad(core, *after((act, gd), col_keep), sp)
    row_got = pair_permute(row_send, CORE)

    left_send, left, right_send, right = first_halves(at, row_keep, row_got, col_keep, col_got)
    left_got, right_got = pair_permute(left_send, FIRST), pair_permute(right_send, SECOND)
    gmix = after(gmix, left, right)
    grads, hg, attn_sums = attention_backward(
        q, k, v, gmix, mixed, lse, cos, sin, x, gm, attn_mods, query_key_value_matrix, local_len
    )
    left_got, right_got, output = after((left_got, right_got, output), grads)
    left_send, left, right_send, right = second_halves(at, left, left_got, right, right_got)
    left_got, right_got = pair_permute(left_send, SECOND), pair_permute(right_send, FIRST)
    grads = after(grads, left, right, output)

    time_row, late_send, late_keep = late_grads(
        core, grads, xm_attn, attn_sums, late_mods, ada_weight, column, early_parts, sp
    )
    hidden_grad = exchange(hg)
    late_got = pair_permute(late_send, CORE)
    left_got, right_got = after((left_got, right_got), late_keep)
    if lax.axis_size("dp") > 2 * SECOND:
        left, right = sum_over_rest(add(left, left_got)), sum_over_rest(add(right, right_got))
        sides = [(left,), (right,)]
    else:
        sides = [(left, left_got), (right, right_got)]
    near_send, near = near_halves(at, sides)
    near_got = pair_permute(near_send, 1, "sp")
    late_got = after(late_got, near)
    own_quarter, *other_quarters = quarters(at, late_keep, late_got)
    quarter_parts = [own_quarter] + [
        pair_permute(p, bit)
        for p, bit in zip(other_quarters, (SECOND, FIRST, FIRST + SECOND))
    ]
    output = hand_over(after(output, own_quarter))
    near_got, hidden_grad = after((near_got, hidden_grad), output)
    near_got = after(near_got, hidden_grad)
    upper = me // 2
    far_send = add(pick(near, 1 - upper), pick(near_got, 1 - upper))
    far = add(pick(near, upper), pick(near_got, upper))
    far_got = pair_permute(far_send, 2, "sp")
    quarter_parts = after(quarter_parts, far, far_send)
    if lax.axis_size("dp") > 2 * SECOND:
        total = sum(p.astype(f32) for p in quarter_parts).astype(bf16)
        quarter_parts = [sum_over_rest(total)]
    late_near_send, late_near = near_halves(at, [quarter_parts])
    late_near_got = pair_permute(late_near_send, 1, "sp")
    early_own = add(far, after(far_got, late_near))
    early_four = spread(early_own)
    late_near_got = after(late_near_got, early_own)
    late_far_send = add(pick(late_near, 1 - upper), pick(late_near_got, 1 - upper))
    late_far = add(pick(late_near, upper), pick(late_near_got, upper))
    late_far_got = pair_permute(late_far_send, 2, "sp")
    late_own = add(late_far, late_far_got)
    hidden_grad = after(hidden_grad, late_own).astype(f32)
    time_rows = after(time_row, late_own)
    for bit in bits("sp"):
        time_rows = double(time_rows, bit, "sp")
    time_grad = jnp.concatenate([pick(time_rows, me ^ s)[None] for s in range(sp)], axis=0)
    time_grad = time_grad.astype(f32)
    early_half = four_chips(at, after(early_four, late_own, time_rows, hidden_grad), True)
    early_other = pair_permute(early_half, CORE)
    late_four = spread(after(late_own, early_half))
    n_row, n_col = row_keep.shape[1] // 2, col_keep.shape[1] // 2
    row_starts = [x * (n_row + n_col) + i for x in range(2) for i in range(0, n_row, half)]
    col_starts = [x * (n_row + n_col) + n_row + i for x in range(2) for i in range(0, n_col, half)]
    down_grad, up_grad, proj_grad, early_vectors = finish(
        core,
        early_half,
        after(early_other, late_four[0]),
        half,
        (
            (sp, 1, row_starts),
            (1, n_up, col_starts[:n_up]),
            (1, 1, col_starts[n_up : n_up + 1]),
            (1, 1, col_starts[n_up + 1 :]),
        ),
    )
    late_half = four_chips(at, after(late_four, down_grad), False)
    late_other = pair_permute(late_half, CORE)
    qkv_grad, ada_weight_grad, *small = late_finish(
        core, late_half, late_other, early_vectors, half, cond, sp
    )
    ada_bias_grad, attn_gain_grad, mlp_gain_grad, up_bias_grad, down_bias_grad = (
        v.reshape(-1) for v in small
    )
    return (
        output,
        hidden_grad,
        time_grad,
        ada_weight_grad,
        ada_bias_grad,
        attn_gain_grad,
        qkv_grad,
        proj_grad,
        mlp_gain_grad,
        up_grad,
        up_bias_grad,
        down_grad,
        down_bias_grad,
    )


def solution(mesh):
    return jax.shard_map(
        body,
        mesh=mesh,
        in_specs=(P("dp", "sp", None), P("dp", None)) + (P(),) * 10 + (P("dp", "sp", None),),
        out_specs=(
            P("dp", "sp", None),
            P("dp", "sp", None),
            P("dp", None),
            P("sp", None),
            P("sp"),
            P("sp"),
            P("sp", None),
            P("sp", None),
            P("sp"),
            P("sp", None),
            P("sp"),
            P("sp", None),
            P("sp"),
        ),
        check_vma=False,
    )
```

```python
import functools

import jax
import jax.numpy as jnp
from jax import lax
from jax.experimental import pallas as pl
from jax.experimental.pallas import tpu as pltpu
from jax.sharding import PartitionSpec as P

HEAD_DIM = 64
MIB = 1 << 20
VMEM = pl.BlockSpec(memory_space=pltpu.VMEM)
SMEM = pl.BlockSpec(memory_space=pltpu.SMEM)
HALF = HEAD_DIM // 2
LANES = 128
EPSILON = 1e-05
LOG2E = 1.4426950408889634
SCALE = HEAD_DIM ** (-0.5)
f32 = jnp.float32
COVER = pl.CostEstimate(flops=40_000_000_000, bytes_accessed=100_000_000, transcendentals=0)
bf16 = jnp.bfloat16


def on_chip(arrays):
    return [pltpu.with_memory_space_constraint(a, pltpu.VMEM) for a in arrays]


def streamed(*arrays):
    return [pltpu.with_memory_space_constraint(a, pltpu.HBM) for a in arrays]


def dot_nn(a, b):
    return lax.dot_general(a, b, (((1,), (0,)), ((), ())), preferred_element_type=f32)


def dot_nt(a, b):
    return lax.dot_general(a, b, (((1,), (1,)), ((), ())), preferred_element_type=f32)


def dot_tn(a, b):
    return lax.dot_general(a, b, (((0,), (0,)), ((), ())), preferred_element_type=f32)


def column_sum(values):
    return jnp.sum(values, axis=0, keepdims=True)


def norm_forward(values):
    center = values - jnp.mean(values, axis=-1, keepdims=True)
    inverse = lax.rsqrt(jnp.mean(center * center, axis=-1, keepdims=True) + EPSILON)
    return center * inverse, inverse


def norm_backward(grad, normed, inverse):
    first = jnp.mean(grad, axis=-1, keepdims=True)
    second = jnp.mean(grad * normed, axis=-1, keepdims=True)
    return inverse * (grad - first - normed * second)


def swap_halves(values):
    lane = lax.broadcasted_iota(jnp.int32, (1, LANES), 1)
    lower = (lane & (HEAD_DIM - 1)) < HALF
    up = pltpu.roll(values, LANES - HALF, 1)
    down = pltpu.roll(values, HALF, 1)
    return lower, up, down


def rotary(values, cos, sin):
    lower, up, down = swap_halves(values)
    return values * cos + jnp.where(lower, -up, down) * sin


def unrotary(values, cos, sin):
    lower, up, down = swap_halves(values * sin)
    return values * cos + jnp.where(lower, up, -down)


def qkv_kernel(x_ref, mod_ref, w_ref, cos_ref, sin_ref, xm_ref, q_ref, k_ref, v_ref):
    width = x_ref.shape[1]
    normed, _ = norm_forward(x_ref[...].astype(f32))
    xm = (normed * mod_ref[0:1, :] + mod_ref[1:2, :]).astype(bf16)
    xm_ref[...] = xm
    cos, sin = cos_ref[...], sin_ref[...]
    for part, ref in enumerate((q_ref, k_ref, v_ref)):
        whole = dot_nn(xm, w_ref[:, part * width : (part + 1) * width]).astype(bf16)
        if part == 2:
            ref[...] = whole
            continue
        for lane in range(0, width, LANES):
            piece = whole[:, lane : lane + LANES].astype(f32)
            ref[:, lane : lane + LANES] = rotary(piece, cos, sin).astype(bf16)


def project_qkv(x, mods, weight, cos, sin, rows=256):
    length, width = x.shape
    block = pl.BlockSpec((rows, width), lambda i: (i, 0))
    table = pl.BlockSpec((rows, LANES), lambda i: (i, 0))
    shape = pltpu.HBM((length, width), bf16)
    return pl.pallas_call(
        qkv_kernel,
        grid=(length // rows,),
        in_specs=[
            block,
            VMEM,
            pl.BlockSpec(weight.shape, lambda i: (0, 0)),
            table,
            table,
        ],
        out_specs=[block] * 4,
        out_shape=[shape] * 4,
        cost_estimate=COVER,
        compiler_params=pltpu.CompilerParams(vmem_limit_bytes=18 * MIB),
        name="project_qkv",
    )(*streamed(x), mods, *streamed(weight, cos, sin))


def attention_forward_kernel(q_ref, k_ref, v_ref, o_ref, lse_ref, *, chunk, ahead):
    k, v = k_ref[...], v_ref[...]
    first = lax.broadcasted_iota(jnp.int32, (1, LANES), 1) < HEAD_DIM
    c = LOG2E * SCALE
    masks = (first, ~first)
    keys = [jnp.where(m, k, jnp.zeros_like(k)) for m in masks]
    values = [jnp.where(m, v, jnp.ones_like(v)) for m in masks]
    items = [(h, start) for start in range(0, q_ref.shape[0], chunk) for h in range(2)]

    def scores(h, start):
        return dot_nt(keys[h], q_ref[start : start + chunk, :])

    waiting = [scores(*item) for item in items[:ahead]]
    outs = {}
    for i, (h, start) in enumerate(items):
        st = waiting.pop(0)
        if i + ahead < len(items):
            waiting.append(scores(*items[i + ahead]))
        rows = slice(start, start + chunk)
        top = jnp.max(st, axis=0, keepdims=True) * c
        p = jnp.exp2(st * c - top).astype(bf16)
        ot = dot_tn(values[h], p)
        own, ones = (ot[:HEAD_DIM], ot[HEAD_DIM:]) if h == 0 else (ot[HEAD_DIM:], ot[:HEAD_DIM])
        total = ones[0:1]
        outs[h] = own * (1.0 / total)
        lse_ref[0, h : h + 1, rows] = top + jnp.log2(total)
        if h == 1:
            o_ref[rows, :] = jnp.concatenate([outs[0], outs[1]], axis=0).T.astype(bf16)


def attention_forward(q, k, v):
    length, width = q.shape
    pairs = width // LANES
    block = pl.BlockSpec((length, LANES), lambda i: (0, i))
    return pl.pallas_call(
        functools.partial(attention_forward_kernel, chunk=length // 2, ahead=2),
        grid=(pairs,),
        in_specs=[block] * 3,
        out_specs=[block, pl.BlockSpec((1, 2, length), lambda i: (i, 0, 0))],
        out_shape=[
            pltpu.HBM((length, width), bf16),
            pltpu.HBM((pairs, 2, length), f32),
        ],
        cost_estimate=COVER,
        compiler_params=pltpu.CompilerParams(vmem_limit_bytes=14 * MIB),
        name="attention_forward",
    )(*streamed(q, k, v))


def attention_backward_kernel(
    q_ref, k_ref, v_ref, do_ref, o_ref, lse_ref, cos_ref, sin_ref, x_ref, gm_ref, mod_ref, w_ref,
    g_ref, hg_ref, sum_ref, held_ref, *, pairs,
):
    step = pl.program_id(0)
    width = x_ref.shape[1]

    @pl.when(step < pairs)
    def _():
        first = lax.broadcasted_iota(jnp.int32, (1, LANES), 1) < HEAD_DIM
        upper = lax.broadcasted_iota(jnp.int32, (LANES, 1), 0) < HEAD_DIM
        c = LOG2E * SCALE
        q, k, v, do = q_ref[...], k_ref[...], v_ref[...], do_ref[...]
        prod = (do.astype(f32) * o_ref[...].astype(f32)).T
        kt = k.T
        zero = jnp.zeros_like(k)
        dq = dk = dv = None
        for h in range(2):
            mine = first if h == 0 else ~first
            row = column_sum(prod[h * HEAD_DIM : (h + 1) * HEAD_DIM])
            st = dot_nt(jnp.where(mine, k, zero), q)
            p = jnp.exp2(st * c - lse_ref[0, h : h + 1, :])
            dp = dot_nt(jnp.where(mine, v, zero), do)
            ds = (p * (dp - row)).astype(bf16)
            dvh = dot_nn(p.astype(bf16), jnp.where(mine, do, zero))
            dkh = dot_nn(ds, jnp.where(mine, q, zero))
            dqh = dot_nn(jnp.where(upper if h == 0 else ~upper, kt, jnp.zeros_like(kt)), ds)
            dq, dk, dv = (dqh, dkh, dvh) if h == 0 else (dq + dqh, dk + dkh, dv + dvh)
        cos, sin = cos_ref[...], sin_ref[...]
        lanes = pl.ds(pl.multiple_of(step * LANES, LANES), LANES)
        for part, value in enumerate(
            (unrotary(dq.T * SCALE, cos, sin), unrotary(dk * SCALE, cos, sin), dv)
        ):
            value = value.astype(bf16)
            g_ref[part] = value
            held_ref[part, :, lanes] = value

    @pl.when(step >= pairs)
    def _():
        rows = x_ref.shape[0]
        tile = pl.ds(pl.multiple_of((step - pairs) * rows, rows), rows)
        normed, inverse = norm_forward(x_ref[...].astype(f32))
        grad = None
        for part in range(3):
            g = dot_nt(held_ref[part, tile, :], w_ref[:, part * width : (part + 1) * width])
            grad = g if grad is None else grad + g
        hg = gm_ref[...] + norm_backward(grad * mod_ref[0:1, :], normed, inverse)
        hg_ref[...] = hg.astype(bf16)
        sums = jnp.concatenate(
            [column_sum(grad), column_sum(grad * normed), jnp.zeros((6, width), f32)], axis=0
        )

        @pl.when(step == pairs)
        def _():
            sum_ref[...] = sums

        @pl.when(step > pairs)
        def _():
            sum_ref[...] += sums


def attention_backward(q, k, v, do, o, lse, cos, sin, x, gm, mods, weight, rows):
    length, width = q.shape
    pairs = width // LANES

    def pair(i):
        return jnp.minimum(i, pairs - 1)

    block = pl.BlockSpec((length, LANES), lambda i: (0, pair(i)))
    table = pl.BlockSpec((length, LANES), lambda i: (0, 0))
    tile = pl.BlockSpec((rows, width), lambda i: (jnp.maximum(i - pairs, 0), 0))
    return pl.pallas_call(
        functools.partial(attention_backward_kernel, pairs=pairs),
        grid=(pairs + length // rows,),
        in_specs=[block] * 5
        + [pl.BlockSpec((1, 2, length), lambda i: (pair(i), 0, 0)), table, table, tile, tile, VMEM, VMEM],
        out_specs=[
            pl.BlockSpec((3, length, LANES), lambda i: (0, 0, pair(i))),
            tile,
            pl.BlockSpec((8, width), lambda i: (0, 0)),
        ],
        out_shape=[
            pltpu.HBM((3, length, width), bf16),
            pltpu.HBM((length, width), bf16),
            jax.ShapeDtypeStruct((8, width), f32),
        ],
        scratch_shapes=[pltpu.VMEM((3, length, width), bf16)],
        cost_estimate=COVER,
        compiler_params=pltpu.CompilerParams(vmem_limit_bytes=34 * MIB),
        name="attention_backward",
    )(q, k, v, do, o, lse, cos, sin, x, gm, mods, weight)


def mlp_kernel(
    x_ref, mixed_ref, cot_ref, mod_ref, bias_ref, wo_ref, wu_ref, wd_ref,
    xm_ref, act_ref, gd_ref, gp_ref, gm_ref, gmix_ref, sum_ref, up_sum_ref, out_ref,
):
    chunk, ff = wu_ref.shape
    gate_attn, scaled, shift = mod_ref[0:1, :], mod_ref[1:2, :], mod_ref[2:3, :]
    gate_mlp, down_bias = mod_ref[3:4, :], mod_ref[4:5, :]
    cot = cot_ref[...].astype(f32)
    projected = dot_nn(mixed_ref[...], wo_ref[...])
    middle = x_ref[...].astype(f32) + gate_attn * projected
    normed, inverse = norm_forward(middle)
    xm = (normed * scaled + shift).astype(bf16)
    xm_ref[0] = xm
    xm_ref[1] = mixed_ref[...]
    gd = (gate_mlp * cot).astype(bf16)
    gd_ref[...] = gd
    down = grad_mod = None
    c0 = 0.7978845608028654
    c1 = c0 * 0.044715
    up_sums = []
    for at in range(0, ff, chunk):
        cols = slice(at, at + chunk)
        pre = dot_nn(xm, wu_ref[:, cols]) + bias_ref[:, cols]
        square = pre * pre
        t = jnp.tanh(pre * (c0 + c1 * square))
        half = 0.5 + 0.5 * t
        wide_act = pre * half
        act = wide_act.astype(bf16)
        act_ref[:, cols] = act
        slope = half + wide_act * (1.0 - half) * (2.0 * c0 + (6.0 * c1) * square)
        wide_gp = slope * dot_nt(gd, wd_ref[cols, :])
        gp = wide_gp.astype(bf16)
        gp_ref[at // chunk] = gp
        up_sums.append(column_sum(wide_gp))
        d = dot_nn(act, wd_ref[cols, :])
        g = dot_nt(gp, wu_ref[:, cols])
        down, grad_mod = (d, g) if down is None else (down + d, grad_mod + g)
    down = down + down_bias
    out_ref[...] = (middle + gate_mlp * down).astype(bf16)
    gm = cot + norm_backward(grad_mod * scaled, normed, inverse)
    gm_ref[...] = gm
    gpj = (gate_attn * gm).astype(bf16)
    gp_ref[ff // chunk] = gpj
    gmix_ref[...] = dot_nt(gpj, wo_ref[...]).astype(bf16)
    sums = jnp.concatenate(
        [
            column_sum(cot * down),
            column_sum(gd.astype(f32)),
            column_sum(grad_mod),
            column_sum(grad_mod * normed),
            column_sum(gm * projected),
            jnp.zeros((3, cot.shape[1]), f32),
        ],
        axis=0,
    )
    up_sum = jnp.concatenate(up_sums, axis=1)

    @pl.when(pl.program_id(0) == 0)
    def _():
        sum_ref[...] = sums
        up_sum_ref[...] = up_sum

    @pl.when(pl.program_id(0) > 0)
    def _():
        sum_ref[...] += sums
        up_sum_ref[...] += up_sum


def feed_forward(x, mixed, cot, mods, up_bias, wo, wu, wd, rows):
    length, width = x.shape
    ff = wu.shape[1]
    block = pl.BlockSpec((rows, width), lambda i: (i, 0))
    wide = pl.BlockSpec((rows, ff), lambda i: (i, 0))

    narrow = pltpu.HBM((length, width), bf16)
    broad = pltpu.HBM((length, ff), bf16)
    return pl.pallas_call(
        mlp_kernel,
        grid=(length // rows,),
        in_specs=[block, block, block] + [VMEM] * 5,
        out_specs=[
            pl.BlockSpec((2, rows, width), lambda i: (0, i, 0)),
            wide,
            block,
            pl.BlockSpec((ff // width + 1, rows, width), lambda i: (0, i, 0)),
            block,
            block,
            pl.BlockSpec((8, width), lambda i: (0, 0)),
            pl.BlockSpec((1, ff), lambda i: (0, 0)),
        ]
        + [block],
        out_shape=[
            pltpu.HBM((2, length, width), bf16), broad, narrow,
            pltpu.HBM((ff // width + 1, length, width), bf16),
            pltpu.HBM((length, width), f32), narrow,
            jax.ShapeDtypeStruct((8, width), f32), jax.ShapeDtypeStruct((1, ff), f32),
        ]
        + [narrow],
        cost_estimate=COVER,
        compiler_params=pltpu.CompilerParams(vmem_limit_bytes=40 * MIB),
        name="feed_forward",
    )(x, *streamed(mixed, cot), mods, up_bias, wo, *streamed(wu, wd))


def late_grads_kernel(
    core_ref, sum_ref, mod_ref, ada_ref, timing_ref, early_ref, xm_ref, block_ref,
    time_ref, send_ref, keep_ref, *, parts,
):
    step = pl.program_id(0)
    width = block_ref.shape[2]

    @pl.when(step < parts)
    def _():
        product = dot_tn(xm_ref[...], block_ref[0])
        half = send_ref.shape[1]
        for i, (send, keep) in enumerate(split_halves(product, half, core_ref[0] == 0)):
            send_ref[i] = send
            keep_ref[i] = keep

    @pl.when(step == parts)
    def _():
        sp, half, _ = send_ref.shape
        shift, scaled = sum_ref[0:1, :], sum_ref[1:2, :]
        scale = scaled * mod_ref[0:1, :]
        gain = scaled * mod_ref[1:2, :]
        row = jnp.concatenate([shift, scale] + [early_ref[i : i + 1, :] for i in range(4)], axis=1)
        high = row.astype(bf16)
        low = (row - high.astype(f32)).astype(bf16)
        time_ref[...] = (dot_nt(high, ada_ref[...]) + dot_nt(low, ada_ref[...])).astype(bf16)
        bias = jnp.concatenate([shift, scale, jnp.zeros((1, 4 * width), f32)], axis=1)
        count, own, quarter = timing_ref.shape[0] // sp, 6 * width // sp, width // sp
        for ref, first in ((send_ref, core_ref[0] == 1), (keep_ref, core_ref[0] == 0)):
            part = jnp.where(first, shift, scale)
            for i in range(sp):
                ref[i, :count] = (timing_ref[i * count : (i + 1) * count, :] * part).astype(bf16)
                mine = bias[:, i * own : (i + 1) * own]
                rest = jnp.concatenate(
                    [
                        mine[:, width:],
                        gain[:, i * quarter : (i + 1) * quarter],
                        jnp.zeros((1, 2 * width - own - quarter), f32),
                    ],
                    axis=1,
                )
                sums = jnp.concatenate(
                    [jnp.where(first, mine[:, :width], rest), jnp.zeros((half - count - 1, width), f32)], axis=0
                )
                ref[i, count:] = sums.astype(bf16)


def late_grads(core, grads, xm, sums, mods, ada, timing, early, sp):
    n, length, width = grads.shape
    half = width // sp // 2
    out = pl.BlockSpec((sp, half, width), lambda i, c: (0, i, 0))
    shape = jax.ShapeDtypeStruct((sp, (n + 1) * half, width), bf16)
    cond = timing.shape[0]
    return pl.pallas_call(
        functools.partial(late_grads_kernel, parts=n),
        grid_spec=pltpu.PrefetchScalarGridSpec(
            num_scalar_prefetch=1,
            grid=(n + 1,),
            in_specs=[VMEM] * 5
            + [
                pl.BlockSpec((length, width), lambda i, c: (0, 0)),
                pl.BlockSpec((1, length, width), lambda i, c: (jnp.minimum(i, n - 1), 0, 0)),
            ],
            out_specs=[pl.BlockSpec((1, cond), lambda i, c: (0, 0)), out, out],
        ),
        out_shape=[jax.ShapeDtypeStruct((1, cond), bf16), shape, shape],
        cost_estimate=COVER,
        compiler_params=pltpu.CompilerParams(vmem_limit_bytes=18 * MIB),
        name="late_grads",
    )(core, sums, mods, ada, timing, early, xm, grads)


def split_halves(product, half, this_core):
    pieces = []
    for at in range(0, product.shape[0], 2 * half):
        low = product[at : at + half].astype(bf16)
        high = product[at + half : at + 2 * half].astype(bf16)
        pieces.append((jnp.where(this_core, high, low), jnp.where(this_core, low, high)))
    return pieces


def row_grad_kernel(core_ref, a_ref, b_ref, send_ref, keep_ref, *, half):
    product = dot_tn(a_ref[...], b_ref[...])
    for i, (send, keep) in enumerate(split_halves(product, half, core_ref[0] == 0)):
        send_ref[0, i * half : (i + 1) * half] = send
        keep_ref[0, i * half : (i + 1) * half] = keep


def row_grad(core, a, b, sp):
    length, width = b.shape
    out = pltpu.HBM((sp, width // 2, width), bf16)
    block = pl.BlockSpec((1, width // 2, width), lambda j, c: (j, 0, 0))
    return pl.pallas_call(
        functools.partial(row_grad_kernel, half=width // sp // 2),
        grid_spec=pltpu.PrefetchScalarGridSpec(
            num_scalar_prefetch=1,
            grid=(sp,),
            in_specs=[
                pl.BlockSpec((length, width), lambda j, c: (0, j)),
                pl.BlockSpec((length, width), lambda j, c: (0, 0)),
            ],
            out_specs=[block, block],
        ),
        out_shape=[out, out],
        cost_estimate=COVER,
        compiler_params=pltpu.CompilerParams(vmem_limit_bytes=18 * MIB),
        name="row_grad",
    )(core, *streamed(a, b))


def column_grad_kernel(
    core_ref, sum_ref, up_sum_ref, mod_ref, timing_ref, a_ref, b_ref, send_ref, keep_ref, parts_ref, *, blocks
):
    step = pl.program_id(0)
    sp, half, width = send_ref.shape

    @pl.when(step < blocks)
    def _():
        product = dot_tn(a_ref[0], b_ref[0])
        for i, (send, keep) in enumerate(split_halves(product, half, core_ref[0] == 0)):
            send_ref[i] = send
            keep_ref[i] = keep

    @pl.when(step == blocks)
    def _():
        scaled = sum_ref[3:4, :]
        parts = [sum_ref[4:5, :], sum_ref[2:3, :], scaled * mod_ref[0:1, :], sum_ref[0:1, :]]
        for i, part in enumerate(parts):
            parts_ref[i : i + 1, :] = part
        gain = scaled * mod_ref[1:2, :]
        bias = jnp.concatenate([jnp.zeros((1, 2 * width), f32)] + parts, axis=1)
        count, own, quarter = timing_ref.shape[0] // sp, 6 * width // sp, width // sp
        for ref, first in ((send_ref, core_ref[0] == 1), (keep_ref, core_ref[0] == 0)):
            for i in range(sp):
                column = timing_ref[i * count : (i + 1) * count, :]
                for p in range(2):
                    part = jnp.where(first, parts[p], parts[p + 2])
                    ref[i, p * count : (p + 1) * count] = (column * part).astype(bf16)
                shard = slice(i * quarter, (i + 1) * quarter)
                mine = bias[:, i * own : (i + 1) * own]
                gains = jnp.concatenate(
                    [gain[:, shard], sum_ref[1:2, shard], jnp.zeros((1, width - 2 * quarter), f32)], axis=1
                )
                rest = jnp.concatenate([mine[:, width:], jnp.zeros((1, 2 * width - own), f32)], axis=1)
                sums = jnp.concatenate(
                    [
                        jnp.where(first, up_sum_ref[:, i * width : (i + 1) * width], gains),
                        jnp.where(first, mine[:, :width], rest),
                        jnp.zeros((half - 2 * count - 2, width), f32),
                    ],
                    axis=0,
                )
                ref[i, 2 * count :] = sums.astype(bf16)


def column_grad(core, sums, up_sum, mods, timing, a, b, sp, second):
    _, length, width = a.shape
    n = b.shape[0]
    half = width // sp // 2
    out = pltpu.HBM((sp, (n + 1) * half, width), bf16)
    block = pl.BlockSpec((sp, half, width), lambda j, c: (0, j, 0))
    return pl.pallas_call(
        functools.partial(column_grad_kernel, blocks=n),
        grid_spec=pltpu.PrefetchScalarGridSpec(
            num_scalar_prefetch=1,
            grid=(n + 1,),
            in_specs=[VMEM] * 4
            + [
                pl.BlockSpec((1, length, width), lambda j, c: (jnp.minimum(j, n - 1) // second, 0, 0)),
                pl.BlockSpec((1, length, width), lambda j, c: (jnp.minimum(j, n - 1), 0, 0)),
            ],
            out_specs=[block, block, pl.BlockSpec((4, width), lambda j, c: (0, 0))],
        ),
        out_shape=[out, out, jax.ShapeDtypeStruct((4, width), f32)],
        cost_estimate=COVER,
        compiler_params=pltpu.CompilerParams(vmem_limit_bytes=18 * MIB),
        name="column_grad",
    )(core, sums, up_sum, mods, timing, *streamed(a, b))


def shift_permute(value, axis, by):
    n = lax.axis_size(axis)
    return lax.ppermute(value, axis, [(i, (i + by) % n) for i in range(n)])


def pair_permute(value, bit, axis="dp"):
    n = lax.axis_size(axis)
    return lax.ppermute(value, axis, [(i, i ^ bit) for i in range(n)])


def pick(values, index, axis=0):
    return lax.dynamic_index_in_dim(values, index, axis, keepdims=False)


def after(values, *others):
    return lax.optimization_barrier((values, others))[0]


def bit_of(index, bit):
    return (index // bit) % 2


def add(a, b):
    return (a.astype(f32) + b.astype(f32)).astype(bf16)


CORE, FIRST, SECOND = 1, 2, 4


def first_halves_kernel(at_ref, row_keep, row_got, col_keep, col_got, *outs):
    columns = outs[0].shape[2]
    start = 0
    for keep, got in ((row_keep, row_got), (col_keep, col_got)):
        total = add(keep[0], got[0])
        n = total.shape[0] // 2
        low, high = total[:n], total[n:]
        for side in range(2):
            cols = slice(side * columns, (side + 1) * columns)
            mine = at_ref[side] == 0
            outs[2 * side][0, start : start + n] = jnp.where(mine, high, low)[:, cols]
            outs[2 * side + 1][0, start : start + n] = jnp.where(mine, low, high)[:, cols]
        start += n


def first_halves(at, row_keep, row_got, col_keep, col_got):
    sp, rows, width = row_keep.shape
    cols = col_keep.shape[1]

    def spec(a):
        return pl.BlockSpec((1,) + a.shape[1:], lambda s, t: (s, 0, 0))

    out = pltpu.HBM((sp, (rows + cols) // 2, width // 2), bf16)
    return pl.pallas_call(
        first_halves_kernel,
        grid_spec=pltpu.PrefetchScalarGridSpec(
            num_scalar_prefetch=1,
            grid=(sp,),
            in_specs=[spec(a) for a in (row_keep, row_got, col_keep, col_got)],
            out_specs=[spec(out)] * 4,
        ),
        out_shape=[out] * 4,
        cost_estimate=COVER,
        compiler_params=pltpu.CompilerParams(vmem_limit_bytes=12 * MIB),
        name="first_halves",
    )(at, *streamed(row_keep, row_got, col_keep, col_got))


def second_halves_kernel(at_ref, *refs):
    for side in range(2):
        mine = at_ref[1 - side]
        keep, got = refs[2 * side : 2 * side + 2]
        for s in range(keep.shape[0]):
            refs[4 + 2 * side][s] = add(keep[s, 1 - mine], got[s, 1 - mine])
            refs[5 + 2 * side][s] = add(keep[s, mine], got[s, mine])


def second_halves(at, *arrays):
    sp, rows, columns = arrays[0].shape
    out = jax.ShapeDtypeStruct((sp, rows // 2, columns), bf16)
    return pl.pallas_call(
        second_halves_kernel,
        in_specs=[SMEM] + [VMEM] * 4,
        out_specs=[VMEM] * 4,
        out_shape=[out] * 4,
        cost_estimate=COVER,
        compiler_params=pltpu.CompilerParams(vmem_limit_bytes=10 * MIB),
        name="second_halves",
    )(at, *streamed(*[a.reshape(sp, 2, rows // 2, columns) for a in arrays]))


def near_halves_kernel(at_ref, *refs, terms, sides):
    ins, outs = refs[:-2], refs[-2:]
    mine = lax.rem(at_ref[2], 2)
    for out, bit in zip(outs, (1 - mine, mine)):
        for s in range(out.shape[0]):
            at = 0
            for side in range(sides):
                total = None
                for ref in ins[side * terms : (side + 1) * terms]:
                    value = ref[2 * s + bit].astype(f32)
                    total = value if total is None else total + value
                out[s, :, at : at + total.shape[1]] = total.astype(bf16)
                at += total.shape[1]


def near_halves(at, sides):
    terms = len(sides[0])
    flat = [a for side in sides for a in side]
    sp, rows, _ = flat[0].shape
    width = sum(side[0].shape[2] for side in sides)
    out = jax.ShapeDtypeStruct((sp // 2, rows, width), bf16)
    return pl.pallas_call(
        functools.partial(near_halves_kernel, terms=terms, sides=len(sides)),
        in_specs=[SMEM] + [VMEM] * len(flat),
        out_specs=[VMEM] * 2,
        out_shape=[out] * 2,
        cost_estimate=COVER,
        compiler_params=pltpu.CompilerParams(vmem_limit_bytes=8 * MIB),
        name="near_halves",
    )(at, *on_chip(flat))


def far_halves_kernel(at_ref, keep, got, send_ref, keep_ref):
    mine = lax.div(at_ref[2], 2)
    send_ref[...] = add(keep[1 - mine], got[1 - mine])
    keep_ref[...] = add(keep[mine], got[mine])


def far_halves(at, keep, got):
    out = jax.ShapeDtypeStruct(keep.shape[1:], bf16)
    return pl.pallas_call(
        far_halves_kernel,
        in_specs=[SMEM] + [VMEM] * 2,
        out_specs=[VMEM] * 2,
        out_shape=[out] * 2,
        cost_estimate=COVER,
        name="far_halves",
    )(at, keep, got)


def hand_over_kernel(in_ref, out_ref):
    out_ref[...] = in_ref[...].astype(out_ref.dtype)


def widen(value):
    return hand_over(value, f32)


def hand_over(value, dtype=bf16):
    block = pl.BlockSpec((1,) + value.shape[1:], lambda i: (i, 0, 0))
    return pl.pallas_call(
        hand_over_kernel,
        grid=(value.shape[0],),
        in_specs=[block],
        out_specs=block,
        out_shape=jax.ShapeDtypeStruct(value.shape, dtype),
        cost_estimate=COVER,
        compiler_params=pltpu.CompilerParams(vmem_limit_bytes=6 * MIB),
        name="hand_over",
    )(value)


def own_kernel(keep_ref, got_ref, out_ref):
    out_ref[...] = add(keep_ref[...], got_ref[...])


def own_sum(keep, got):
    return pl.pallas_call(
        own_kernel,
        in_specs=[VMEM] * 2,
        out_specs=VMEM,
        out_shape=jax.ShapeDtypeStruct(keep.shape, bf16),
        cost_estimate=COVER,
        name="own_sum",
    )(keep, got)


def quarters_kernel(at_ref, keep_ref, got_ref, *outs):
    for i, out in enumerate(outs):
        index = 2 * (at_ref[0] ^ (i // 2)) + (at_ref[1] ^ (i % 2))
        for s in range(keep_ref.shape[0]):
            out[s] = add(keep_ref[s, index], got_ref[s, index])


def quarters(at, keep, got):
    sp, rows, width = keep.shape
    out = jax.ShapeDtypeStruct((sp, rows // 4, width), bf16)
    return pl.pallas_call(
        quarters_kernel,
        in_specs=[SMEM] + [VMEM] * 2,
        out_specs=[VMEM] * 4,
        out_shape=[out] * 4,
        cost_estimate=COVER,
        compiler_params=pltpu.CompilerParams(vmem_limit_bytes=10 * MIB),
        name="quarters",
    )(at, *on_chip([a.reshape(sp, 4, rows // 4, width) for a in (keep, got)]))


def four_chips_kernel(at_ref, *refs, crossed):
    pieces, out_ref = refs[:4], refs[4]
    columns = out_ref.shape[2] // 2
    for i, piece in enumerate(pieces):
        x, y = at_ref[0] ^ (i // 2), at_ref[1] ^ (i % 2)
        out_ref[2 * x + y, :, :columns] = piece[:, :columns]
        out_ref[2 * y + x if crossed else 2 * x + y, :, columns:] = piece[:, columns:]


def four_chips(at, pieces, crossed):
    rows, width = pieces[0].shape
    return pl.pallas_call(
        functools.partial(four_chips_kernel, crossed=crossed),
        in_specs=[SMEM] + [VMEM] * 4,
        out_specs=VMEM,
        out_shape=jax.ShapeDtypeStruct((4, rows, width), bf16),
        cost_estimate=COVER,
        compiler_params=pltpu.CompilerParams(vmem_limit_bytes=8 * MIB),
        name="four_chips",
    )(at, *on_chip(pieces)).reshape(4 * rows, width)


def spread(own):
    return [own] + [pair_permute(own, bit) for bit in (SECOND, FIRST, FIRST + SECOND)]


def finish_kernel(core_ref, mine_ref, other_ref, *outs, half, layout):
    first = core_ref[0] == 0
    width = mine_ref.shape[1]
    for out, (_, across, starts) in zip(outs, layout):
        for n, at in enumerate(starts):
            cols = slice(n % across * width, (n % across + 1) * width)
            mine = mine_ref[at : at + half].astype(f32)
            other = other_ref[at : at + half].astype(f32)
            to = n // across * 2 * half
            out[to : to + half, cols] = jnp.where(first, mine, other)
            out[to + half : to + 2 * half, cols] = jnp.where(first, other, mine)


def finish(core, mine, other, half, layout):
    width = mine.shape[1]
    shapes = [(2 * half * down, width * across) for down, across, _ in layout]
    return pl.pallas_call(
        functools.partial(finish_kernel, half=half, layout=layout),
        grid=(1,),
        in_specs=[SMEM] + [VMEM] * 2,
        out_specs=[pl.BlockSpec(s, lambda i: (0, 0)) for s in shapes],
        out_shape=[jax.ShapeDtypeStruct(s, f32) for s in shapes],
        cost_estimate=COVER,
        compiler_params=pltpu.CompilerParams(vmem_limit_bytes=16 * MIB),
        name="finish",
    )(core, *on_chip([mine, other]))


def late_finish_kernel(
    core_ref, mine_ref, other_ref, early_ref, qkv_ref, ada_ref, bias_ref, attn_gain_ref, mlp_gain_ref, up_ref,
    down_ref, *, half,
):
    core_first = core_ref[0] == 0
    width = mine_ref.shape[1]
    for n in range(3):
        cols = slice(n * width, (n + 1) * width)
        mine = mine_ref[n * half : (n + 1) * half].astype(f32)
        other = other_ref[n * half : (n + 1) * half].astype(f32)
        qkv_ref[:half, cols] = jnp.where(core_first, mine, other)
        qkv_ref[half:, cols] = jnp.where(core_first, other, mine)
    mine, other = mine_ref[3 * half :].astype(f32), other_ref[3 * half :].astype(f32)
    late = (jnp.where(core_first, mine, other), jnp.where(core_first, other, mine))
    count = ada_ref.shape[0]
    quarter, own = attn_gain_ref.shape[1], bias_ref.size
    for p in range(2):
        ada_ref[:, p * width : (p + 1) * width] = late[p][:count]
    for p in range(4):
        start = p // 2 * half + p % 2 * count
        ada_ref[:, (2 + p) * width : (3 + p) * width] = early_ref[start : start + count, :]
    row, rest = 2 * count, own - width
    sums = (late[0][count : count + 1], late[1][count : count + 1])
    for lane in range(0, own, LANES):
        i, side = lane // LANES, lane // width
        cols = slice(lane % width, lane % width + LANES)
        at = side * half + row + 1
        bias_ref[i : i + 1, :] = early_ref[at : at + 1, cols] + sums[side][:, cols]
    for lane in range(0, width, LANES):
        i = lane // LANES
        up_ref[i : i + 1, :] = early_ref[row : row + 1, lane : lane + LANES]
    attn_gain_ref[...] = sums[1][:, rest : rest + quarter]
    mlp_gain_ref[...] = early_ref[half + row : half + row + 1, :quarter]
    down_ref[...] = early_ref[half + row : half + row + 1, quarter : 2 * quarter]


def late_finish(core, mine, other, early, half, cond, sp):
    width = early.shape[1]
    one = (1, width // sp)
    shapes = [
        (2 * half, 3 * width), (cond // sp, 6 * width), (6 * width // sp // LANES, LANES),
        one, one, (width // LANES, LANES), one,
    ]
    return pl.pallas_call(
        functools.partial(late_finish_kernel, half=half),
        grid=(1,),
        in_specs=[SMEM] + [VMEM] * 3,
        out_specs=[pl.BlockSpec(s, lambda i: (0, 0)) for s in shapes],
        out_shape=[jax.ShapeDtypeStruct(s, f32) for s in shapes],
        cost_estimate=COVER,
        compiler_params=pltpu.CompilerParams(vmem_limit_bytes=12 * MIB),
        name="late_finish",
    )(core, *on_chip([mine, other, early]))


def sum_over_rest(total):
    bit = 2 * SECOND
    while bit < lax.axis_size("dp"):
        total = add(total, pair_permute(total, bit))
        bit *= 2
    return total


def double(rows, bit, axis):
    return jnp.concatenate([rows, pair_permute(rows, bit, axis)], axis=0)


def bits(axis):
    n, bit = lax.axis_size(axis), 1
    while bit < n:
        yield bit
        bit *= 2


def body(
    hidden_in,
    time_embed,
    ada_weight,
    ada_bias,
    attn_gain,
    query_key_value_matrix,
    attention_output_matrix,
    mlp_gain,
    up_projection_matrix,
    up_bias,
    down_projection_matrix,
    down_bias,
    out_cotangent,
):
    sequences, local_len, width = hidden_in.shape
    sp, me = lax.axis_size("sp"), lax.axis_index("sp")
    assert sequences == sp
    def exchange(values):
        values = values.reshape(sp, local_len, width)
        return lax.all_to_all(values, "sp", split_axis=0, concat_axis=0, tiled=True)

    x = exchange(hidden_in).reshape(-1, width)
    cot = exchange(after(out_cotangent, x)).reshape(-1, width)
    here = lax.axis_index("dp")
    core = bit_of(here, CORE).reshape(1)
    at = jnp.stack([bit_of(here, FIRST), bit_of(here, SECOND), me])

    timing = lax.dynamic_slice_in_dim(time_embed, me, 1, 0)
    modulation = dot_nn(timing, ada_weight) + ada_bias.astype(f32)[None]
    shift_attn, scale_attn, gate_attn, shift_mlp, scale_mlp, gate_mlp = jnp.split(
        modulation, 6, axis=-1
    )
    gain_attn = attn_gain.astype(f32)[None]
    gain_mlp = mlp_gain.astype(f32)[None]
    zero = jnp.zeros_like(shift_attn)
    attn_mods = jnp.concatenate(
        [gain_attn * (1.0 + scale_attn), shift_attn] + [zero] * 6, axis=0
    )
    mlp_mods = jnp.concatenate(
        [gate_attn, gain_mlp * (1.0 + scale_mlp), shift_mlp, gate_mlp, down_bias.astype(f32)[None]]
        + [zero] * 3,
        axis=0,
    )
    late_mods = jnp.concatenate([gain_attn, 1.0 + scale_attn] + [zero] * 6, axis=0)
    mlp_grad_mods = jnp.concatenate([gain_mlp, 1.0 + scale_mlp] + [zero] * 6, axis=0)
    column = timing.astype(f32).reshape(timing.shape[1], 1)
    attn_mods, mlp_mods, late_mods, mlp_grad_mods, column, at, core = lax.optimization_barrier(
        (attn_mods, mlp_mods, late_mods, mlp_grad_mods, column, at, core)
    )
    lane = lax.broadcasted_iota(jnp.int32, (1, LANES), 1)
    frequency = 10000.0 ** (-((lane % HALF).astype(f32) * 2.0 / HEAD_DIM))
    row = lax.broadcasted_iota(jnp.int32, (sp * local_len, 1), 0)
    angles = row.astype(f32) * frequency
    cos, sin = jnp.cos(angles), jnp.sin(angles)

    xm_attn, q, k, v = project_qkv(x, attn_mods, query_key_value_matrix, cos, sin)
    mixed, lse = attention_forward(q, k, v)
    both_in, act, gd, both_grad, gm, gmix, sums, up_sum, out = feed_forward(
        x,
        mixed,
        cot,
        mlp_mods,
        up_bias.astype(f32)[None],
        attention_output_matrix,
        up_projection_matrix,
        down_projection_matrix,
        local_len,
    )
    ff = up_bias.shape[0]
    assert ff == sp * width
    n_up = ff // width
    half = width // sp // 2
    quarter = width // sp
    cond = timing.shape[1]
    output = exchange(out)
    col_send, col_keep, early_parts = column_grad(
        core, sums, up_sum, mlp_grad_mods, column, both_in, both_grad, sp, n_up
    )
    col_got = pair_permute(col_send, CORE)
    row_send, row_keep = row_grad(core, *after((act, gd), col_keep), sp)
    row_got = pair_permute(row_send, CORE)

    left_send, left, right_send, right = first_halves(at, row_keep, row_got, col_keep, col_got)
    left_got, right_got = pair_permute(left_send, FIRST), pair_permute(right_send, SECOND)
    gmix = after(gmix, left, right)
    grads, hg, attn_sums = attention_backward(
        q, k, v, gmix, mixed, lse, cos, sin, x, gm, attn_mods, query_key_value_matrix, local_len
    )
    left_got, right_got, output = after((left_got, right_got, output), grads)
    left_send, left, right_send, right = second_halves(at, left, left_got, right, right_got)
    left_got, right_got = pair_permute(left_send, SECOND), pair_permute(right_send, FIRST)
    grads = after(grads, left, right, output)

    time_row, late_send, late_keep = late_grads(
        core, grads, xm_attn, attn_sums, late_mods, ada_weight, column, early_parts, sp
    )
    hidden_grad = exchange(hg)
    late_got = pair_permute(late_send, CORE)
    left_got, right_got = after((left_got, right_got), late_keep)
    if lax.axis_size("dp") > 2 * SECOND:
        left, right = sum_over_rest(add(left, left_got)), sum_over_rest(add(right, right_got))
        sides = [(left,), (right,)]
    else:
        sides = [(left, left_got), (right, right_got)]
    near_send, near = near_halves(at, sides)
    near_got = pair_permute(near_send, 1, "sp")
    late_got = after(late_got, near)
    own_quarter, *other_quarters = quarters(at, late_keep, late_got)
    quarter_parts = [own_quarter] + [
        pair_permute(p, bit)
        for p, bit in zip(other_quarters, (SECOND, FIRST, FIRST + SECOND))
    ]
    output = hand_over(after(output, own_quarter))
    near_got, hidden_grad = after((near_got, hidden_grad), output)
    near_got = after(near_got, hidden_grad)
    upper = me // 2
    far_send = add(pick(near, 1 - upper), pick(near_got, 1 - upper))
    far = add(pick(near, upper), pick(near_got, upper))
    far_got = pair_permute(far_send, 2, "sp")
    quarter_parts = after(quarter_parts, far, far_send)
    if lax.axis_size("dp") > 2 * SECOND:
        total = sum(p.astype(f32) for p in quarter_parts).astype(bf16)
        quarter_parts = [sum_over_rest(total)]
    late_near_send, late_near = near_halves(at, [quarter_parts])
    late_near_got = pair_permute(late_near_send, 1, "sp")
    early_own = add(far, after(far_got, late_near))
    early_four = spread(early_own)
    late_near_got = after(late_near_got, early_own)
    late_far_send = add(pick(late_near, 1 - upper), pick(late_near_got, 1 - upper))
    late_far = add(pick(late_near, upper), pick(late_near_got, upper))
    late_far_got = pair_permute(late_far_send, 2, "sp")
    late_own = add(late_far, late_far_got)
    hidden_grad = after(hidden_grad, late_own).astype(f32)
    time_rows = after(time_row, late_own)
    for bit in bits("sp"):
        time_rows = double(time_rows, bit, "sp")
    time_grad = jnp.concatenate([pick(time_rows, me ^ s)[None] for s in range(sp)], axis=0)
    time_grad = time_grad.astype(f32)
    early_half = four_chips(at, after(early_four, late_own, time_rows, hidden_grad), True)
    early_other = pair_permute(early_half, CORE)
    late_four = spread(after(late_own, early_half))
    n_row, n_col = row_keep.shape[1] // 2, col_keep.shape[1] // 2
    row_starts = [x * (n_row + n_col) + i for x in range(2) for i in range(0, n_row, half)]
    col_starts = [x * (n_row + n_col) + n_row + i for x in range(2) for i in range(0, n_col, half)]
    down_grad, up_grad, proj_grad, early_vectors = finish(
        core,
        early_half,
        after(early_other, late_four[0]),
        half,
        (
            (sp, 1, row_starts),
            (1, n_up, col_starts[:n_up]),
            (1, 1, col_starts[n_up : n_up + 1]),
            (1, 1, col_starts[n_up + 1 :]),
        ),
    )
    late_half = four_chips(at, after(late_four, down_grad), False)
    late_other = pair_permute(late_half, CORE)
    qkv_grad, ada_weight_grad, *small = late_finish(
        core, late_half, late_other, early_vectors, half, cond, sp
    )
    ada_bias_grad, attn_gain_grad, mlp_gain_grad, up_bias_grad, down_bias_grad = (
        v.reshape(-1) for v in small
    )
    return (
        output,
        hidden_grad,
        time_grad,
        ada_weight_grad,
        ada_bias_grad,
        attn_gain_grad,
        qkv_grad,
        proj_grad,
        mlp_gain_grad,
        up_grad,
        up_bias_grad,
        down_grad,
        down_bias_grad,
    )


def solution(mesh):
    return jax.shard_map(
        body,
        mesh=mesh,
        in_specs=(P("dp", "sp", None), P("dp", None)) + (P(),) * 10 + (P("dp", "sp", None),),
        out_specs=(
            P("dp", "sp", None),
            P("dp", "sp", None),
            P("dp", None),
            P("sp", None),
            P("sp"),
            P("sp"),
            P("sp", None),
            P("sp", None),
            P("sp"),
            P("sp", None),
            P("sp"),
            P("sp", None),
            P("sp"),
        ),
        check_vma=False,
    )
```

```python
import functools

import jax
import jax.numpy as jnp
from jax import lax
from jax.experimental import pallas as pl
from jax.experimental.pallas import tpu as pltpu
from jax.sharding import PartitionSpec as P

HEAD_DIM = 64
MIB = 1 << 20
VMEM = pl.BlockSpec(memory_space=pltpu.VMEM)
SMEM = pl.BlockSpec(memory_space=pltpu.SMEM)
HALF = HEAD_DIM // 2
LANES = 128
EPSILON = 1e-05
LOG2E = 1.4426950408889634
SCALE = HEAD_DIM ** (-0.5)
f32 = jnp.float32
COVER = pl.CostEstimate(flops=40_000_000_000, bytes_accessed=100_000_000, transcendentals=0)
bf16 = jnp.bfloat16


def on_chip(arrays):
    return [pltpu.with_memory_space_constraint(a, pltpu.VMEM) for a in arrays]


def streamed(*arrays):
    return [pltpu.with_memory_space_constraint(a, pltpu.HBM) for a in arrays]


def dot_nn(a, b):
    return lax.dot_general(a, b, (((1,), (0,)), ((), ())), preferred_element_type=f32)


def dot_nt(a, b):
    return lax.dot_general(a, b, (((1,), (1,)), ((), ())), preferred_element_type=f32)


def dot_tn(a, b):
    return lax.dot_general(a, b, (((0,), (0,)), ((), ())), preferred_element_type=f32)


def column_sum(values):
    return jnp.sum(values, axis=0, keepdims=True)


def norm_forward(values):
    center = values - jnp.mean(values, axis=-1, keepdims=True)
    inverse = lax.rsqrt(jnp.mean(center * center, axis=-1, keepdims=True) + EPSILON)
    return center * inverse, inverse


def norm_backward(grad, normed, inverse):
    first = jnp.mean(grad, axis=-1, keepdims=True)
    second = jnp.mean(grad * normed, axis=-1, keepdims=True)
    return inverse * (grad - first - normed * second)


def swap_halves(values):
    lane = lax.broadcasted_iota(jnp.int32, (1, LANES), 1)
    lower = (lane & (HEAD_DIM - 1)) < HALF
    up = pltpu.roll(values, LANES - HALF, 1)
    down = pltpu.roll(values, HALF, 1)
    return lower, up, down


def rotary(values, cos, sin):
    lower, up, down = swap_halves(values)
    return values * cos + jnp.where(lower, -up, down) * sin


def unrotary(values, cos, sin):
    lower, up, down = swap_halves(values * sin)
    return values * cos + jnp.where(lower, up, -down)


def qkv_kernel(x_ref, mod_ref, w_ref, cos_ref, sin_ref, xm_ref, q_ref, k_ref, v_ref):
    width = x_ref.shape[1]
    normed, _ = norm_forward(x_ref[...].astype(f32))
    xm = (normed * mod_ref[0:1, :] + mod_ref[1:2, :]).astype(bf16)
    xm_ref[...] = xm
    cos, sin = cos_ref[...], sin_ref[...]
    for part, ref in enumerate((q_ref, k_ref, v_ref)):
        whole = dot_nn(xm, w_ref[:, part * width : (part + 1) * width]).astype(bf16)
        if part == 2:
            ref[...] = whole
            continue
        for lane in range(0, width, LANES):
            piece = whole[:, lane : lane + LANES].astype(f32)
            ref[:, lane : lane + LANES] = rotary(piece, cos, sin).astype(bf16)


def project_qkv(x, mods, weight, cos, sin, rows=256):
    length, width = x.shape
    block = pl.BlockSpec((rows, width), lambda i: (i, 0))
    table = pl.BlockSpec((rows, LANES), lambda i: (i, 0))
    shape = pltpu.HBM((length, width), bf16)
    return pl.pallas_call(
        qkv_kernel,
        grid=(length // rows,),
        in_specs=[
            block,
            VMEM,
            pl.BlockSpec(weight.shape, lambda i: (0, 0)),
            table,
            table,
        ],
        out_specs=[block] * 4,
        out_shape=[shape] * 4,
        cost_estimate=COVER,
        compiler_params=pltpu.CompilerParams(vmem_limit_bytes=18 * MIB),
        name="project_qkv",
    )(x, mods, *streamed(weight, cos, sin))


def attention_forward_kernel(q_ref, k_ref, v_ref, o_ref, lse_ref, *, chunk, ahead):
    k, v = k_ref[...], v_ref[...]
    first = lax.broadcasted_iota(jnp.int32, (1, LANES), 1) < HEAD_DIM
    c = LOG2E * SCALE
    masks = (first, ~first)
    keys = [jnp.where(m, k, jnp.zeros_like(k)) for m in masks]
    values = [jnp.where(m, v, jnp.ones_like(v)) for m in masks]
    items = [(h, start) for start in range(0, q_ref.shape[0], chunk) for h in range(2)]

    def scores(h, start):
        return dot_nt(keys[h], q_ref[start : start + chunk, :])

    waiting = [scores(*item) for item in items[:ahead]]
    outs = {}
    for i, (h, start) in enumerate(items):
        st = waiting.pop(0)
        if i + ahead < len(items):
            waiting.append(scores(*items[i + ahead]))
        rows = slice(start, start + chunk)
        top = jnp.max(st, axis=0, keepdims=True) * c
        p = jnp.exp2(st * c - top).astype(bf16)
        ot = dot_tn(values[h], p)
        own, ones = (ot[:HEAD_DIM], ot[HEAD_DIM:]) if h == 0 else (ot[HEAD_DIM:], ot[:HEAD_DIM])
        total = ones[0:1]
        outs[h] = own * (1.0 / total)
        lse_ref[0, h : h + 1, rows] = top + jnp.log2(total)
        if h == 1:
            o_ref[rows, :] = jnp.concatenate([outs[0], outs[1]], axis=0).T.astype(bf16)


def attention_forward(q, k, v):
    length, width = q.shape
    pairs = width // LANES
    block = pl.BlockSpec((length, LANES), lambda i: (0, i))
    return pl.pallas_call(
        functools.partial(attention_forward_kernel, chunk=length // 2, ahead=2),
        grid=(pairs,),
        in_specs=[block] * 3,
        out_specs=[block, pl.BlockSpec((1, 2, length), lambda i: (i, 0, 0))],
        out_shape=[
            pltpu.HBM((length, width), bf16),
            pltpu.HBM((pairs, 2, length), f32),
        ],
        cost_estimate=COVER,
        compiler_params=pltpu.CompilerParams(vmem_limit_bytes=14 * MIB),
        name="attention_forward",
    )(*streamed(q, k, v))


def attention_backward_kernel(
    q_ref, k_ref, v_ref, do_ref, o_ref, lse_ref, cos_ref, sin_ref, x_ref, gm_ref, mod_ref, w_ref,
    g_ref, hg_ref, sum_ref, held_ref, *, pairs,
):
    step = pl.program_id(0)
    width = x_ref.shape[1]

    @pl.when(step < pairs)
    def _():
        first = lax.broadcasted_iota(jnp.int32, (1, LANES), 1) < HEAD_DIM
        upper = lax.broadcasted_iota(jnp.int32, (LANES, 1), 0) < HEAD_DIM
        c = LOG2E * SCALE
        q, k, v, do = q_ref[...], k_ref[...], v_ref[...], do_ref[...]
        prod = (do.astype(f32) * o_ref[...].astype(f32)).T
        kt = k.T
        zero = jnp.zeros_like(k)
        dq = dk = dv = None
        for h in range(2):
            mine = first if h == 0 else ~first
            row = column_sum(prod[h * HEAD_DIM : (h + 1) * HEAD_DIM])
            st = dot_nt(jnp.where(mine, k, zero), q)
            p = jnp.exp2(st * c - lse_ref[0, h : h + 1, :])
            dp = dot_nt(jnp.where(mine, v, zero), do)
            ds = (p * (dp - row)).astype(bf16)
            dvh = dot_nn(p.astype(bf16), jnp.where(mine, do, zero))
            dkh = dot_nn(ds, jnp.where(mine, q, zero))
            dqh = dot_nn(jnp.where(upper if h == 0 else ~upper, kt, jnp.zeros_like(kt)), ds)
            dq, dk, dv = (dqh, dkh, dvh) if h == 0 else (dq + dqh, dk + dkh, dv + dvh)
        cos, sin = cos_ref[...], sin_ref[...]
        lanes = pl.ds(pl.multiple_of(step * LANES, LANES), LANES)
        for part, value in enumerate(
            (unrotary(dq.T * SCALE, cos, sin), unrotary(dk * SCALE, cos, sin), dv)
        ):
            value = value.astype(bf16)
            g_ref[part] = value
            held_ref[part, :, lanes] = value

    @pl.when(step >= pairs)
    def _():
        rows = x_ref.shape[0]
        tile = pl.ds(pl.multiple_of((step - pairs) * rows, rows), rows)
        normed, inverse = norm_forward(x_ref[...].astype(f32))
        grad = None
        for part in range(3):
            g = dot_nt(held_ref[part, tile, :], w_ref[:, part * width : (part + 1) * width])
            grad = g if grad is None else grad + g
        hg = gm_ref[...] + norm_backward(grad * mod_ref[0:1, :], normed, inverse)
        hg_ref[...] = hg.astype(bf16)
        sums = jnp.concatenate(
            [column_sum(grad), column_sum(grad * normed), jnp.zeros((6, width), f32)], axis=0
        )

        @pl.when(step == pairs)
        def _():
            sum_ref[...] = sums

        @pl.when(step > pairs)
        def _():
            sum_ref[...] += sums


def attention_backward(q, k, v, do, o, lse, cos, sin, x, gm, mods, weight, rows):
    length, width = q.shape
    pairs = width // LANES

    def pair(i):
        return jnp.minimum(i, pairs - 1)

    block = pl.BlockSpec((length, LANES), lambda i: (0, pair(i)))
    table = pl.BlockSpec((length, LANES), lambda i: (0, 0))
    tile = pl.BlockSpec((rows, width), lambda i: (jnp.maximum(i - pairs, 0), 0))
    return pl.pallas_call(
        functools.partial(attention_backward_kernel, pairs=pairs),
        grid=(pairs + length // rows,),
        in_specs=[block] * 5
        + [pl.BlockSpec((1, 2, length), lambda i: (pair(i), 0, 0)), table, table, tile, tile, VMEM, VMEM],
        out_specs=[
            pl.BlockSpec((3, length, LANES), lambda i: (0, 0, pair(i))),
            tile,
            pl.BlockSpec((8, width), lambda i: (0, 0)),
        ],
        out_shape=[
            pltpu.HBM((3, length, width), bf16),
            pltpu.HBM((length, width), bf16),
            jax.ShapeDtypeStruct((8, width), f32),
        ],
        scratch_shapes=[pltpu.VMEM((3, length, width), bf16)],
        cost_estimate=COVER,
        compiler_params=pltpu.CompilerParams(vmem_limit_bytes=34 * MIB),
        name="attention_backward",
    )(q, k, v, do, o, lse, cos, sin, x, gm, mods, weight)


def mlp_kernel(
    x_ref, mixed_ref, cot_ref, mod_ref, bias_ref, wo_ref, wu_ref, wd_ref,
    xm_ref, act_ref, gd_ref, gp_ref, gm_ref, gmix_ref, sum_ref, up_sum_ref, out_ref,
):
    chunk, ff = wu_ref.shape
    gate_attn, scaled, shift = mod_ref[0:1, :], mod_ref[1:2, :], mod_ref[2:3, :]
    gate_mlp, down_bias = mod_ref[3:4, :], mod_ref[4:5, :]
    cot = cot_ref[...].astype(f32)
    projected = dot_nn(mixed_ref[...], wo_ref[...])
    middle = x_ref[...].astype(f32) + gate_attn * projected
    normed, inverse = norm_forward(middle)
    xm = (normed * scaled + shift).astype(bf16)
    xm_ref[0] = xm
    xm_ref[1] = mixed_ref[...]
    gd = (gate_mlp * cot).astype(bf16)
    gd_ref[...] = gd
    down = grad_mod = None
    c0 = 0.7978845608028654
    c1 = c0 * 0.044715
    up_sums = []
    for at in range(0, ff, chunk):
        cols = slice(at, at + chunk)
        pre = dot_nn(xm, wu_ref[:, cols]) + bias_ref[:, cols]
        square = pre * pre
        t = jnp.tanh(pre * (c0 + c1 * square))
        half = 0.5 + 0.5 * t
        wide_act = pre * half
        act = wide_act.astype(bf16)
        act_ref[:, cols] = act
        slope = half + wide_act * (1.0 - half) * (2.0 * c0 + (6.0 * c1) * square)
        wide_gp = slope * dot_nt(gd, wd_ref[cols, :])
        gp = wide_gp.astype(bf16)
        gp_ref[at // chunk] = gp
        up_sums.append(column_sum(wide_gp))
        d = dot_nn(act, wd_ref[cols, :])
        g = dot_nt(gp, wu_ref[:, cols])
        down, grad_mod = (d, g) if down is None else (down + d, grad_mod + g)
    down = down + down_bias
    out_ref[...] = (middle + gate_mlp * down).astype(bf16)
    gm = cot + norm_backward(grad_mod * scaled, normed, inverse)
    gm_ref[...] = gm
    gpj = (gate_attn * gm).astype(bf16)
    gp_ref[ff // chunk] = gpj
    gmix_ref[...] = dot_nt(gpj, wo_ref[...]).astype(bf16)
    sums = jnp.concatenate(
        [
            column_sum(cot * down),
            column_sum(gd.astype(f32)),
            column_sum(grad_mod),
            column_sum(grad_mod * normed),
            column_sum(gm * projected),
            jnp.zeros((3, cot.shape[1]), f32),
        ],
        axis=0,
    )
    up_sum = jnp.concatenate(up_sums, axis=1)

    @pl.when(pl.program_id(0) == 0)
    def _():
        sum_ref[...] = sums
        up_sum_ref[...] = up_sum

    @pl.when(pl.program_id(0) > 0)
    def _():
        sum_ref[...] += sums
        up_sum_ref[...] += up_sum


def feed_forward(x, mixed, cot, mods, up_bias, wo, wu, wd, rows):
    length, width = x.shape
    ff = wu.shape[1]
    block = pl.BlockSpec((rows, width), lambda i: (i, 0))
    wide = pl.BlockSpec((rows, ff), lambda i: (i, 0))

    narrow = pltpu.HBM((length, width), bf16)
    broad = pltpu.HBM((length, ff), bf16)
    return pl.pallas_call(
        mlp_kernel,
        grid=(length // rows,),
        in_specs=[block, block, block] + [VMEM] * 5,
        out_specs=[
            pl.BlockSpec((2, rows, width), lambda i: (0, i, 0)),
            wide,
            block,
            pl.BlockSpec((ff // width + 1, rows, width), lambda i: (0, i, 0)),
            block,
            block,
            pl.BlockSpec((8, width), lambda i: (0, 0)),
            pl.BlockSpec((1, ff), lambda i: (0, 0)),
        ]
        + [block],
        out_shape=[
            pltpu.HBM((2, length, width), bf16), broad, narrow,
            pltpu.HBM((ff // width + 1, length, width), bf16),
            pltpu.HBM((length, width), f32), narrow,
            jax.ShapeDtypeStruct((8, width), f32), jax.ShapeDtypeStruct((1, ff), f32),
        ]
        + [narrow],
        cost_estimate=COVER,
        compiler_params=pltpu.CompilerParams(vmem_limit_bytes=40 * MIB),
        name="feed_forward",
    )(x, *streamed(mixed, cot), mods, up_bias, wo, *streamed(wu, wd))


def late_grads_kernel(
    core_ref, sum_ref, mod_ref, ada_ref, timing_ref, early_ref, xm_ref, block_ref,
    time_ref, send_ref, keep_ref, *, parts,
):
    step = pl.program_id(0)
    width = block_ref.shape[2]

    @pl.when(step < parts)
    def _():
        product = dot_tn(xm_ref[...], block_ref[0])
        half = send_ref.shape[1]
        for i, (send, keep) in enumerate(split_halves(product, half, core_ref[0] == 0)):
            send_ref[i] = send
            keep_ref[i] = keep

    @pl.when(step == parts)
    def _():
        sp, half, _ = send_ref.shape
        shift, scaled = sum_ref[0:1, :], sum_ref[1:2, :]
        scale = scaled * mod_ref[0:1, :]
        gain = scaled * mod_ref[1:2, :]
        row = jnp.concatenate([shift, scale] + [early_ref[i : i + 1, :] for i in range(4)], axis=1)
        high = row.astype(bf16)
        low = (row - high.astype(f32)).astype(bf16)
        time_ref[...] = (dot_nt(high, ada_ref[...]) + dot_nt(low, ada_ref[...])).astype(bf16)
        bias = jnp.concatenate([shift, scale, jnp.zeros((1, 4 * width), f32)], axis=1)
        count, own, quarter = timing_ref.shape[0] // sp, 6 * width // sp, width // sp
        for ref, first in ((send_ref, core_ref[0] == 1), (keep_ref, core_ref[0] == 0)):
            part = jnp.where(first, shift, scale)
            for i in range(sp):
                ref[i, :count] = (timing_ref[i * count : (i + 1) * count, :] * part).astype(bf16)
                mine = bias[:, i * own : (i + 1) * own]
                rest = jnp.concatenate(
                    [
                        mine[:, width:],
                        gain[:, i * quarter : (i + 1) * quarter],
                        jnp.zeros((1, 2 * width - own - quarter), f32),
                    ],
                    axis=1,
                )
                sums = jnp.concatenate(
                    [jnp.where(first, mine[:, :width], rest), jnp.zeros((half - count - 1, width), f32)], axis=0
                )
                ref[i, count:] = sums.astype(bf16)


def late_grads(core, grads, xm, sums, mods, ada, timing, early, sp):
    n, length, width = grads.shape
    half = width // sp // 2
    out = pl.BlockSpec((sp, half, width), lambda i, c: (0, i, 0))
    shape = jax.ShapeDtypeStruct((sp, (n + 1) * half, width), bf16)
    cond = timing.shape[0]
    return pl.pallas_call(
        functools.partial(late_grads_kernel, parts=n),
        grid_spec=pltpu.PrefetchScalarGridSpec(
            num_scalar_prefetch=1,
            grid=(n + 1,),
            in_specs=[VMEM] * 5
            + [
                pl.BlockSpec((length, width), lambda i, c: (0, 0)),
                pl.BlockSpec((1, length, width), lambda i, c: (jnp.minimum(i, n - 1), 0, 0)),
            ],
            out_specs=[pl.BlockSpec((1, cond), lambda i, c: (0, 0)), out, out],
        ),
        out_shape=[jax.ShapeDtypeStruct((1, cond), bf16), shape, shape],
        cost_estimate=COVER,
        compiler_params=pltpu.CompilerParams(vmem_limit_bytes=18 * MIB),
        name="late_grads",
    )(core, sums, mods, ada, timing, early, xm, grads)


def split_halves(product, half, this_core):
    pieces = []
    for at in range(0, product.shape[0], 2 * half):
        low = product[at : at + half].astype(bf16)
        high = product[at + half : at + 2 * half].astype(bf16)
        pieces.append((jnp.where(this_core, high, low), jnp.where(this_core, low, high)))
    return pieces


def row_grad_kernel(core_ref, a_ref, b_ref, send_ref, keep_ref, *, half):
    product = dot_tn(a_ref[...], b_ref[...])
    for i, (send, keep) in enumerate(split_halves(product, half, core_ref[0] == 0)):
        send_ref[0, i * half : (i + 1) * half] = send
        keep_ref[0, i * half : (i + 1) * half] = keep


def row_grad(core, a, b, sp):
    length, width = b.shape
    out = pltpu.HBM((sp, width // 2, width), bf16)
    block = pl.BlockSpec((1, width // 2, width), lambda j, c: (j, 0, 0))
    return pl.pallas_call(
        functools.partial(row_grad_kernel, half=width // sp // 2),
        grid_spec=pltpu.PrefetchScalarGridSpec(
            num_scalar_prefetch=1,
            grid=(sp,),
            in_specs=[
                pl.BlockSpec((length, width), lambda j, c: (0, j)),
                pl.BlockSpec((length, width), lambda j, c: (0, 0)),
            ],
            out_specs=[block, block],
        ),
        out_shape=[out, out],
        cost_estimate=COVER,
        compiler_params=pltpu.CompilerParams(vmem_limit_bytes=18 * MIB),
        name="row_grad",
    )(core, *streamed(a, b))


def column_grad_kernel(
    core_ref, sum_ref, up_sum_ref, mod_ref, timing_ref, a_ref, b_ref, send_ref, keep_ref, parts_ref, *, blocks
):
    step = pl.program_id(0)
    sp, half, width = send_ref.shape

    @pl.when(step < blocks)
    def _():
        product = dot_tn(a_ref[0], b_ref[0])
        for i, (send, keep) in enumerate(split_halves(product, half, core_ref[0] == 0)):
            send_ref[i] = send
            keep_ref[i] = keep

    @pl.when(step == blocks)
    def _():
        scaled = sum_ref[3:4, :]
        parts = [sum_ref[4:5, :], sum_ref[2:3, :], scaled * mod_ref[0:1, :], sum_ref[0:1, :]]
        for i, part in enumerate(parts):
            parts_ref[i : i + 1, :] = part
        gain = scaled * mod_ref[1:2, :]
        bias = jnp.concatenate([jnp.zeros((1, 2 * width), f32)] + parts, axis=1)
        count, own, quarter = timing_ref.shape[0] // sp, 6 * width // sp, width // sp
        for ref, first in ((send_ref, core_ref[0] == 1), (keep_ref, core_ref[0] == 0)):
            for i in range(sp):
                column = timing_ref[i * count : (i + 1) * count, :]
                for p in range(2):
                    part = jnp.where(first, parts[p], parts[p + 2])
                    ref[i, p * count : (p + 1) * count] = (column * part).astype(bf16)
                shard = slice(i * quarter, (i + 1) * quarter)
                mine = bias[:, i * own : (i + 1) * own]
                gains = jnp.concatenate(
                    [gain[:, shard], sum_ref[1:2, shard], jnp.zeros((1, width - 2 * quarter), f32)], axis=1
                )
                rest = jnp.concatenate([mine[:, width:], jnp.zeros((1, 2 * width - own), f32)], axis=1)
                sums = jnp.concatenate(
                    [
                        jnp.where(first, up_sum_ref[:, i * width : (i + 1) * width], gains),
                        jnp.where(first, mine[:, :width], rest),
                        jnp.zeros((half - 2 * count - 2, width), f32),
                    ],
                    axis=0,
                )
                ref[i, 2 * count :] = sums.astype(bf16)


def column_grad(core, sums, up_sum, mods, timing, a, b, sp, second):
    _, length, width = a.shape
    n = b.shape[0]
    half = width // sp // 2
    out = pltpu.HBM((sp, (n + 1) * half, width), bf16)
    block = pl.BlockSpec((sp, half, width), lambda j, c: (0, j, 0))
    return pl.pallas_call(
        functools.partial(column_grad_kernel, blocks=n),
        grid_spec=pltpu.PrefetchScalarGridSpec(
            num_scalar_prefetch=1,
            grid=(n + 1,),
            in_specs=[VMEM] * 4
            + [
                pl.BlockSpec((1, length, width), lambda j, c: (jnp.minimum(j, n - 1) // second, 0, 0)),
                pl.BlockSpec((1, length, width), lambda j, c: (jnp.minimum(j, n - 1), 0, 0)),
            ],
            out_specs=[block, block, pl.BlockSpec((4, width), lambda j, c: (0, 0))],
        ),
        out_shape=[out, out, jax.ShapeDtypeStruct((4, width), f32)],
        cost_estimate=COVER,
        compiler_params=pltpu.CompilerParams(vmem_limit_bytes=18 * MIB),
        name="column_grad",
    )(core, sums, up_sum, mods, timing, *streamed(a, b))


def shift_permute(value, axis, by):
    n = lax.axis_size(axis)
    return lax.ppermute(value, axis, [(i, (i + by) % n) for i in range(n)])


def pair_permute(value, bit, axis="dp"):
    n = lax.axis_size(axis)
    return lax.ppermute(value, axis, [(i, i ^ bit) for i in range(n)])


def pick(values, index, axis=0):
    return lax.dynamic_index_in_dim(values, index, axis, keepdims=False)


def after(values, *others):
    return lax.optimization_barrier((values, others))[0]


def bit_of(index, bit):
    return (index // bit) % 2


def add(a, b):
    return (a.astype(f32) + b.astype(f32)).astype(bf16)


CORE, FIRST, SECOND = 1, 2, 4


def first_halves_kernel(at_ref, row_keep, row_got, col_keep, col_got, *outs):
    columns = outs[0].shape[2]
    start = 0
    for keep, got in ((row_keep, row_got), (col_keep, col_got)):
        total = add(keep[0], got[0])
        n = total.shape[0] // 2
        low, high = total[:n], total[n:]
        for side in range(2):
            cols = slice(side * columns, (side + 1) * columns)
            mine = at_ref[side] == 0
            outs[2 * side][0, start : start + n] = jnp.where(mine, high, low)[:, cols]
            outs[2 * side + 1][0, start : start + n] = jnp.where(mine, low, high)[:, cols]
        start += n


def first_halves(at, row_keep, row_got, col_keep, col_got):
    sp, rows, width = row_keep.shape
    cols = col_keep.shape[1]

    def spec(a):
        return pl.BlockSpec((1,) + a.shape[1:], lambda s, t: (s, 0, 0))

    out = pltpu.HBM((sp, (rows + cols) // 2, width // 2), bf16)
    return pl.pallas_call(
        first_halves_kernel,
        grid_spec=pltpu.PrefetchScalarGridSpec(
            num_scalar_prefetch=1,
            grid=(sp,),
            in_specs=[spec(a) for a in (row_keep, row_got, col_keep, col_got)],
            out_specs=[spec(out)] * 4,
        ),
        out_shape=[out] * 4,
        cost_estimate=COVER,
        compiler_params=pltpu.CompilerParams(vmem_limit_bytes=12 * MIB),
        name="first_halves",
    )(at, *streamed(row_keep, row_got, col_keep, col_got))


def second_halves_kernel(at_ref, *refs):
    for side in range(2):
        mine = at_ref[1 - side]
        keep, got = refs[2 * side : 2 * side + 2]
        for s in range(keep.shape[0]):
            refs[4 + 2 * side][s] = add(keep[s, 1 - mine], got[s, 1 - mine])
            refs[5 + 2 * side][s] = add(keep[s, mine], got[s, mine])


def second_halves(at, *arrays):
    sp, rows, columns = arrays[0].shape
    out = jax.ShapeDtypeStruct((sp, rows // 2, columns), bf16)
    return pl.pallas_call(
        second_halves_kernel,
        in_specs=[SMEM] + [VMEM] * 4,
        out_specs=[VMEM] * 4,
        out_shape=[out] * 4,
        cost_estimate=COVER,
        compiler_params=pltpu.CompilerParams(vmem_limit_bytes=10 * MIB),
        name="second_halves",
    )(at, *streamed(*[a.reshape(sp, 2, rows // 2, columns) for a in arrays]))


def near_halves_kernel(at_ref, *refs, terms, sides):
    ins, outs = refs[:-2], refs[-2:]
    mine = lax.rem(at_ref[2], 2)
    for out, bit in zip(outs, (1 - mine, mine)):
        for s in range(out.shape[0]):
            at = 0
            for side in range(sides):
                total = None
                for ref in ins[side * terms : (side + 1) * terms]:
                    value = ref[2 * s + bit].astype(f32)
                    total = value if total is None else total + value
                out[s, :, at : at + total.shape[1]] = total.astype(bf16)
                at += total.shape[1]


def near_halves(at, sides):
    terms = len(sides[0])
    flat = [a for side in sides for a in side]
    sp, rows, _ = flat[0].shape
    width = sum(side[0].shape[2] for side in sides)
    out = jax.ShapeDtypeStruct((sp // 2, rows, width), bf16)
    return pl.pallas_call(
        functools.partial(near_halves_kernel, terms=terms, sides=len(sides)),
        in_specs=[SMEM] + [VMEM] * len(flat),
        out_specs=[VMEM] * 2,
        out_shape=[out] * 2,
        cost_estimate=COVER,
        compiler_params=pltpu.CompilerParams(vmem_limit_bytes=8 * MIB),
        name="near_halves",
    )(at, *on_chip(flat))


def far_halves_kernel(at_ref, keep, got, send_ref, keep_ref):
    mine = lax.div(at_ref[2], 2)
    send_ref[...] = add(keep[1 - mine], got[1 - mine])
    keep_ref[...] = add(keep[mine], got[mine])


def far_halves(at, keep, got):
    out = jax.ShapeDtypeStruct(keep.shape[1:], bf16)
    return pl.pallas_call(
        far_halves_kernel,
        in_specs=[SMEM] + [VMEM] * 2,
        out_specs=[VMEM] * 2,
        out_shape=[out] * 2,
        cost_estimate=COVER,
        name="far_halves",
    )(at, keep, got)


def hand_over_kernel(in_ref, out_ref):
    out_ref[...] = in_ref[...].astype(out_ref.dtype)


def widen(value):
    return hand_over(value, f32)


def hand_over(value, dtype=bf16):
    block = pl.BlockSpec((1,) + value.shape[1:], lambda i: (i, 0, 0))
    return pl.pallas_call(
        hand_over_kernel,
        grid=(value.shape[0],),
        in_specs=[block],
        out_specs=block,
        out_shape=jax.ShapeDtypeStruct(value.shape, dtype),
        cost_estimate=COVER,
        compiler_params=pltpu.CompilerParams(vmem_limit_bytes=6 * MIB),
        name="hand_over",
    )(value)


def own_kernel(keep_ref, got_ref, out_ref):
    out_ref[...] = add(keep_ref[...], got_ref[...])


def own_sum(keep, got):
    return pl.pallas_call(
        own_kernel,
        in_specs=[VMEM] * 2,
        out_specs=VMEM,
        out_shape=jax.ShapeDtypeStruct(keep.shape, bf16),
        cost_estimate=COVER,
        name="own_sum",
    )(keep, got)


def quarters_kernel(at_ref, keep_ref, got_ref, *outs):
    for i, out in enumerate(outs):
        index = 2 * (at_ref[0] ^ (i // 2)) + (at_ref[1] ^ (i % 2))
        for s in range(keep_ref.shape[0]):
            out[s] = add(keep_ref[s, index], got_ref[s, index])


def quarters(at, keep, got):
    sp, rows, width = keep.shape
    out = jax.ShapeDtypeStruct((sp, rows // 4, width), bf16)
    return pl.pallas_call(
        quarters_kernel,
        in_specs=[SMEM] + [VMEM] * 2,
        out_specs=[VMEM] * 4,
        out_shape=[out] * 4,
        cost_estimate=COVER,
        compiler_params=pltpu.CompilerParams(vmem_limit_bytes=10 * MIB),
        name="quarters",
    )(at, *on_chip([a.reshape(sp, 4, rows // 4, width) for a in (keep, got)]))


def four_chips_kernel(at_ref, *refs, crossed):
    pieces, out_ref = refs[:4], refs[4]
    columns = out_ref.shape[2] // 2
    for i, piece in enumerate(pieces):
        x, y = at_ref[0] ^ (i // 2), at_ref[1] ^ (i % 2)
        out_ref[2 * x + y, :, :columns] = piece[:, :columns]
        out_ref[2 * y + x if crossed else 2 * x + y, :, columns:] = piece[:, columns:]


def four_chips(at, pieces, crossed):
    rows, width = pieces[0].shape
    return pl.pallas_call(
        functools.partial(four_chips_kernel, crossed=crossed),
        in_specs=[SMEM] + [VMEM] * 4,
        out_specs=VMEM,
        out_shape=jax.ShapeDtypeStruct((4, rows, width), bf16),
        cost_estimate=COVER,
        compiler_params=pltpu.CompilerParams(vmem_limit_bytes=8 * MIB),
        name="four_chips",
    )(at, *on_chip(pieces)).reshape(4 * rows, width)


def spread(own):
    return [own] + [pair_permute(own, bit) for bit in (SECOND, FIRST, FIRST + SECOND)]


def finish_kernel(core_ref, mine_ref, other_ref, *outs, half, layout):
    first = core_ref[0] == 0
    width = mine_ref.shape[1]
    for out, (_, across, starts) in zip(outs, layout):
        for n, at in enumerate(starts):
            cols = slice(n % across * width, (n % across + 1) * width)
            mine = mine_ref[at : at + half].astype(f32)
            other = other_ref[at : at + half].astype(f32)
            to = n // across * 2 * half
            out[to : to + half, cols] = jnp.where(first, mine, other)
            out[to + half : to + 2 * half, cols] = jnp.where(first, other, mine)


def finish(core, mine, other, half, layout):
    width = mine.shape[1]
    shapes = [(2 * half * down, width * across) for down, across, _ in layout]
    return pl.pallas_call(
        functools.partial(finish_kernel, half=half, layout=layout),
        grid=(1,),
        in_specs=[SMEM] + [VMEM] * 2,
        out_specs=[pl.BlockSpec(s, lambda i: (0, 0)) for s in shapes],
        out_shape=[jax.ShapeDtypeStruct(s, f32) for s in shapes],
        cost_estimate=COVER,
        compiler_params=pltpu.CompilerParams(vmem_limit_bytes=16 * MIB),
        name="finish",
    )(core, *on_chip([mine, other]))


def late_finish_kernel(
    core_ref, mine_ref, other_ref, early_ref, qkv_ref, ada_ref, bias_ref, attn_gain_ref, mlp_gain_ref, up_ref,
    down_ref, *, half,
):
    core_first = core_ref[0] == 0
    width = mine_ref.shape[1]
    for n in range(3):
        cols = slice(n * width, (n + 1) * width)
        mine = mine_ref[n * half : (n + 1) * half].astype(f32)
        other = other_ref[n * half : (n + 1) * half].astype(f32)
        qkv_ref[:half, cols] = jnp.where(core_first, mine, other)
        qkv_ref[half:, cols] = jnp.where(core_first, other, mine)
    mine, other = mine_ref[3 * half :].astype(f32), other_ref[3 * half :].astype(f32)
    late = (jnp.where(core_first, mine, other), jnp.where(core_first, other, mine))
    count = ada_ref.shape[0]
    quarter, own = attn_gain_ref.shape[1], bias_ref.size
    for p in range(2):
        ada_ref[:, p * width : (p + 1) * width] = late[p][:count]
    for p in range(4):
        start = p // 2 * half + p % 2 * count
        ada_ref[:, (2 + p) * width : (3 + p) * width] = early_ref[start : start + count, :]
    row, rest = 2 * count, own - width
    sums = (late[0][count : count + 1], late[1][count : count + 1])
    for lane in range(0, own, LANES):
        i, side = lane // LANES, lane // width
        cols = slice(lane % width, lane % width + LANES)
        at = side * half + row + 1
        bias_ref[i : i + 1, :] = early_ref[at : at + 1, cols] + sums[side][:, cols]
    for lane in range(0, width, LANES):
        i = lane // LANES
        up_ref[i : i + 1, :] = early_ref[row : row + 1, lane : lane + LANES]
    attn_gain_ref[...] = sums[1][:, rest : rest + quarter]
    mlp_gain_ref[...] = early_ref[half + row : half + row + 1, :quarter]
    down_ref[...] = early_ref[half + row : half + row + 1, quarter : 2 * quarter]


def late_finish(core, mine, other, early, half, cond, sp):
    width = early.shape[1]
    one = (1, width // sp)
    shapes = [
        (2 * half, 3 * width), (cond // sp, 6 * width), (6 * width // sp // LANES, LANES),
        one, one, (width // LANES, LANES), one,
    ]
    return pl.pallas_call(
        functools.partial(late_finish_kernel, half=half),
        grid=(1,),
        in_specs=[SMEM] + [VMEM] * 3,
        out_specs=[pl.BlockSpec(s, lambda i: (0, 0)) for s in shapes],
        out_shape=[jax.ShapeDtypeStruct(s, f32) for s in shapes],
        cost_estimate=COVER,
        compiler_params=pltpu.CompilerParams(vmem_limit_bytes=12 * MIB),
        name="late_finish",
    )(core, *on_chip([mine, other, early]))


def sum_over_rest(total):
    bit = 2 * SECOND
    while bit < lax.axis_size("dp"):
        total = add(total, pair_permute(total, bit))
        bit *= 2
    return total


def double(rows, bit, axis):
    return jnp.concatenate([rows, pair_permute(rows, bit, axis)], axis=0)


def bits(axis):
    n, bit = lax.axis_size(axis), 1
    while bit < n:
        yield bit
        bit *= 2


def body(
    hidden_in,
    time_embed,
    ada_weight,
    ada_bias,
    attn_gain,
    query_key_value_matrix,
    attention_output_matrix,
    mlp_gain,
    up_projection_matrix,
    up_bias,
    down_projection_matrix,
    down_bias,
    out_cotangent,
):
    sequences, local_len, width = hidden_in.shape
    sp, me = lax.axis_size("sp"), lax.axis_index("sp")
    assert sequences == sp
    def exchange(values):
        values = values.reshape(sp, local_len, width)
        return lax.all_to_all(values, "sp", split_axis=0, concat_axis=0, tiled=True)

    x = exchange(hidden_in).reshape(-1, width)
    cot = exchange(after(out_cotangent, x)).reshape(-1, width)
    here = lax.axis_index("dp")
    core = bit_of(here, CORE).reshape(1)
    at = jnp.stack([bit_of(here, FIRST), bit_of(here, SECOND), me])

    timing = lax.dynamic_slice_in_dim(time_embed, me, 1, 0)
    modulation = dot_nn(timing, ada_weight) + ada_bias.astype(f32)[None]
    shift_attn, scale_attn, gate_attn, shift_mlp, scale_mlp, gate_mlp = jnp.split(
        modulation, 6, axis=-1
    )
    gain_attn = attn_gain.astype(f32)[None]
    gain_mlp = mlp_gain.astype(f32)[None]
    zero = jnp.zeros_like(shift_attn)
    attn_mods = jnp.concatenate(
        [gain_attn * (1.0 + scale_attn), shift_attn] + [zero] * 6, axis=0
    )
    mlp_mods = jnp.concatenate(
        [gate_attn, gain_mlp * (1.0 + scale_mlp), shift_mlp, gate_mlp, down_bias.astype(f32)[None]]
        + [zero] * 3,
        axis=0,
    )
    late_mods = jnp.concatenate([gain_attn, 1.0 + scale_attn] + [zero] * 6, axis=0)
    mlp_grad_mods = jnp.concatenate([gain_mlp, 1.0 + scale_mlp] + [zero] * 6, axis=0)
    column = timing.astype(f32).reshape(timing.shape[1], 1)
    attn_mods, mlp_mods, late_mods, mlp_grad_mods, column, at, core = lax.optimization_barrier(
        (attn_mods, mlp_mods, late_mods, mlp_grad_mods, column, at, core)
    )
    lane = lax.broadcasted_iota(jnp.int32, (1, LANES), 1)
    frequency = 10000.0 ** (-((lane % HALF).astype(f32) * 2.0 / HEAD_DIM))
    row = lax.broadcasted_iota(jnp.int32, (sp * local_len, 1), 0)
    angles = row.astype(f32) * frequency
    cos, sin = jnp.cos(angles), jnp.sin(angles)

    xm_attn, q, k, v = project_qkv(x, attn_mods, query_key_value_matrix, cos, sin)
    mixed, lse = attention_forward(q, k, v)
    both_in, act, gd, both_grad, gm, gmix, sums, up_sum, out = feed_forward(
        x,
        mixed,
        cot,
        mlp_mods,
        up_bias.astype(f32)[None],
        attention_output_matrix,
        up_projection_matrix,
        down_projection_matrix,
        local_len,
    )
    ff = up_bias.shape[0]
    assert ff == sp * width
    n_up = ff // width
    half = width // sp // 2
    quarter = width // sp
    cond = timing.shape[1]
    output = exchange(out)
    col_send, col_keep, early_parts = column_grad(
        core, sums, up_sum, mlp_grad_mods, column, both_in, both_grad, sp, n_up
    )
    col_got = pair_permute(col_send, CORE)
    row_send, row_keep = row_grad(core, *after((act, gd), col_keep), sp)
    row_got = pair_permute(row_send, CORE)

    left_send, left, right_send, right = first_halves(at, row_keep, row_got, col_keep, col_got)
    left_got, right_got = pair_permute(left_send, FIRST), pair_permute(right_send, SECOND)
    gmix = after(gmix, left, right)
    grads, hg, attn_sums = attention_backward(
        q, k, v, gmix, mixed, lse, cos, sin, x, gm, attn_mods, query_key_value_matrix, local_len
    )
    left_got, right_got, output = after((left_got, right_got, output), grads)
    left_send, left, right_send, right = second_halves(at, left, left_got, right, right_got)
    left_got, right_got = pair_permute(left_send, SECOND), pair_permute(right_send, FIRST)
    grads = after(grads, left, right, output)

    time_row, late_send, late_keep = late_grads(
        core, grads, xm_attn, attn_sums, late_mods, ada_weight, column, early_parts, sp
    )
    hidden_grad = exchange(hg)
    late_got = pair_permute(late_send, CORE)
    left_got, right_got = after((left_got, right_got), late_keep)
    if lax.axis_size("dp") > 2 * SECOND:
        left, right = sum_over_rest(add(left, left_got)), sum_over_rest(add(right, right_got))
        sides = [(left,), (right,)]
    else:
        sides = [(left, left_got), (right, right_got)]
    near_send, near = near_halves(at, sides)
    near_got = pair_permute(near_send, 1, "sp")
    late_got = after(late_got, near)
    own_quarter, *other_quarters = quarters(at, late_keep, late_got)
    quarter_parts = [own_quarter] + [
        pair_permute(p, bit)
        for p, bit in zip(other_quarters, (SECOND, FIRST, FIRST + SECOND))
    ]
    output = hand_over(after(output, own_quarter))
    near_got, hidden_grad = after((near_got, hidden_grad), output)
    near_got = after(near_got, hidden_grad)
    upper = me // 2
    far_send = add(pick(near, 1 - upper), pick(near_got, 1 - upper))
    far = add(pick(near, upper), pick(near_got, upper))
    far_got = pair_permute(far_send, 2, "sp")
    quarter_parts = after(quarter_parts, far, far_send)
    if lax.axis_size("dp") > 2 * SECOND:
        total = sum(p.astype(f32) for p in quarter_parts).astype(bf16)
        quarter_parts = [sum_over_rest(total)]
    late_near_send, late_near = near_halves(at, [quarter_parts])
    late_near_got = pair_permute(late_near_send, 1, "sp")
    early_own = add(far, after(far_got, late_near))
    early_four = spread(early_own)
    late_near_got = after(late_near_got, early_own)
    late_far_send = add(pick(late_near, 1 - upper), pick(late_near_got, 1 - upper))
    late_far = add(pick(late_near, upper), pick(late_near_got, upper))
    late_far_got = pair_permute(late_far_send, 2, "sp")
    late_own = add(late_far, late_far_got)
    hidden_grad = after(hidden_grad, late_own).astype(f32)
    time_rows = after(time_row, late_own)
    for bit in bits("sp"):
        time_rows = double(time_rows, bit, "sp")
    time_grad = jnp.concatenate([pick(time_rows, me ^ s)[None] for s in range(sp)], axis=0)
    time_grad = time_grad.astype(f32)
    early_half = four_chips(at, after(early_four, late_own, time_rows, hidden_grad), True)
    early_other = pair_permute(early_half, CORE)
    late_four = spread(after(late_own, early_half))
    n_row, n_col = row_keep.shape[1] // 2, col_keep.shape[1] // 2
    row_starts = [x * (n_row + n_col) + i for x in range(2) for i in range(0, n_row, half)]
    col_starts = [x * (n_row + n_col) + n_row + i for x in range(2) for i in range(0, n_col, half)]
    down_grad, up_grad, proj_grad, early_vectors = finish(
        core,
        early_half,
        after(early_other, late_four[0]),
        half,
        (
            (sp, 1, row_starts),
            (1, n_up, col_starts[:n_up]),
            (1, 1, col_starts[n_up : n_up + 1]),
            (1, 1, col_starts[n_up + 1 :]),
        ),
    )
    late_half = four_chips(at, after(late_four, down_grad), False)
    late_other = pair_permute(late_half, CORE)
    qkv_grad, ada_weight_grad, *small = late_finish(
        core, late_half, late_other, early_vectors, half, cond, sp
    )
    ada_bias_grad, attn_gain_grad, mlp_gain_grad, up_bias_grad, down_bias_grad = (
        v.reshape(-1) for v in small
    )
    return (
        output,
        hidden_grad,
        time_grad,
        ada_weight_grad,
        ada_bias_grad,
        attn_gain_grad,
        qkv_grad,
        proj_grad,
        mlp_gain_grad,
        up_grad,
        up_bias_grad,
        down_grad,
        down_bias_grad,
    )


def solution(mesh):
    return jax.shard_map(
        body,
        mesh=mesh,
        in_specs=(P("dp", "sp", None), P("dp", None)) + (P(),) * 10 + (P("dp", "sp", None),),
        out_specs=(
            P("dp", "sp", None),
            P("dp", "sp", None),
            P("dp", None),
            P("sp", None),
            P("sp"),
            P("sp"),
            P("sp", None),
            P("sp", None),
            P("sp"),
            P("sp", None),
            P("sp"),
            P("sp", None),
            P("sp"),
        ),
        check_vma=False,
    )
```

```python
import functools

import jax
import jax.numpy as jnp
from jax import lax
from jax.experimental import pallas as pl
from jax.experimental.pallas import tpu as pltpu
from jax.sharding import PartitionSpec as P

HEAD_DIM = 64
MIB = 1 << 20
VMEM = pl.BlockSpec(memory_space=pltpu.VMEM)
SMEM = pl.BlockSpec(memory_space=pltpu.SMEM)
HALF = HEAD_DIM // 2
LANES = 128
EPSILON = 1e-05
LOG2E = 1.4426950408889634
SCALE = HEAD_DIM ** (-0.5)
f32 = jnp.float32
COVER = pl.CostEstimate(flops=40_000_000_000, bytes_accessed=100_000_000, transcendentals=0)
bf16 = jnp.bfloat16


def on_chip(arrays):
    return [pltpu.with_memory_space_constraint(a, pltpu.VMEM) for a in arrays]


def streamed(*arrays):
    return [pltpu.with_memory_space_constraint(a, pltpu.HBM) for a in arrays]


def dot_nn(a, b):
    return lax.dot_general(a, b, (((1,), (0,)), ((), ())), preferred_element_type=f32)


def dot_nt(a, b):
    return lax.dot_general(a, b, (((1,), (1,)), ((), ())), preferred_element_type=f32)


def dot_tn(a, b):
    return lax.dot_general(a, b, (((0,), (0,)), ((), ())), preferred_element_type=f32)


def column_sum(values):
    return jnp.sum(values, axis=0, keepdims=True)


def norm_forward(values):
    center = values - jnp.mean(values, axis=-1, keepdims=True)
    inverse = lax.rsqrt(jnp.mean(center * center, axis=-1, keepdims=True) + EPSILON)
    return center * inverse, inverse


def norm_backward(grad, normed, inverse):
    first = jnp.mean(grad, axis=-1, keepdims=True)
    second = jnp.mean(grad * normed, axis=-1, keepdims=True)
    return inverse * (grad - first - normed * second)


def swap_halves(values):
    lane = lax.broadcasted_iota(jnp.int32, (1, LANES), 1)
    lower = (lane & (HEAD_DIM - 1)) < HALF
    up = pltpu.roll(values, LANES - HALF, 1)
    down = pltpu.roll(values, HALF, 1)
    return lower, up, down


def rotary(values, cos, sin):
    lower, up, down = swap_halves(values)
    return values * cos + jnp.where(lower, -up, down) * sin


def unrotary(values, cos, sin):
    lower, up, down = swap_halves(values * sin)
    return values * cos + jnp.where(lower, up, -down)


def qkv_kernel(x_ref, mod_ref, w_ref, cos_ref, sin_ref, xm_ref, q_ref, k_ref, v_ref):
    width = x_ref.shape[1]
    normed, _ = norm_forward(x_ref[...].astype(f32))
    xm = (normed * mod_ref[0:1, :] + mod_ref[1:2, :]).astype(bf16)
    xm_ref[...] = xm
    cos, sin = cos_ref[...], sin_ref[...]
    for part, ref in enumerate((q_ref, k_ref, v_ref)):
        whole = dot_nn(xm, w_ref[:, part * width : (part + 1) * width]).astype(bf16)
        if part == 2:
            ref[...] = whole
            continue
        for lane in range(0, width, LANES):
            piece = whole[:, lane : lane + LANES].astype(f32)
            ref[:, lane : lane + LANES] = rotary(piece, cos, sin).astype(bf16)


def project_qkv(x, mods, weight, cos, sin, rows=256):
    length, width = x.shape
    block = pl.BlockSpec((rows, width), lambda i: (i, 0))
    table = pl.BlockSpec((rows, LANES), lambda i: (i, 0))
    shape = pltpu.HBM((length, width), bf16)
    return pl.pallas_call(
        qkv_kernel,
        grid=(length // rows,),
        in_specs=[
            block,
            VMEM,
            pl.BlockSpec(weight.shape, lambda i: (0, 0)),
            table,
            table,
        ],
        out_specs=[block] * 4,
        out_shape=[shape] * 4,
        cost_estimate=COVER,
        compiler_params=pltpu.CompilerParams(vmem_limit_bytes=18 * MIB),
        name="project_qkv",
    )(x, mods, *streamed(weight, cos, sin))


def attention_forward_kernel(q_ref, k_ref, v_ref, o_ref, lse_ref, *, chunk, ahead):
    k, v = k_ref[...], v_ref[...]
    first = lax.broadcasted_iota(jnp.int32, (1, LANES), 1) < HEAD_DIM
    c = LOG2E * SCALE
    masks = (first, ~first)
    keys = [jnp.where(m, k, jnp.zeros_like(k)) for m in masks]
    values = [jnp.where(m, v, jnp.ones_like(v)) for m in masks]
    items = [(h, start) for start in range(0, q_ref.shape[0], chunk) for h in range(2)]

    def scores(h, start):
        return dot_nt(keys[h], q_ref[start : start + chunk, :])

    waiting = [scores(*item) for item in items[:ahead]]
    outs = {}
    for i, (h, start) in enumerate(items):
        st = waiting.pop(0)
        if i + ahead < len(items):
            waiting.append(scores(*items[i + ahead]))
        rows = slice(start, start + chunk)
        top = jnp.max(st, axis=0, keepdims=True) * c
        p = jnp.exp2(st * c - top).astype(bf16)
        ot = dot_tn(values[h], p)
        own, ones = (ot[:HEAD_DIM], ot[HEAD_DIM:]) if h == 0 else (ot[HEAD_DIM:], ot[:HEAD_DIM])
        total = ones[0:1]
        outs[h] = own * (1.0 / total)
        lse_ref[0, h : h + 1, rows] = top + jnp.log2(total)
        if h == 1:
            o_ref[rows, :] = jnp.concatenate([outs[0], outs[1]], axis=0).T.astype(bf16)


def attention_forward(q, k, v):
    length, width = q.shape
    pairs = width // LANES
    block = pl.BlockSpec((length, LANES), lambda i: (0, i))
    return pl.pallas_call(
        functools.partial(attention_forward_kernel, chunk=length // 2, ahead=2),
        grid=(pairs,),
        in_specs=[block] * 3,
        out_specs=[block, pl.BlockSpec((1, 2, length), lambda i: (i, 0, 0))],
        out_shape=[
            pltpu.HBM((length, width), bf16),
            pltpu.HBM((pairs, 2, length), f32),
        ],
        cost_estimate=COVER,
        compiler_params=pltpu.CompilerParams(vmem_limit_bytes=14 * MIB),
        name="attention_forward",
    )(*streamed(q, k, v))


def attention_backward_kernel(
    q_ref, k_ref, v_ref, do_ref, o_ref, lse_ref, cos_ref, sin_ref, x_ref, gm_ref, mod_ref, w_ref,
    g_ref, hg_ref, sum_ref, held_ref, *, pairs,
):
    step = pl.program_id(0)
    width = x_ref.shape[1]

    @pl.when(step < pairs)
    def _():
        first = lax.broadcasted_iota(jnp.int32, (1, LANES), 1) < HEAD_DIM
        upper = lax.broadcasted_iota(jnp.int32, (LANES, 1), 0) < HEAD_DIM
        c = LOG2E * SCALE
        q, k, v, do = q_ref[...], k_ref[...], v_ref[...], do_ref[...]
        prod = (do.astype(f32) * o_ref[...].astype(f32)).T
        kt = k.T
        zero = jnp.zeros_like(k)
        dq = dk = dv = None
        for h in range(2):
            mine = first if h == 0 else ~first
            row = column_sum(prod[h * HEAD_DIM : (h + 1) * HEAD_DIM])
            st = dot_nt(jnp.where(mine, k, zero), q)
            p = jnp.exp2(st * c - lse_ref[0, h : h + 1, :])
            dp = dot_nt(jnp.where(mine, v, zero), do)
            ds = (p * (dp - row)).astype(bf16)
            dvh = dot_nn(p.astype(bf16), jnp.where(mine, do, zero))
            dkh = dot_nn(ds, jnp.where(mine, q, zero))
            dqh = dot_nn(jnp.where(upper if h == 0 else ~upper, kt, jnp.zeros_like(kt)), ds)
            dq, dk, dv = (dqh, dkh, dvh) if h == 0 else (dq + dqh, dk + dkh, dv + dvh)
        cos, sin = cos_ref[...], sin_ref[...]
        lanes = pl.ds(pl.multiple_of(step * LANES, LANES), LANES)
        for part, value in enumerate(
            (unrotary(dq.T * SCALE, cos, sin), unrotary(dk * SCALE, cos, sin), dv)
        ):
            value = value.astype(bf16)
            g_ref[part] = value
            held_ref[part, :, lanes] = value

    @pl.when(step >= pairs)
    def _():
        rows = x_ref.shape[0]
        tile = pl.ds(pl.multiple_of((step - pairs) * rows, rows), rows)
        normed, inverse = norm_forward(x_ref[...].astype(f32))
        grad = None
        for part in range(3):
            g = dot_nt(held_ref[part, tile, :], w_ref[:, part * width : (part + 1) * width])
            grad = g if grad is None else grad + g
        hg = gm_ref[...] + norm_backward(grad * mod_ref[0:1, :], normed, inverse)
        hg_ref[...] = hg.astype(bf16)
        sums = jnp.concatenate(
            [column_sum(grad), column_sum(grad * normed), jnp.zeros((6, width), f32)], axis=0
        )

        @pl.when(step == pairs)
        def _():
            sum_ref[...] = sums

        @pl.when(step > pairs)
        def _():
            sum_ref[...] += sums


def attention_backward(q, k, v, do, o, lse, cos, sin, x, gm, mods, weight, rows):
    length, width = q.shape
    pairs = width // LANES

    def pair(i):
        return jnp.minimum(i, pairs - 1)

    block = pl.BlockSpec((length, LANES), lambda i: (0, pair(i)))
    table = pl.BlockSpec((length, LANES), lambda i: (0, 0))
    tile = pl.BlockSpec((rows, width), lambda i: (jnp.maximum(i - pairs, 0), 0))
    return pl.pallas_call(
        functools.partial(attention_backward_kernel, pairs=pairs),
        grid=(pairs + length // rows,),
        in_specs=[block] * 5
        + [pl.BlockSpec((1, 2, length), lambda i: (pair(i), 0, 0)), table, table, tile, tile, VMEM, VMEM],
        out_specs=[
            pl.BlockSpec((3, length, LANES), lambda i: (0, 0, pair(i))),
            tile,
            pl.BlockSpec((8, width), lambda i: (0, 0)),
        ],
        out_shape=[
            pltpu.HBM((3, length, width), bf16),
            pltpu.HBM((length, width), bf16),
            jax.ShapeDtypeStruct((8, width), f32),
        ],
        scratch_shapes=[pltpu.VMEM((3, length, width), bf16)],
        cost_estimate=COVER,
        compiler_params=pltpu.CompilerParams(vmem_limit_bytes=34 * MIB),
        name="attention_backward",
    )(q, k, v, do, o, lse, cos, sin, x, gm, mods, weight)


def mlp_kernel(
    x_ref, mixed_ref, cot_ref, mod_ref, bias_ref, wo_ref, wu_ref, wd_ref,
    xm_ref, act_ref, gd_ref, gp_ref, gm_ref, gmix_ref, sum_ref, up_sum_ref, out_ref,
):
    chunk, ff = wu_ref.shape
    gate_attn, scaled, shift = mod_ref[0:1, :], mod_ref[1:2, :], mod_ref[2:3, :]
    gate_mlp, down_bias = mod_ref[3:4, :], mod_ref[4:5, :]
    cot = cot_ref[...].astype(f32)
    projected = dot_nn(mixed_ref[...], wo_ref[...])
    middle = x_ref[...].astype(f32) + gate_attn * projected
    normed, inverse = norm_forward(middle)
    xm = (normed * scaled + shift).astype(bf16)
    xm_ref[0] = xm
    xm_ref[1] = mixed_ref[...]
    gd = (gate_mlp * cot).astype(bf16)
    gd_ref[...] = gd
    down = grad_mod = None
    c0 = 0.7978845608028654
    c1 = c0 * 0.044715
    up_sums = []
    for at in range(0, ff, chunk):
        cols = slice(at, at + chunk)
        pre = dot_nn(xm, wu_ref[:, cols]) + bias_ref[:, cols]
        square = pre * pre
        t = jnp.tanh(pre * (c0 + c1 * square))
        half = 0.5 + 0.5 * t
        wide_act = pre * half
        act = wide_act.astype(bf16)
        act_ref[:, cols] = act
        slope = half + wide_act * (1.0 - half) * (2.0 * c0 + (6.0 * c1) * square)
        wide_gp = slope * dot_nt(gd, wd_ref[cols, :])
        gp = wide_gp.astype(bf16)
        gp_ref[at // chunk] = gp
        up_sums.append(column_sum(wide_gp))
        d = dot_nn(act, wd_ref[cols, :])
        g = dot_nt(gp, wu_ref[:, cols])
        down, grad_mod = (d, g) if down is None else (down + d, grad_mod + g)
    down = down + down_bias
    out_ref[...] = (middle + gate_mlp * down).astype(bf16)
    gm = cot + norm_backward(grad_mod * scaled, normed, inverse)
    gm_ref[...] = gm
    gpj = (gate_attn * gm).astype(bf16)
    gp_ref[ff // chunk] = gpj
    gmix_ref[...] = dot_nt(gpj, wo_ref[...]).astype(bf16)
    sums = jnp.concatenate(
        [
            column_sum(cot * down),
            column_sum(gd.astype(f32)),
            column_sum(grad_mod),
            column_sum(grad_mod * normed),
            column_sum(gm * projected),
            jnp.zeros((3, cot.shape[1]), f32),
        ],
        axis=0,
    )
    up_sum = jnp.concatenate(up_sums, axis=1)

    @pl.when(pl.program_id(0) == 0)
    def _():
        sum_ref[...] = sums
        up_sum_ref[...] = up_sum

    @pl.when(pl.program_id(0) > 0)
    def _():
        sum_ref[...] += sums
        up_sum_ref[...] += up_sum


def feed_forward(x, mixed, cot, mods, up_bias, wo, wu, wd, rows):
    length, width = x.shape
    ff = wu.shape[1]
    block = pl.BlockSpec((rows, width), lambda i: (i, 0))
    wide = pl.BlockSpec((rows, ff), lambda i: (i, 0))

    narrow = pltpu.HBM((length, width), bf16)
    broad = pltpu.HBM((length, ff), bf16)
    return pl.pallas_call(
        mlp_kernel,
        grid=(length // rows,),
        in_specs=[block, block, block] + [VMEM] * 5,
        out_specs=[
            pl.BlockSpec((2, rows, width), lambda i: (0, i, 0)),
            wide,
            block,
            pl.BlockSpec((ff // width + 1, rows, width), lambda i: (0, i, 0)),
            block,
            block,
            pl.BlockSpec((8, width), lambda i: (0, 0)),
            pl.BlockSpec((1, ff), lambda i: (0, 0)),
        ]
        + [block],
        out_shape=[
            pltpu.HBM((2, length, width), bf16), broad, narrow,
            pltpu.HBM((ff // width + 1, length, width), bf16),
            pltpu.HBM((length, width), f32), narrow,
            jax.ShapeDtypeStruct((8, width), f32), jax.ShapeDtypeStruct((1, ff), f32),
        ]
        + [narrow],
        cost_estimate=COVER,
        compiler_params=pltpu.CompilerParams(vmem_limit_bytes=40 * MIB),
        name="feed_forward",
    )(x, *streamed(mixed, cot), mods, up_bias, wo, *streamed(wu, wd))


def late_grads_kernel(
    core_ref, sum_ref, mod_ref, ada_ref, timing_ref, early_ref, xm_ref, block_ref,
    time_ref, send_ref, keep_ref, *, parts,
):
    step = pl.program_id(0)
    width = block_ref.shape[2]

    @pl.when(step < parts)
    def _():
        product = dot_tn(xm_ref[...], block_ref[0])
        half = send_ref.shape[1]
        for i, (send, keep) in enumerate(split_halves(product, half, core_ref[0] == 0)):
            send_ref[i] = send
            keep_ref[i] = keep

    @pl.when(step == parts)
    def _():
        sp, half, _ = send_ref.shape
        shift, scaled = sum_ref[0:1, :], sum_ref[1:2, :]
        scale = scaled * mod_ref[0:1, :]
        gain = scaled * mod_ref[1:2, :]
        row = jnp.concatenate([shift, scale] + [early_ref[i : i + 1, :] for i in range(4)], axis=1)
        high = row.astype(bf16)
        low = (row - high.astype(f32)).astype(bf16)
        time_ref[...] = (dot_nt(high, ada_ref[...]) + dot_nt(low, ada_ref[...])).astype(bf16)
        bias = jnp.concatenate([shift, scale, jnp.zeros((1, 4 * width), f32)], axis=1)
        count, own, quarter = timing_ref.shape[0] // sp, 6 * width // sp, width // sp
        for ref, first in ((send_ref, core_ref[0] == 1), (keep_ref, core_ref[0] == 0)):
            part = jnp.where(first, shift, scale)
            for i in range(sp):
                ref[i, :count] = (timing_ref[i * count : (i + 1) * count, :] * part).astype(bf16)
                mine = bias[:, i * own : (i + 1) * own]
                rest = jnp.concatenate(
                    [
                        mine[:, width:],
                        gain[:, i * quarter : (i + 1) * quarter],
                        jnp.zeros((1, 2 * width - own - quarter), f32),
                    ],
                    axis=1,
                )
                sums = jnp.concatenate(
                    [jnp.where(first, mine[:, :width], rest), jnp.zeros((half - count - 1, width), f32)], axis=0
                )
                ref[i, count:] = sums.astype(bf16)


def late_grads(core, grads, xm, sums, mods, ada, timing, early, sp):
    n, length, width = grads.shape
    half = width // sp // 2
    out = pl.BlockSpec((sp, half, width), lambda i, c: (0, i, 0))
    shape = jax.ShapeDtypeStruct((sp, (n + 1) * half, width), bf16)
    cond = timing.shape[0]
    return pl.pallas_call(
        functools.partial(late_grads_kernel, parts=n),
        grid_spec=pltpu.PrefetchScalarGridSpec(
            num_scalar_prefetch=1,
            grid=(n + 1,),
            in_specs=[VMEM] * 5
            + [
                pl.BlockSpec((length, width), lambda i, c: (0, 0)),
                pl.BlockSpec((1, length, width), lambda i, c: (jnp.minimum(i, n - 1), 0, 0)),
            ],
            out_specs=[pl.BlockSpec((1, cond), lambda i, c: (0, 0)), out, out],
        ),
        out_shape=[jax.ShapeDtypeStruct((1, cond), bf16), shape, shape],
        cost_estimate=COVER,
        compiler_params=pltpu.CompilerParams(vmem_limit_bytes=18 * MIB),
        name="late_grads",
    )(core, sums, mods, ada, timing, early, xm, grads)


def split_halves(product, half, this_core):
    pieces = []
    for at in range(0, product.shape[0], 2 * half):
        low = product[at : at + half].astype(bf16)
        high = product[at + half : at + 2 * half].astype(bf16)
        pieces.append((jnp.where(this_core, high, low), jnp.where(this_core, low, high)))
    return pieces


def row_grad_kernel(core_ref, a_ref, b_ref, send_ref, keep_ref, *, half):
    product = dot_tn(a_ref[...], b_ref[...])
    for i, (send, keep) in enumerate(split_halves(product, half, core_ref[0] == 0)):
        send_ref[0, i * half : (i + 1) * half] = send
        keep_ref[0, i * half : (i + 1) * half] = keep


def row_grad(core, a, b, sp):
    length, width = b.shape
    out = pltpu.HBM((sp, width // 2, width), bf16)
    block = pl.BlockSpec((1, width // 2, width), lambda j, c: (j, 0, 0))
    return pl.pallas_call(
        functools.partial(row_grad_kernel, half=width // sp // 2),
        grid_spec=pltpu.PrefetchScalarGridSpec(
            num_scalar_prefetch=1,
            grid=(sp,),
            in_specs=[
                pl.BlockSpec((length, width), lambda j, c: (0, j)),
                pl.BlockSpec((length, width), lambda j, c: (0, 0)),
            ],
            out_specs=[block, block],
        ),
        out_shape=[out, out],
        cost_estimate=COVER,
        compiler_params=pltpu.CompilerParams(vmem_limit_bytes=18 * MIB),
        name="row_grad",
    )(core, *streamed(a, b))


def column_grad_kernel(
    core_ref, sum_ref, up_sum_ref, mod_ref, timing_ref, a_ref, b_ref, send_ref, keep_ref, parts_ref, *, blocks
):
    step = pl.program_id(0)
    sp, half, width = send_ref.shape

    @pl.when(step < blocks)
    def _():
        product = dot_tn(a_ref[0], b_ref[0])
        for i, (send, keep) in enumerate(split_halves(product, half, core_ref[0] == 0)):
            send_ref[i] = send
            keep_ref[i] = keep

    @pl.when(step == blocks)
    def _():
        scaled = sum_ref[3:4, :]
        parts = [sum_ref[4:5, :], sum_ref[2:3, :], scaled * mod_ref[0:1, :], sum_ref[0:1, :]]
        for i, part in enumerate(parts):
            parts_ref[i : i + 1, :] = part
        gain = scaled * mod_ref[1:2, :]
        bias = jnp.concatenate([jnp.zeros((1, 2 * width), f32)] + parts, axis=1)
        count, own, quarter = timing_ref.shape[0] // sp, 6 * width // sp, width // sp
        for ref, first in ((send_ref, core_ref[0] == 1), (keep_ref, core_ref[0] == 0)):
            for i in range(sp):
                column = timing_ref[i * count : (i + 1) * count, :]
                for p in range(2):
                    part = jnp.where(first, parts[p], parts[p + 2])
                    ref[i, p * count : (p + 1) * count] = (column * part).astype(bf16)
                shard = slice(i * quarter, (i + 1) * quarter)
                mine = bias[:, i * own : (i + 1) * own]
                gains = jnp.concatenate(
                    [gain[:, shard], sum_ref[1:2, shard], jnp.zeros((1, width - 2 * quarter), f32)], axis=1
                )
                rest = jnp.concatenate([mine[:, width:], jnp.zeros((1, 2 * width - own), f32)], axis=1)
                sums = jnp.concatenate(
                    [
                        jnp.where(first, up_sum_ref[:, i * width : (i + 1) * width], gains),
                        jnp.where(first, mine[:, :width], rest),
                        jnp.zeros((half - 2 * count - 2, width), f32),
                    ],
                    axis=0,
                )
                ref[i, 2 * count :] = sums.astype(bf16)


def column_grad(core, sums, up_sum, mods, timing, a, b, sp, second):
    _, length, width = a.shape
    n = b.shape[0]
    half = width // sp // 2
    out = pltpu.HBM((sp, (n + 1) * half, width), bf16)
    block = pl.BlockSpec((sp, half, width), lambda j, c: (0, j, 0))
    return pl.pallas_call(
        functools.partial(column_grad_kernel, blocks=n),
        grid_spec=pltpu.PrefetchScalarGridSpec(
            num_scalar_prefetch=1,
            grid=(n + 1,),
            in_specs=[VMEM] * 4
            + [
                pl.BlockSpec((1, length, width), lambda j, c: (jnp.minimum(j, n - 1) // second, 0, 0)),
                pl.BlockSpec((1, length, width), lambda j, c: (jnp.minimum(j, n - 1), 0, 0)),
            ],
            out_specs=[block, block, pl.BlockSpec((4, width), lambda j, c: (0, 0))],
        ),
        out_shape=[out, out, jax.ShapeDtypeStruct((4, width), f32)],
        cost_estimate=COVER,
        compiler_params=pltpu.CompilerParams(vmem_limit_bytes=18 * MIB),
        name="column_grad",
    )(core, sums, up_sum, mods, timing, *streamed(a, b))


def shift_permute(value, axis, by):
    n = lax.axis_size(axis)
    return lax.ppermute(value, axis, [(i, (i + by) % n) for i in range(n)])


def pair_permute(value, bit, axis="dp"):
    n = lax.axis_size(axis)
    return lax.ppermute(value, axis, [(i, i ^ bit) for i in range(n)])


def pick(values, index, axis=0):
    return lax.dynamic_index_in_dim(values, index, axis, keepdims=False)


def after(values, *others):
    return lax.optimization_barrier((values, others))[0]


def bit_of(index, bit):
    return (index // bit) % 2


def add(a, b):
    return (a.astype(f32) + b.astype(f32)).astype(bf16)


CORE, FIRST, SECOND = 1, 2, 4


def first_halves_kernel(at_ref, row_keep, row_got, col_keep, col_got, *outs):
    columns = outs[0].shape[2]
    start = 0
    for keep, got in ((row_keep, row_got), (col_keep, col_got)):
        total = add(keep[0], got[0])
        n = total.shape[0] // 2
        low, high = total[:n], total[n:]
        for side in range(2):
            cols = slice(side * columns, (side + 1) * columns)
            mine = at_ref[side] == 0
            outs[2 * side][0, start : start + n] = jnp.where(mine, high, low)[:, cols]
            outs[2 * side + 1][0, start : start + n] = jnp.where(mine, low, high)[:, cols]
        start += n


def first_halves(at, row_keep, row_got, col_keep, col_got):
    sp, rows, width = row_keep.shape
    cols = col_keep.shape[1]

    def spec(a):
        return pl.BlockSpec((1,) + a.shape[1:], lambda s, t: (s, 0, 0))

    out = pltpu.HBM((sp, (rows + cols) // 2, width // 2), bf16)
    return pl.pallas_call(
        first_halves_kernel,
        grid_spec=pltpu.PrefetchScalarGridSpec(
            num_scalar_prefetch=1,
            grid=(sp,),
            in_specs=[spec(a) for a in (row_keep, row_got, col_keep, col_got)],
            out_specs=[spec(out)] * 4,
        ),
        out_shape=[out] * 4,
        cost_estimate=COVER,
        compiler_params=pltpu.CompilerParams(vmem_limit_bytes=12 * MIB),
        name="first_halves",
    )(at, *streamed(row_keep, row_got, col_keep, col_got))


def second_halves_kernel(at_ref, *refs):
    for side in range(2):
        mine = at_ref[1 - side]
        keep, got = refs[2 * side : 2 * side + 2]
        for s in range(keep.shape[0]):
            refs[4 + 2 * side][s] = add(keep[s, 1 - mine], got[s, 1 - mine])
            refs[5 + 2 * side][s] = add(keep[s, mine], got[s, mine])


def second_halves(at, *arrays):
    sp, rows, columns = arrays[0].shape
    out = pltpu.HBM((sp, rows // 2, columns), bf16)
    return pl.pallas_call(
        second_halves_kernel,
        in_specs=[SMEM] + [VMEM] * 4,
        out_specs=[VMEM] * 4,
        out_shape=[out] * 4,
        cost_estimate=COVER,
        compiler_params=pltpu.CompilerParams(vmem_limit_bytes=10 * MIB),
        name="second_halves",
    )(at, *streamed(*[a.reshape(sp, 2, rows // 2, columns) for a in arrays]))


def near_halves_kernel(at_ref, *refs, terms, sides):
    ins, outs = refs[:-2], refs[-2:]
    mine = lax.rem(at_ref[2], 2)
    for out, bit in zip(outs, (1 - mine, mine)):
        for s in range(out.shape[0]):
            at = 0
            for side in range(sides):
                total = None
                for ref in ins[side * terms : (side + 1) * terms]:
                    value = ref[2 * s + bit].astype(f32)
                    total = value if total is None else total + value
                out[s, :, at : at + total.shape[1]] = total.astype(bf16)
                at += total.shape[1]


def near_halves(at, sides):
    terms = len(sides[0])
    flat = [a for side in sides for a in side]
    sp, rows, _ = flat[0].shape
    width = sum(side[0].shape[2] for side in sides)
    out = jax.ShapeDtypeStruct((sp // 2, rows, width), bf16)
    return pl.pallas_call(
        functools.partial(near_halves_kernel, terms=terms, sides=len(sides)),
        in_specs=[SMEM] + [VMEM] * len(flat),
        out_specs=[VMEM] * 2,
        out_shape=[out] * 2,
        cost_estimate=COVER,
        compiler_params=pltpu.CompilerParams(vmem_limit_bytes=8 * MIB),
        name="near_halves",
    )(at, *on_chip(flat))


def far_halves_kernel(at_ref, keep, got, send_ref, keep_ref):
    mine = lax.div(at_ref[2], 2)
    send_ref[...] = add(keep[1 - mine], got[1 - mine])
    keep_ref[...] = add(keep[mine], got[mine])


def far_halves(at, keep, got):
    out = jax.ShapeDtypeStruct(keep.shape[1:], bf16)
    return pl.pallas_call(
        far_halves_kernel,
        in_specs=[SMEM] + [VMEM] * 2,
        out_specs=[VMEM] * 2,
        out_shape=[out] * 2,
        cost_estimate=COVER,
        name="far_halves",
    )(at, keep, got)


def hand_over_kernel(in_ref, out_ref):
    out_ref[...] = in_ref[...].astype(out_ref.dtype)


def widen(value):
    return hand_over(value, f32)


def hand_over(value, dtype=bf16):
    block = pl.BlockSpec((1,) + value.shape[1:], lambda i: (i, 0, 0))
    return pl.pallas_call(
        hand_over_kernel,
        grid=(value.shape[0],),
        in_specs=[block],
        out_specs=block,
        out_shape=jax.ShapeDtypeStruct(value.shape, dtype),
        cost_estimate=COVER,
        compiler_params=pltpu.CompilerParams(vmem_limit_bytes=6 * MIB),
        name="hand_over",
    )(value)


def own_kernel(keep_ref, got_ref, out_ref):
    out_ref[...] = add(keep_ref[...], got_ref[...])


def own_sum(keep, got):
    return pl.pallas_call(
        own_kernel,
        in_specs=[VMEM] * 2,
        out_specs=VMEM,
        out_shape=jax.ShapeDtypeStruct(keep.shape, bf16),
        cost_estimate=COVER,
        name="own_sum",
    )(keep, got)


def quarters_kernel(at_ref, keep_ref, got_ref, *outs):
    for i, out in enumerate(outs):
        index = 2 * (at_ref[0] ^ (i // 2)) + (at_ref[1] ^ (i % 2))
        for s in range(keep_ref.shape[0]):
            out[s] = add(keep_ref[s, index], got_ref[s, index])


def quarters(at, keep, got):
    sp, rows, width = keep.shape
    out = jax.ShapeDtypeStruct((sp, rows // 4, width), bf16)
    return pl.pallas_call(
        quarters_kernel,
        in_specs=[SMEM] + [VMEM] * 2,
        out_specs=[VMEM] * 4,
        out_shape=[out] * 4,
        cost_estimate=COVER,
        compiler_params=pltpu.CompilerParams(vmem_limit_bytes=10 * MIB),
        name="quarters",
    )(at, *on_chip([a.reshape(sp, 4, rows // 4, width) for a in (keep, got)]))


def four_chips_kernel(at_ref, *refs, crossed):
    pieces, out_ref = refs[:4], refs[4]
    columns = out_ref.shape[2] // 2
    for i, piece in enumerate(pieces):
        x, y = at_ref[0] ^ (i // 2), at_ref[1] ^ (i % 2)
        out_ref[2 * x + y, :, :columns] = piece[:, :columns]
        out_ref[2 * y + x if crossed else 2 * x + y, :, columns:] = piece[:, columns:]


def four_chips(at, pieces, crossed):
    rows, width = pieces[0].shape
    return pl.pallas_call(
        functools.partial(four_chips_kernel, crossed=crossed),
        in_specs=[SMEM] + [VMEM] * 4,
        out_specs=VMEM,
        out_shape=jax.ShapeDtypeStruct((4, rows, width), bf16),
        cost_estimate=COVER,
        compiler_params=pltpu.CompilerParams(vmem_limit_bytes=8 * MIB),
        name="four_chips",
    )(at, *on_chip(pieces)).reshape(4 * rows, width)


def spread(own):
    return [own] + [pair_permute(own, bit) for bit in (SECOND, FIRST, FIRST + SECOND)]


def finish_kernel(core_ref, mine_ref, other_ref, *outs, half, layout):
    first = core_ref[0] == 0
    width = mine_ref.shape[1]
    for out, (_, across, starts) in zip(outs, layout):
        for n, at in enumerate(starts):
            cols = slice(n % across * width, (n % across + 1) * width)
            mine = mine_ref[at : at + half].astype(f32)
            other = other_ref[at : at + half].astype(f32)
            to = n // across * 2 * half
            out[to : to + half, cols] = jnp.where(first, mine, other)
            out[to + half : to + 2 * half, cols] = jnp.where(first, other, mine)


def finish(core, mine, other, half, layout):
    width = mine.shape[1]
    shapes = [(2 * half * down, width * across) for down, across, _ in layout]
    return pl.pallas_call(
        functools.partial(finish_kernel, half=half, layout=layout),
        grid=(1,),
        in_specs=[SMEM] + [VMEM] * 2,
        out_specs=[pl.BlockSpec(s, lambda i: (0, 0)) for s in shapes],
        out_shape=[jax.ShapeDtypeStruct(s, f32) for s in shapes],
        cost_estimate=COVER,
        compiler_params=pltpu.CompilerParams(vmem_limit_bytes=16 * MIB),
        name="finish",
    )(core, *on_chip([mine, other]))


def late_finish_kernel(
    core_ref, mine_ref, other_ref, early_ref, qkv_ref, ada_ref, bias_ref, attn_gain_ref, mlp_gain_ref, up_ref,
    down_ref, *, half,
):
    core_first = core_ref[0] == 0
    width = mine_ref.shape[1]
    for n in range(3):
        cols = slice(n * width, (n + 1) * width)
        mine = mine_ref[n * half : (n + 1) * half].astype(f32)
        other = other_ref[n * half : (n + 1) * half].astype(f32)
        qkv_ref[:half, cols] = jnp.where(core_first, mine, other)
        qkv_ref[half:, cols] = jnp.where(core_first, other, mine)
    mine, other = mine_ref[3 * half :].astype(f32), other_ref[3 * half :].astype(f32)
    late = (jnp.where(core_first, mine, other), jnp.where(core_first, other, mine))
    count = ada_ref.shape[0]
    quarter, own = attn_gain_ref.shape[1], bias_ref.size
    for p in range(2):
        ada_ref[:, p * width : (p + 1) * width] = late[p][:count]
    for p in range(4):
        start = p // 2 * half + p % 2 * count
        ada_ref[:, (2 + p) * width : (3 + p) * width] = early_ref[start : start + count, :]
    row, rest = 2 * count, own - width
    sums = (late[0][count : count + 1], late[1][count : count + 1])
    for lane in range(0, own, LANES):
        i, side = lane // LANES, lane // width
        cols = slice(lane % width, lane % width + LANES)
        at = side * half + row + 1
        bias_ref[i : i + 1, :] = early_ref[at : at + 1, cols] + sums[side][:, cols]
    for lane in range(0, width, LANES):
        i = lane // LANES
        up_ref[i : i + 1, :] = early_ref[row : row + 1, lane : lane + LANES]
    attn_gain_ref[...] = sums[1][:, rest : rest + quarter]
    mlp_gain_ref[...] = early_ref[half + row : half + row + 1, :quarter]
    down_ref[...] = early_ref[half + row : half + row + 1, quarter : 2 * quarter]


def late_finish(core, mine, other, early, half, cond, sp):
    width = early.shape[1]
    one = (1, width // sp)
    shapes = [
        (2 * half, 3 * width), (cond // sp, 6 * width), (6 * width // sp // LANES, LANES),
        one, one, (width // LANES, LANES), one,
    ]
    return pl.pallas_call(
        functools.partial(late_finish_kernel, half=half),
        grid=(1,),
        in_specs=[SMEM] + [VMEM] * 3,
        out_specs=[pl.BlockSpec(s, lambda i: (0, 0)) for s in shapes],
        out_shape=[jax.ShapeDtypeStruct(s, f32) for s in shapes],
        cost_estimate=COVER,
        compiler_params=pltpu.CompilerParams(vmem_limit_bytes=12 * MIB),
        name="late_finish",
    )(core, *on_chip([mine, other, early]))


def sum_over_rest(total):
    bit = 2 * SECOND
    while bit < lax.axis_size("dp"):
        total = add(total, pair_permute(total, bit))
        bit *= 2
    return total


def double(rows, bit, axis):
    return jnp.concatenate([rows, pair_permute(rows, bit, axis)], axis=0)


def bits(axis):
    n, bit = lax.axis_size(axis), 1
    while bit < n:
        yield bit
        bit *= 2


def body(
    hidden_in,
    time_embed,
    ada_weight,
    ada_bias,
    attn_gain,
    query_key_value_matrix,
    attention_output_matrix,
    mlp_gain,
    up_projection_matrix,
    up_bias,
    down_projection_matrix,
    down_bias,
    out_cotangent,
):
    sequences, local_len, width = hidden_in.shape
    sp, me = lax.axis_size("sp"), lax.axis_index("sp")
    assert sequences == sp
    def exchange(values):
        values = values.reshape(sp, local_len, width)
        return lax.all_to_all(values, "sp", split_axis=0, concat_axis=0, tiled=True)

    x = exchange(hidden_in).reshape(-1, width)
    cot = exchange(after(out_cotangent, x)).reshape(-1, width)
    here = lax.axis_index("dp")
    core = bit_of(here, CORE).reshape(1)
    at = jnp.stack([bit_of(here, FIRST), bit_of(here, SECOND), me])

    timing = lax.dynamic_slice_in_dim(time_embed, me, 1, 0)
    modulation = dot_nn(timing, ada_weight) + ada_bias.astype(f32)[None]
    shift_attn, scale_attn, gate_attn, shift_mlp, scale_mlp, gate_mlp = jnp.split(
        modulation, 6, axis=-1
    )
    gain_attn = attn_gain.astype(f32)[None]
    gain_mlp = mlp_gain.astype(f32)[None]
    zero = jnp.zeros_like(shift_attn)
    attn_mods = jnp.concatenate(
        [gain_attn * (1.0 + scale_attn), shift_attn] + [zero] * 6, axis=0
    )
    mlp_mods = jnp.concatenate(
        [gate_attn, gain_mlp * (1.0 + scale_mlp), shift_mlp, gate_mlp, down_bias.astype(f32)[None]]
        + [zero] * 3,
        axis=0,
    )
    late_mods = jnp.concatenate([gain_attn, 1.0 + scale_attn] + [zero] * 6, axis=0)
    mlp_grad_mods = jnp.concatenate([gain_mlp, 1.0 + scale_mlp] + [zero] * 6, axis=0)
    column = timing.astype(f32).reshape(timing.shape[1], 1)
    attn_mods, mlp_mods, late_mods, mlp_grad_mods, column, at, core = lax.optimization_barrier(
        (attn_mods, mlp_mods, late_mods, mlp_grad_mods, column, at, core)
    )
    lane = lax.broadcasted_iota(jnp.int32, (1, LANES), 1)
    frequency = 10000.0 ** (-((lane % HALF).astype(f32) * 2.0 / HEAD_DIM))
    row = lax.broadcasted_iota(jnp.int32, (sp * local_len, 1), 0)
    angles = row.astype(f32) * frequency
    cos, sin = jnp.cos(angles), jnp.sin(angles)

    xm_attn, q, k, v = project_qkv(x, attn_mods, query_key_value_matrix, cos, sin)
    mixed, lse = attention_forward(q, k, v)
    both_in, act, gd, both_grad, gm, gmix, sums, up_sum, out = feed_forward(
        x,
        mixed,
        cot,
        mlp_mods,
        up_bias.astype(f32)[None],
        attention_output_matrix,
        up_projection_matrix,
        down_projection_matrix,
        local_len,
    )
    ff = up_bias.shape[0]
    assert ff == sp * width
    n_up = ff // width
    half = width // sp // 2
    quarter = width // sp
    cond = timing.shape[1]
    output = exchange(out)
    col_send, col_keep, early_parts = column_grad(
        core, sums, up_sum, mlp_grad_mods, column, both_in, both_grad, sp, n_up
    )
    col_got = pair_permute(col_send, CORE)
    row_send, row_keep = row_grad(core, *after((act, gd), col_keep), sp)
    row_got = pair_permute(row_send, CORE)

    left_send, left, right_send, right = first_halves(at, row_keep, row_got, col_keep, col_got)
    left_got, right_got = pair_permute(left_send, FIRST), pair_permute(right_send, SECOND)
    gmix = after(gmix, left, right)
    grads, hg, attn_sums = attention_backward(
        q, k, v, gmix, mixed, lse, cos, sin, x, gm, attn_mods, query_key_value_matrix, local_len
    )
    left_got, right_got, output = after((left_got, right_got, output), grads)
    left_send, left, right_send, right = second_halves(at, left, left_got, right, right_got)
    left_got, right_got = pair_permute(left_send, SECOND), pair_permute(right_send, FIRST)
    grads = after(grads, left, right, output)

    time_row, late_send, late_keep = late_grads(
        core, grads, xm_attn, attn_sums, late_mods, ada_weight, column, early_parts, sp
    )
    hidden_grad = exchange(after(hg, left, right))
    late_got = pair_permute(late_send, CORE)
    left_got, right_got = after((left_got, right_got), late_keep)
    if lax.axis_size("dp") > 2 * SECOND:
        left, right = sum_over_rest(add(left, left_got)), sum_over_rest(add(right, right_got))
        sides = [(left,), (right,)]
    else:
        sides = [(left, left_got), (right, right_got)]
    near_send, near = near_halves(at, sides)
    near_got = pair_permute(near_send, 1, "sp")
    late_got = after(late_got, near)
    own_quarter, *other_quarters = quarters(at, late_keep, late_got)
    quarter_parts = [own_quarter] + [
        pair_permute(p, bit)
        for p, bit in zip(other_quarters, (SECOND, FIRST, FIRST + SECOND))
    ]
    output = hand_over(after(output, own_quarter))
    near_got, hidden_grad = after((near_got, hidden_grad), output)
    near_got = after(near_got, hidden_grad)
    upper = me // 2
    far_send = add(pick(near, 1 - upper), pick(near_got, 1 - upper))
    far = add(pick(near, upper), pick(near_got, upper))
    far_got = pair_permute(far_send, 2, "sp")
    quarter_parts = after(quarter_parts, far, far_send)
    if lax.axis_size("dp") > 2 * SECOND:
        total = sum(p.astype(f32) for p in quarter_parts).astype(bf16)
        quarter_parts = [sum_over_rest(total)]
    late_near_send, late_near = near_halves(at, [quarter_parts])
    late_near_got = pair_permute(late_near_send, 1, "sp")
    early_own = add(far, after(far_got, late_near))
    early_four = spread(early_own)
    late_near_got = after(late_near_got, early_own)
    late_far_send = add(pick(late_near, 1 - upper), pick(late_near_got, 1 - upper))
    late_far = add(pick(late_near, upper), pick(late_near_got, upper))
    late_far_got = pair_permute(late_far_send, 2, "sp")
    late_own = add(late_far, late_far_got)
    hidden_grad = after(hidden_grad, late_own).astype(f32)
    time_rows = after(time_row, late_own)
    for bit in bits("sp"):
        time_rows = double(time_rows, bit, "sp")
    time_grad = jnp.concatenate([pick(time_rows, me ^ s)[None] for s in range(sp)], axis=0)
    time_grad = time_grad.astype(f32)
    early_half = four_chips(at, after(early_four, late_own, time_rows, hidden_grad), True)
    early_other = pair_permute(early_half, CORE)
    late_four = spread(after(late_own, early_half))
    n_row, n_col = row_keep.shape[1] // 2, col_keep.shape[1] // 2
    row_starts = [x * (n_row + n_col) + i for x in range(2) for i in range(0, n_row, half)]
    col_starts = [x * (n_row + n_col) + n_row + i for x in range(2) for i in range(0, n_col, half)]
    down_grad, up_grad, proj_grad, early_vectors = finish(
        core,
        early_half,
        after(early_other, late_four[0]),
        half,
        (
            (sp, 1, row_starts),
            (1, n_up, col_starts[:n_up]),
            (1, 1, col_starts[n_up : n_up + 1]),
            (1, 1, col_starts[n_up + 1 :]),
        ),
    )
    late_half = four_chips(at, after(late_four, down_grad), False)
    late_other = pair_permute(late_half, CORE)
    qkv_grad, ada_weight_grad, *small = late_finish(
        core, late_half, late_other, early_vectors, half, cond, sp
    )
    ada_bias_grad, attn_gain_grad, mlp_gain_grad, up_bias_grad, down_bias_grad = (
        v.reshape(-1) for v in small
    )
    return (
        output,
        hidden_grad,
        time_grad,
        ada_weight_grad,
        ada_bias_grad,
        attn_gain_grad,
        qkv_grad,
        proj_grad,
        mlp_gain_grad,
        up_grad,
        up_bias_grad,
        down_grad,
        down_bias_grad,
    )


def solution(mesh):
    return jax.shard_map(
        body,
        mesh=mesh,
        in_specs=(P("dp", "sp", None), P("dp", None)) + (P(),) * 10 + (P("dp", "sp", None),),
        out_specs=(
            P("dp", "sp", None),
            P("dp", "sp", None),
            P("dp", None),
            P("sp", None),
            P("sp"),
            P("sp"),
            P("sp", None),
            P("sp", None),
            P("sp"),
            P("sp", None),
            P("sp"),
            P("sp", None),
            P("sp"),
        ),
        check_vma=False,
    )
```

```python
import functools

import jax
import jax.numpy as jnp
from jax import lax
from jax.experimental import pallas as pl
from jax.experimental.pallas import tpu as pltpu
from jax.sharding import PartitionSpec as P

HEAD_DIM = 64
MIB = 1 << 20
VMEM = pl.BlockSpec(memory_space=pltpu.VMEM)
SMEM = pl.BlockSpec(memory_space=pltpu.SMEM)
HALF = HEAD_DIM // 2
LANES = 128
EPSILON = 1e-05
LOG2E = 1.4426950408889634
SCALE = HEAD_DIM ** (-0.5)
f32 = jnp.float32
COVER = pl.CostEstimate(flops=40_000_000_000, bytes_accessed=100_000_000, transcendentals=0)
bf16 = jnp.bfloat16


def on_chip(arrays):
    return [pltpu.with_memory_space_constraint(a, pltpu.VMEM) for a in arrays]


def streamed(*arrays):
    return [pltpu.with_memory_space_constraint(a, pltpu.HBM) for a in arrays]


def dot_nn(a, b):
    return lax.dot_general(a, b, (((1,), (0,)), ((), ())), preferred_element_type=f32)


def dot_nt(a, b):
    return lax.dot_general(a, b, (((1,), (1,)), ((), ())), preferred_element_type=f32)


def dot_tn(a, b):
    return lax.dot_general(a, b, (((0,), (0,)), ((), ())), preferred_element_type=f32)


def column_sum(values):
    return jnp.sum(values, axis=0, keepdims=True)


def norm_forward(values):
    center = values - jnp.mean(values, axis=-1, keepdims=True)
    inverse = lax.rsqrt(jnp.mean(center * center, axis=-1, keepdims=True) + EPSILON)
    return center * inverse, inverse


def norm_backward(grad, normed, inverse):
    first = jnp.mean(grad, axis=-1, keepdims=True)
    second = jnp.mean(grad * normed, axis=-1, keepdims=True)
    return inverse * (grad - first - normed * second)


def swap_halves(values):
    lane = lax.broadcasted_iota(jnp.int32, (1, LANES), 1)
    lower = (lane & (HEAD_DIM - 1)) < HALF
    up = pltpu.roll(values, LANES - HALF, 1)
    down = pltpu.roll(values, HALF, 1)
    return lower, up, down


def rotary(values, cos, sin):
    lower, up, down = swap_halves(values)
    return values * cos + jnp.where(lower, -up, down) * sin


def unrotary(values, cos, sin):
    lower, up, down = swap_halves(values * sin)
    return values * cos + jnp.where(lower, up, -down)


def qkv_kernel(x_ref, mod_ref, w_ref, cos_ref, sin_ref, xm_ref, q_ref, k_ref, v_ref):
    width = x_ref.shape[1]
    normed, _ = norm_forward(x_ref[...].astype(f32))
    xm = (normed * mod_ref[0:1, :] + mod_ref[1:2, :]).astype(bf16)
    xm_ref[...] = xm
    cos, sin = cos_ref[...], sin_ref[...]
    for part, ref in enumerate((q_ref, k_ref, v_ref)):
        whole = dot_nn(xm, w_ref[:, part * width : (part + 1) * width]).astype(bf16)
        if part == 2:
            ref[...] = whole
            continue
        for lane in range(0, width, LANES):
            piece = whole[:, lane : lane + LANES].astype(f32)
            ref[:, lane : lane + LANES] = rotary(piece, cos, sin).astype(bf16)


def project_qkv(x, mods, weight, cos, sin, rows=256):
    length, width = x.shape
    block = pl.BlockSpec((rows, width), lambda i: (i, 0))
    table = pl.BlockSpec((rows, LANES), lambda i: (i, 0))
    shape = pltpu.HBM((length, width), bf16)
    return pl.pallas_call(
        qkv_kernel,
        grid=(length // rows,),
        in_specs=[
            block,
            VMEM,
            pl.BlockSpec(weight.shape, lambda i: (0, 0)),
            table,
            table,
        ],
        out_specs=[block] * 4,
        out_shape=[shape] * 4,
        cost_estimate=COVER,
        compiler_params=pltpu.CompilerParams(vmem_limit_bytes=18 * MIB),
        name="project_qkv",
    )(x, mods, *streamed(weight, cos, sin))


def attention_forward_kernel(q_ref, k_ref, v_ref, o_ref, lse_ref, *, chunk, ahead):
    k, v = k_ref[...], v_ref[...]
    first = lax.broadcasted_iota(jnp.int32, (1, LANES), 1) < HEAD_DIM
    c = LOG2E * SCALE
    masks = (first, ~first)
    keys = [jnp.where(m, k, jnp.zeros_like(k)) for m in masks]
    values = [jnp.where(m, v, jnp.ones_like(v)) for m in masks]
    items = [(h, start) for start in range(0, q_ref.shape[0], chunk) for h in range(2)]

    def scores(h, start):
        return dot_nt(keys[h], q_ref[start : start + chunk, :])

    waiting = [scores(*item) for item in items[:ahead]]
    outs = {}
    for i, (h, start) in enumerate(items):
        st = waiting.pop(0)
        if i + ahead < len(items):
            waiting.append(scores(*items[i + ahead]))
        rows = slice(start, start + chunk)
        top = jnp.max(st, axis=0, keepdims=True) * c
        p = jnp.exp2(st * c - top).astype(bf16)
        ot = dot_tn(values[h], p)
        own, ones = (ot[:HEAD_DIM], ot[HEAD_DIM:]) if h == 0 else (ot[HEAD_DIM:], ot[:HEAD_DIM])
        total = ones[0:1]
        outs[h] = own * (1.0 / total)
        lse_ref[0, h : h + 1, rows] = top + jnp.log2(total)
        if h == 1:
            o_ref[rows, :] = jnp.concatenate([outs[0], outs[1]], axis=0).T.astype(bf16)


def attention_forward(q, k, v):
    length, width = q.shape
    pairs = width // LANES
    block = pl.BlockSpec((length, LANES), lambda i: (0, i))
    return pl.pallas_call(
        functools.partial(attention_forward_kernel, chunk=length // 2, ahead=2),
        grid=(pairs,),
        in_specs=[block] * 3,
        out_specs=[block, pl.BlockSpec((1, 2, length), lambda i: (i, 0, 0))],
        out_shape=[
            pltpu.HBM((length, width), bf16),
            pltpu.HBM((pairs, 2, length), f32),
        ],
        cost_estimate=COVER,
        compiler_params=pltpu.CompilerParams(vmem_limit_bytes=14 * MIB),
        name="attention_forward",
    )(*streamed(q, k, v))


def attention_backward_kernel(
    q_ref, k_ref, v_ref, do_ref, o_ref, lse_ref, cos_ref, sin_ref, x_ref, gm_ref, mod_ref, w_ref,
    g_ref, hg_ref, sum_ref, held_ref, *, pairs,
):
    step = pl.program_id(0)
    width = x_ref.shape[1]

    @pl.when(step < pairs)
    def _():
        first = lax.broadcasted_iota(jnp.int32, (1, LANES), 1) < HEAD_DIM
        upper = lax.broadcasted_iota(jnp.int32, (LANES, 1), 0) < HEAD_DIM
        c = LOG2E * SCALE
        q, k, v, do = q_ref[...], k_ref[...], v_ref[...], do_ref[...]
        prod = (do.astype(f32) * o_ref[...].astype(f32)).T
        kt = k.T
        zero = jnp.zeros_like(k)
        dq = dk = dv = None
        for h in range(2):
            mine = first if h == 0 else ~first
            row = column_sum(prod[h * HEAD_DIM : (h + 1) * HEAD_DIM])
            st = dot_nt(jnp.where(mine, k, zero), q)
            p = jnp.exp2(st * c - lse_ref[0, h : h + 1, :])
            dp = dot_nt(jnp.where(mine, v, zero), do)
            ds = (p * (dp - row)).astype(bf16)
            dvh = dot_nn(p.astype(bf16), jnp.where(mine, do, zero))
            dkh = dot_nn(ds, jnp.where(mine, q, zero))
            dqh = dot_nn(jnp.where(upper if h == 0 else ~upper, kt, jnp.zeros_like(kt)), ds)
            dq, dk, dv = (dqh, dkh, dvh) if h == 0 else (dq + dqh, dk + dkh, dv + dvh)
        cos, sin = cos_ref[...], sin_ref[...]
        lanes = pl.ds(pl.multiple_of(step * LANES, LANES), LANES)
        for part, value in enumerate(
            (unrotary(dq.T * SCALE, cos, sin), unrotary(dk * SCALE, cos, sin), dv)
        ):
            value = value.astype(bf16)
            g_ref[part] = value
            held_ref[part, :, lanes] = value

    @pl.when(step >= pairs)
    def _():
        rows = x_ref.shape[0]
        tile = pl.ds(pl.multiple_of((step - pairs) * rows, rows), rows)
        normed, inverse = norm_forward(x_ref[...].astype(f32))
        grad = None
        for part in range(3):
            g = dot_nt(held_ref[part, tile, :], w_ref[:, part * width : (part + 1) * width])
            grad = g if grad is None else grad + g
        hg = gm_ref[...] + norm_backward(grad * mod_ref[0:1, :], normed, inverse)
        hg_ref[...] = hg.astype(bf16)
        sums = jnp.concatenate(
            [column_sum(grad), column_sum(grad * normed), jnp.zeros((6, width), f32)], axis=0
        )

        @pl.when(step == pairs)
        def _():
            sum_ref[...] = sums

        @pl.when(step > pairs)
        def _():
            sum_ref[...] += sums


def attention_backward(q, k, v, do, o, lse, cos, sin, x, gm, mods, weight, rows):
    length, width = q.shape
    pairs = width // LANES

    def pair(i):
        return jnp.minimum(i, pairs - 1)

    block = pl.BlockSpec((length, LANES), lambda i: (0, pair(i)))
    table = pl.BlockSpec((length, LANES), lambda i: (0, 0))
    tile = pl.BlockSpec((rows, width), lambda i: (jnp.maximum(i - pairs, 0), 0))
    return pl.pallas_call(
        functools.partial(attention_backward_kernel, pairs=pairs),
        grid=(pairs + length // rows,),
        in_specs=[block] * 5
        + [pl.BlockSpec((1, 2, length), lambda i: (pair(i), 0, 0)), table, table, tile, tile, VMEM, VMEM],
        out_specs=[
            pl.BlockSpec((3, length, LANES), lambda i: (0, 0, pair(i))),
            tile,
            pl.BlockSpec((8, width), lambda i: (0, 0)),
        ],
        out_shape=[
            pltpu.HBM((3, length, width), bf16),
            pltpu.HBM((length, width), bf16),
            jax.ShapeDtypeStruct((8, width), f32),
        ],
        scratch_shapes=[pltpu.VMEM((3, length, width), bf16)],
        cost_estimate=COVER,
        compiler_params=pltpu.CompilerParams(vmem_limit_bytes=34 * MIB),
        name="attention_backward",
    )(q, k, v, do, o, lse, cos, sin, x, gm, mods, weight)


def mlp_kernel(
    x_ref, mixed_ref, cot_ref, mod_ref, bias_ref, wo_ref, wu_ref, wd_ref,
    xm_ref, act_ref, gd_ref, gp_ref, gm_ref, gmix_ref, sum_ref, up_sum_ref, out_ref,
):
    chunk, ff = wu_ref.shape
    gate_attn, scaled, shift = mod_ref[0:1, :], mod_ref[1:2, :], mod_ref[2:3, :]
    gate_mlp, down_bias = mod_ref[3:4, :], mod_ref[4:5, :]
    cot = cot_ref[...].astype(f32)
    projected = dot_nn(mixed_ref[...], wo_ref[...])
    middle = x_ref[...].astype(f32) + gate_attn * projected
    normed, inverse = norm_forward(middle)
    xm = (normed * scaled + shift).astype(bf16)
    xm_ref[0] = xm
    xm_ref[1] = mixed_ref[...]
    gd = (gate_mlp * cot).astype(bf16)
    gd_ref[...] = gd
    down = grad_mod = None
    c0 = 0.7978845608028654
    c1 = c0 * 0.044715
    up_sums = []
    for at in range(0, ff, chunk):
        cols = slice(at, at + chunk)
        pre = dot_nn(xm, wu_ref[:, cols]) + bias_ref[:, cols]
        square = pre * pre
        t = jnp.tanh(pre * (c0 + c1 * square))
        half = 0.5 + 0.5 * t
        wide_act = pre * half
        act = wide_act.astype(bf16)
        act_ref[:, cols] = act
        slope = half + wide_act * (1.0 - half) * (2.0 * c0 + (6.0 * c1) * square)
        wide_gp = slope * dot_nt(gd, wd_ref[cols, :])
        gp = wide_gp.astype(bf16)
        gp_ref[at // chunk] = gp
        up_sums.append(column_sum(wide_gp))
        d = dot_nn(act, wd_ref[cols, :])
        g = dot_nt(gp, wu_ref[:, cols])
        down, grad_mod = (d, g) if down is None else (down + d, grad_mod + g)
    down = down + down_bias
    out_ref[...] = (middle + gate_mlp * down).astype(bf16)
    gm = cot + norm_backward(grad_mod * scaled, normed, inverse)
    gm_ref[...] = gm
    gpj = (gate_attn * gm).astype(bf16)
    gp_ref[ff // chunk] = gpj
    gmix_ref[...] = dot_nt(gpj, wo_ref[...]).astype(bf16)
    sums = jnp.concatenate(
        [
            column_sum(cot * down),
            column_sum(gd.astype(f32)),
            column_sum(grad_mod),
            column_sum(grad_mod * normed),
            column_sum(gm * projected),
            jnp.zeros((3, cot.shape[1]), f32),
        ],
        axis=0,
    )
    up_sum = jnp.concatenate(up_sums, axis=1)

    @pl.when(pl.program_id(0) == 0)
    def _():
        sum_ref[...] = sums
        up_sum_ref[...] = up_sum

    @pl.when(pl.program_id(0) > 0)
    def _():
        sum_ref[...] += sums
        up_sum_ref[...] += up_sum


def feed_forward(x, mixed, cot, mods, up_bias, wo, wu, wd, rows):
    length, width = x.shape
    ff = wu.shape[1]
    block = pl.BlockSpec((rows, width), lambda i: (i, 0))
    wide = pl.BlockSpec((rows, ff), lambda i: (i, 0))

    narrow = pltpu.HBM((length, width), bf16)
    broad = pltpu.HBM((length, ff), bf16)
    return pl.pallas_call(
        mlp_kernel,
        grid=(length // rows,),
        in_specs=[block, block, block] + [VMEM] * 5,
        out_specs=[
            pl.BlockSpec((2, rows, width), lambda i: (0, i, 0)),
            wide,
            block,
            pl.BlockSpec((ff // width + 1, rows, width), lambda i: (0, i, 0)),
            block,
            block,
            pl.BlockSpec((8, width), lambda i: (0, 0)),
            pl.BlockSpec((1, ff), lambda i: (0, 0)),
        ]
        + [block],
        out_shape=[
            pltpu.HBM((2, length, width), bf16), broad, narrow,
            pltpu.HBM((ff // width + 1, length, width), bf16),
            pltpu.HBM((length, width), f32), narrow,
            jax.ShapeDtypeStruct((8, width), f32), jax.ShapeDtypeStruct((1, ff), f32),
        ]
        + [narrow],
        cost_estimate=COVER,
        compiler_params=pltpu.CompilerParams(vmem_limit_bytes=40 * MIB),
        name="feed_forward",
    )(x, *streamed(mixed, cot), mods, up_bias, wo, *streamed(wu, wd))


def late_grads_kernel(
    core_ref, sum_ref, mod_ref, ada_ref, timing_ref, early_ref, xm_ref, block_ref,
    time_ref, send_ref, keep_ref, *, parts,
):
    step = pl.program_id(0)
    width = block_ref.shape[2]

    @pl.when(step < parts)
    def _():
        product = dot_tn(xm_ref[...], block_ref[0])
        half = send_ref.shape[1]
        for i, (send, keep) in enumerate(split_halves(product, half, core_ref[0] == 0)):
            send_ref[i] = send
            keep_ref[i] = keep

    @pl.when(step == parts)
    def _():
        sp, half, _ = send_ref.shape
        shift, scaled = sum_ref[0:1, :], sum_ref[1:2, :]
        scale = scaled * mod_ref[0:1, :]
        gain = scaled * mod_ref[1:2, :]
        row = jnp.concatenate([shift, scale] + [early_ref[i : i + 1, :] for i in range(4)], axis=1)
        high = row.astype(bf16)
        low = (row - high.astype(f32)).astype(bf16)
        time_ref[...] = (dot_nt(high, ada_ref[...]) + dot_nt(low, ada_ref[...])).astype(bf16)
        bias = jnp.concatenate([shift, scale, jnp.zeros((1, 4 * width), f32)], axis=1)
        count, own, quarter = timing_ref.shape[0] // sp, 6 * width // sp, width // sp
        for ref, first in ((send_ref, core_ref[0] == 1), (keep_ref, core_ref[0] == 0)):
            part = jnp.where(first, shift, scale)
            for i in range(sp):
                ref[i, :count] = (timing_ref[i * count : (i + 1) * count, :] * part).astype(bf16)
                mine = bias[:, i * own : (i + 1) * own]
                rest = jnp.concatenate(
                    [
                        mine[:, width:],
                        gain[:, i * quarter : (i + 1) * quarter],
                        jnp.zeros((1, 2 * width - own - quarter), f32),
                    ],
                    axis=1,
                )
                sums = jnp.concatenate(
                    [jnp.where(first, mine[:, :width], rest), jnp.zeros((half - count - 1, width), f32)], axis=0
                )
                ref[i, count:] = sums.astype(bf16)


def late_grads(core, grads, xm, sums, mods, ada, timing, early, sp):
    n, length, width = grads.shape
    half = width // sp // 2
    out = pl.BlockSpec((sp, half, width), lambda i, c: (0, i, 0))
    shape = jax.ShapeDtypeStruct((sp, (n + 1) * half, width), bf16)
    cond = timing.shape[0]
    return pl.pallas_call(
        functools.partial(late_grads_kernel, parts=n),
        grid_spec=pltpu.PrefetchScalarGridSpec(
            num_scalar_prefetch=1,
            grid=(n + 1,),
            in_specs=[VMEM] * 5
            + [
                pl.BlockSpec((length, width), lambda i, c: (0, 0)),
                pl.BlockSpec((1, length, width), lambda i, c: (jnp.minimum(i, n - 1), 0, 0)),
            ],
            out_specs=[pl.BlockSpec((1, cond), lambda i, c: (0, 0)), out, out],
        ),
        out_shape=[jax.ShapeDtypeStruct((1, cond), bf16), shape, shape],
        cost_estimate=COVER,
        compiler_params=pltpu.CompilerParams(vmem_limit_bytes=18 * MIB),
        name="late_grads",
    )(core, sums, mods, ada, timing, early, xm, grads)


def split_halves(product, half, this_core):
    pieces = []
    for at in range(0, product.shape[0], 2 * half):
        low = product[at : at + half].astype(bf16)
        high = product[at + half : at + 2 * half].astype(bf16)
        pieces.append((jnp.where(this_core, high, low), jnp.where(this_core, low, high)))
    return pieces


def row_grad_kernel(core_ref, a_ref, b_ref, send_ref, keep_ref, *, half):
    product = dot_tn(a_ref[...], b_ref[...])
    for i, (send, keep) in enumerate(split_halves(product, half, core_ref[0] == 0)):
        send_ref[0, i * half : (i + 1) * half] = send
        keep_ref[0, i * half : (i + 1) * half] = keep


def row_grad(core, a, b, sp):
    length, width = b.shape
    out = pltpu.HBM((sp, width // 2, width), bf16)
    block = pl.BlockSpec((1, width // 2, width), lambda j, c: (j, 0, 0))
    return pl.pallas_call(
        functools.partial(row_grad_kernel, half=width // sp // 2),
        grid_spec=pltpu.PrefetchScalarGridSpec(
            num_scalar_prefetch=1,
            grid=(sp,),
            in_specs=[
                pl.BlockSpec((length, width), lambda j, c: (0, j)),
                pl.BlockSpec((length, width), lambda j, c: (0, 0)),
            ],
            out_specs=[block, block],
        ),
        out_shape=[out, out],
        cost_estimate=COVER,
        compiler_params=pltpu.CompilerParams(vmem_limit_bytes=18 * MIB),
        name="row_grad",
    )(core, *streamed(a, b))


def column_grad_kernel(
    core_ref, sum_ref, up_sum_ref, mod_ref, timing_ref, a_ref, b_ref, send_ref, keep_ref, parts_ref, *, blocks
):
    step = pl.program_id(0)
    sp, half, width = send_ref.shape

    @pl.when(step < blocks)
    def _():
        product = dot_tn(a_ref[0], b_ref[0])
        for i, (send, keep) in enumerate(split_halves(product, half, core_ref[0] == 0)):
            send_ref[i] = send
            keep_ref[i] = keep

    @pl.when(step == blocks)
    def _():
        scaled = sum_ref[3:4, :]
        parts = [sum_ref[4:5, :], sum_ref[2:3, :], scaled * mod_ref[0:1, :], sum_ref[0:1, :]]
        for i, part in enumerate(parts):
            parts_ref[i : i + 1, :] = part
        gain = scaled * mod_ref[1:2, :]
        bias = jnp.concatenate([jnp.zeros((1, 2 * width), f32)] + parts, axis=1)
        count, own, quarter = timing_ref.shape[0] // sp, 6 * width // sp, width // sp
        for ref, first in ((send_ref, core_ref[0] == 1), (keep_ref, core_ref[0] == 0)):
            for i in range(sp):
                column = timing_ref[i * count : (i + 1) * count, :]
                for p in range(2):
                    part = jnp.where(first, parts[p], parts[p + 2])
                    ref[i, p * count : (p + 1) * count] = (column * part).astype(bf16)
                shard = slice(i * quarter, (i + 1) * quarter)
                mine = bias[:, i * own : (i + 1) * own]
                gains = jnp.concatenate(
                    [gain[:, shard], sum_ref[1:2, shard], jnp.zeros((1, width - 2 * quarter), f32)], axis=1
                )
                rest = jnp.concatenate([mine[:, width:], jnp.zeros((1, 2 * width - own), f32)], axis=1)
                sums = jnp.concatenate(
                    [
                        jnp.where(first, up_sum_ref[:, i * width : (i + 1) * width], gains),
                        jnp.where(first, mine[:, :width], rest),
                        jnp.zeros((half - 2 * count - 2, width), f32),
                    ],
                    axis=0,
                )
                ref[i, 2 * count :] = sums.astype(bf16)


def column_grad(core, sums, up_sum, mods, timing, a, b, sp, second):
    _, length, width = a.shape
    n = b.shape[0]
    half = width // sp // 2
    out = pltpu.HBM((sp, (n + 1) * half, width), bf16)
    block = pl.BlockSpec((sp, half, width), lambda j, c: (0, j, 0))
    return pl.pallas_call(
        functools.partial(column_grad_kernel, blocks=n),
        grid_spec=pltpu.PrefetchScalarGridSpec(
            num_scalar_prefetch=1,
            grid=(n + 1,),
            in_specs=[VMEM] * 4
            + [
                pl.BlockSpec((1, length, width), lambda j, c: (jnp.minimum(j, n - 1) // second, 0, 0)),
                pl.BlockSpec((1, length, width), lambda j, c: (jnp.minimum(j, n - 1), 0, 0)),
            ],
            out_specs=[block, block, pl.BlockSpec((4, width), lambda j, c: (0, 0))],
        ),
        out_shape=[out, out, jax.ShapeDtypeStruct((4, width), f32)],
        cost_estimate=COVER,
        compiler_params=pltpu.CompilerParams(vmem_limit_bytes=18 * MIB),
        name="column_grad",
    )(core, sums, up_sum, mods, timing, *streamed(a, b))


def shift_permute(value, axis, by):
    n = lax.axis_size(axis)
    return lax.ppermute(value, axis, [(i, (i + by) % n) for i in range(n)])


def pair_permute(value, bit, axis="dp"):
    n = lax.axis_size(axis)
    return lax.ppermute(value, axis, [(i, i ^ bit) for i in range(n)])


def pick(values, index, axis=0):
    return lax.dynamic_index_in_dim(values, index, axis, keepdims=False)


def after(values, *others):
    return lax.optimization_barrier((values, others))[0]


def bit_of(index, bit):
    return (index // bit) % 2


def add(a, b):
    return (a.astype(f32) + b.astype(f32)).astype(bf16)


CORE, FIRST, SECOND = 1, 2, 4


def first_halves_kernel(at_ref, row_keep, row_got, col_keep, col_got, *outs):
    columns = outs[0].shape[2]
    start = 0
    for keep, got in ((row_keep, row_got), (col_keep, col_got)):
        total = add(keep[0], got[0])
        n = total.shape[0] // 2
        low, high = total[:n], total[n:]
        for side in range(2):
            cols = slice(side * columns, (side + 1) * columns)
            mine = at_ref[side] == 0
            outs[2 * side][0, start : start + n] = jnp.where(mine, high, low)[:, cols]
            outs[2 * side + 1][0, start : start + n] = jnp.where(mine, low, high)[:, cols]
        start += n


def first_halves(at, row_keep, row_got, col_keep, col_got):
    sp, rows, width = row_keep.shape
    cols = col_keep.shape[1]

    def spec(a):
        return pl.BlockSpec((1,) + a.shape[1:], lambda s, t: (s, 0, 0))

    out = pltpu.HBM((sp, (rows + cols) // 2, width // 2), bf16)
    return pl.pallas_call(
        first_halves_kernel,
        grid_spec=pltpu.PrefetchScalarGridSpec(
            num_scalar_prefetch=1,
            grid=(sp,),
            in_specs=[spec(a) for a in (row_keep, row_got, col_keep, col_got)],
            out_specs=[spec(out)] * 4,
        ),
        out_shape=[out] * 4,
        cost_estimate=COVER,
        compiler_params=pltpu.CompilerParams(vmem_limit_bytes=12 * MIB),
        name="first_halves",
    )(at, *streamed(row_keep, row_got, col_keep, col_got))


def second_halves_kernel(at_ref, *refs):
    for side in range(2):
        mine = at_ref[1 - side]
        keep, got = refs[2 * side : 2 * side + 2]
        for s in range(keep.shape[0]):
            refs[4 + 2 * side][s] = add(keep[s, 1 - mine], got[s, 1 - mine])
            refs[5 + 2 * side][s] = add(keep[s, mine], got[s, mine])


def second_halves(at, *arrays):
    sp, rows, columns = arrays[0].shape
    out = pltpu.HBM((sp, rows // 2, columns), bf16)
    return pl.pallas_call(
        second_halves_kernel,
        in_specs=[SMEM] + [VMEM] * 4,
        out_specs=[VMEM] * 4,
        out_shape=[out] * 4,
        cost_estimate=COVER,
        compiler_params=pltpu.CompilerParams(vmem_limit_bytes=10 * MIB),
        name="second_halves",
    )(at, *streamed(*[a.reshape(sp, 2, rows // 2, columns) for a in arrays]))


def near_halves_kernel(at_ref, *refs, terms, sides):
    ins, outs = refs[:-2], refs[-2:]
    mine = lax.rem(at_ref[2], 2)
    for out, bit in zip(outs, (1 - mine, mine)):
        for s in range(out.shape[0]):
            at = 0
            for side in range(sides):
                total = None
                for ref in ins[side * terms : (side + 1) * terms]:
                    value = ref[2 * s + bit].astype(f32)
                    total = value if total is None else total + value
                out[s, :, at : at + total.shape[1]] = total.astype(bf16)
                at += total.shape[1]


def near_halves(at, sides):
    terms = len(sides[0])
    flat = [a for side in sides for a in side]
    sp, rows, _ = flat[0].shape
    width = sum(side[0].shape[2] for side in sides)
    out = jax.ShapeDtypeStruct((sp // 2, rows, width), bf16)
    return pl.pallas_call(
        functools.partial(near_halves_kernel, terms=terms, sides=len(sides)),
        in_specs=[SMEM] + [VMEM] * len(flat),
        out_specs=[VMEM] * 2,
        out_shape=[out] * 2,
        cost_estimate=COVER,
        compiler_params=pltpu.CompilerParams(vmem_limit_bytes=8 * MIB),
        name="near_halves",
    )(at, *on_chip(flat))


def far_halves_kernel(at_ref, keep, got, send_ref, keep_ref):
    mine = lax.div(at_ref[2], 2)
    send_ref[...] = add(keep[1 - mine], got[1 - mine])
    keep_ref[...] = add(keep[mine], got[mine])


def far_halves(at, keep, got):
    out = jax.ShapeDtypeStruct(keep.shape[1:], bf16)
    return pl.pallas_call(
        far_halves_kernel,
        in_specs=[SMEM] + [VMEM] * 2,
        out_specs=[VMEM] * 2,
        out_shape=[out] * 2,
        cost_estimate=COVER,
        name="far_halves",
    )(at, keep, got)


def hand_over_kernel(in_ref, out_ref):
    out_ref[...] = in_ref[...].astype(out_ref.dtype)


def widen(value):
    return hand_over(value, f32)


def hand_over(value, dtype=bf16):
    block = pl.BlockSpec((1,) + value.shape[1:], lambda i: (i, 0, 0))
    return pl.pallas_call(
        hand_over_kernel,
        grid=(value.shape[0],),
        in_specs=[block],
        out_specs=block,
        out_shape=jax.ShapeDtypeStruct(value.shape, dtype),
        cost_estimate=COVER,
        compiler_params=pltpu.CompilerParams(vmem_limit_bytes=6 * MIB),
        name="hand_over",
    )(value)


def own_kernel(keep_ref, got_ref, out_ref):
    out_ref[...] = add(keep_ref[...], got_ref[...])


def own_sum(keep, got):
    return pl.pallas_call(
        own_kernel,
        in_specs=[VMEM] * 2,
        out_specs=VMEM,
        out_shape=jax.ShapeDtypeStruct(keep.shape, bf16),
        cost_estimate=COVER,
        name="own_sum",
    )(keep, got)


def quarters_kernel(at_ref, keep_ref, got_ref, *outs):
    for i, out in enumerate(outs):
        index = 2 * (at_ref[0] ^ (i // 2)) + (at_ref[1] ^ (i % 2))
        for s in range(keep_ref.shape[0]):
            out[s] = add(keep_ref[s, index], got_ref[s, index])


def quarters(at, keep, got):
    sp, rows, width = keep.shape
    out = jax.ShapeDtypeStruct((sp, rows // 4, width), bf16)
    return pl.pallas_call(
        quarters_kernel,
        in_specs=[SMEM] + [VMEM] * 2,
        out_specs=[VMEM] * 4,
        out_shape=[out] * 4,
        cost_estimate=COVER,
        compiler_params=pltpu.CompilerParams(vmem_limit_bytes=10 * MIB),
        name="quarters",
    )(at, *on_chip([a.reshape(sp, 4, rows // 4, width) for a in (keep, got)]))


def four_chips_kernel(at_ref, *refs, crossed):
    pieces, out_ref = refs[:4], refs[4]
    columns = out_ref.shape[2] // 2
    for i, piece in enumerate(pieces):
        x, y = at_ref[0] ^ (i // 2), at_ref[1] ^ (i % 2)
        out_ref[2 * x + y, :, :columns] = piece[:, :columns]
        out_ref[2 * y + x if crossed else 2 * x + y, :, columns:] = piece[:, columns:]


def four_chips(at, pieces, crossed):
    rows, width = pieces[0].shape
    return pl.pallas_call(
        functools.partial(four_chips_kernel, crossed=crossed),
        in_specs=[SMEM] + [VMEM] * 4,
        out_specs=VMEM,
        out_shape=jax.ShapeDtypeStruct((4, rows, width), bf16),
        cost_estimate=COVER,
        compiler_params=pltpu.CompilerParams(vmem_limit_bytes=8 * MIB),
        name="four_chips",
    )(at, *on_chip(pieces)).reshape(4 * rows, width)


def spread(own):
    return [own] + [pair_permute(own, bit) for bit in (SECOND, FIRST, FIRST + SECOND)]


def finish_kernel(core_ref, mine_ref, other_ref, *outs, half, layout):
    first = core_ref[0] == 0
    width = mine_ref.shape[1]
    for out, (_, across, starts) in zip(outs, layout):
        for n, at in enumerate(starts):
            cols = slice(n % across * width, (n % across + 1) * width)
            mine = mine_ref[at : at + half].astype(f32)
            other = other_ref[at : at + half].astype(f32)
            to = n // across * 2 * half
            out[to : to + half, cols] = jnp.where(first, mine, other)
            out[to + half : to + 2 * half, cols] = jnp.where(first, other, mine)


def finish(core, mine, other, half, layout):
    width = mine.shape[1]
    shapes = [(2 * half * down, width * across) for down, across, _ in layout]
    return pl.pallas_call(
        functools.partial(finish_kernel, half=half, layout=layout),
        grid=(1,),
        in_specs=[SMEM] + [VMEM] * 2,
        out_specs=[pl.BlockSpec(s, lambda i: (0, 0)) for s in shapes],
        out_shape=[jax.ShapeDtypeStruct(s, f32) for s in shapes],
        cost_estimate=COVER,
        compiler_params=pltpu.CompilerParams(vmem_limit_bytes=16 * MIB),
        name="finish",
    )(core, *on_chip([mine, other]))


def late_finish_kernel(
    core_ref, mine_ref, other_ref, early_ref, qkv_ref, ada_ref, bias_ref, attn_gain_ref, mlp_gain_ref, up_ref,
    down_ref, *, half,
):
    core_first = core_ref[0] == 0
    width = mine_ref.shape[1]
    for n in range(3):
        cols = slice(n * width, (n + 1) * width)
        mine = mine_ref[n * half : (n + 1) * half].astype(f32)
        other = other_ref[n * half : (n + 1) * half].astype(f32)
        qkv_ref[:half, cols] = jnp.where(core_first, mine, other)
        qkv_ref[half:, cols] = jnp.where(core_first, other, mine)
    mine, other = mine_ref[3 * half :].astype(f32), other_ref[3 * half :].astype(f32)
    late = (jnp.where(core_first, mine, other), jnp.where(core_first, other, mine))
    count = ada_ref.shape[0]
    quarter, own = attn_gain_ref.shape[1], bias_ref.size
    for p in range(2):
        ada_ref[:, p * width : (p + 1) * width] = late[p][:count]
    for p in range(4):
        start = p // 2 * half + p % 2 * count
        ada_ref[:, (2 + p) * width : (3 + p) * width] = early_ref[start : start + count, :]
    row, rest = 2 * count, own - width
    sums = (late[0][count : count + 1], late[1][count : count + 1])
    for lane in range(0, own, LANES):
        i, side = lane // LANES, lane // width
        cols = slice(lane % width, lane % width + LANES)
        at = side * half + row + 1
        bias_ref[i : i + 1, :] = early_ref[at : at + 1, cols] + sums[side][:, cols]
    for lane in range(0, width, LANES):
        i = lane // LANES
        up_ref[i : i + 1, :] = early_ref[row : row + 1, lane : lane + LANES]
    attn_gain_ref[...] = sums[1][:, rest : rest + quarter]
    mlp_gain_ref[...] = early_ref[half + row : half + row + 1, :quarter]
    down_ref[...] = early_ref[half + row : half + row + 1, quarter : 2 * quarter]


def late_finish(core, mine, other, early, half, cond, sp):
    width = early.shape[1]
    one = (1, width // sp)
    shapes = [
        (2 * half, 3 * width), (cond // sp, 6 * width), (6 * width // sp // LANES, LANES),
        one, one, (width // LANES, LANES), one,
    ]
    return pl.pallas_call(
        functools.partial(late_finish_kernel, half=half),
        grid=(1,),
        in_specs=[SMEM] + [VMEM] * 3,
        out_specs=[pl.BlockSpec(s, lambda i: (0, 0)) for s in shapes],
        out_shape=[jax.ShapeDtypeStruct(s, f32) for s in shapes],
        cost_estimate=COVER,
        compiler_params=pltpu.CompilerParams(vmem_limit_bytes=12 * MIB),
        name="late_finish",
    )(core, *on_chip([mine, other, early]))


def sum_over_rest(total):
    bit = 2 * SECOND
    while bit < lax.axis_size("dp"):
        total = add(total, pair_permute(total, bit))
        bit *= 2
    return total


def double(rows, bit, axis):
    return jnp.concatenate([rows, pair_permute(rows, bit, axis)], axis=0)


def bits(axis):
    n, bit = lax.axis_size(axis), 1
    while bit < n:
        yield bit
        bit *= 2


def body(
    hidden_in,
    time_embed,
    ada_weight,
    ada_bias,
    attn_gain,
    query_key_value_matrix,
    attention_output_matrix,
    mlp_gain,
    up_projection_matrix,
    up_bias,
    down_projection_matrix,
    down_bias,
    out_cotangent,
):
    sequences, local_len, width = hidden_in.shape
    sp, me = lax.axis_size("sp"), lax.axis_index("sp")
    assert sequences == sp
    def exchange(values):
        values = values.reshape(sp, local_len, width)
        return lax.all_to_all(values, "sp", split_axis=0, concat_axis=0, tiled=True)

    x = exchange(hidden_in).reshape(-1, width)
    cot = exchange(after(out_cotangent, x)).reshape(-1, width)
    here = lax.axis_index("dp")
    core = bit_of(here, CORE).reshape(1)
    at = jnp.stack([bit_of(here, FIRST), bit_of(here, SECOND), me])

    timing = lax.dynamic_slice_in_dim(time_embed, me, 1, 0)
    modulation = dot_nn(timing, ada_weight) + ada_bias.astype(f32)[None]
    shift_attn, scale_attn, gate_attn, shift_mlp, scale_mlp, gate_mlp = jnp.split(
        modulation, 6, axis=-1
    )
    gain_attn = attn_gain.astype(f32)[None]
    gain_mlp = mlp_gain.astype(f32)[None]
    zero = jnp.zeros_like(shift_attn)
    attn_mods = jnp.concatenate(
        [gain_attn * (1.0 + scale_attn), shift_attn] + [zero] * 6, axis=0
    )
    mlp_mods = jnp.concatenate(
        [gate_attn, gain_mlp * (1.0 + scale_mlp), shift_mlp, gate_mlp, down_bias.astype(f32)[None]]
        + [zero] * 3,
        axis=0,
    )
    late_mods = jnp.concatenate([gain_attn, 1.0 + scale_attn] + [zero] * 6, axis=0)
    mlp_grad_mods = jnp.concatenate([gain_mlp, 1.0 + scale_mlp] + [zero] * 6, axis=0)
    column = timing.astype(f32).reshape(timing.shape[1], 1)
    attn_mods, mlp_mods, late_mods, mlp_grad_mods, column, at, core = lax.optimization_barrier(
        (attn_mods, mlp_mods, late_mods, mlp_grad_mods, column, at, core)
    )
    lane = lax.broadcasted_iota(jnp.int32, (1, LANES), 1)
    frequency = 10000.0 ** (-((lane % HALF).astype(f32) * 2.0 / HEAD_DIM))
    row = lax.broadcasted_iota(jnp.int32, (sp * local_len, 1), 0)
    angles = row.astype(f32) * frequency
    cos, sin = jnp.cos(angles), jnp.sin(angles)

    xm_attn, q, k, v = project_qkv(x, attn_mods, query_key_value_matrix, cos, sin)
    mixed, lse = attention_forward(q, k, v)
    both_in, act, gd, both_grad, gm, gmix, sums, up_sum, out = feed_forward(
        x,
        mixed,
        cot,
        mlp_mods,
        up_bias.astype(f32)[None],
        attention_output_matrix,
        up_projection_matrix,
        down_projection_matrix,
        local_len,
    )
    ff = up_bias.shape[0]
    assert ff == sp * width
    n_up = ff // width
    half = width // sp // 2
    quarter = width // sp
    cond = timing.shape[1]
    output = exchange(out)
    col_send, col_keep, early_parts = column_grad(
        core, sums, up_sum, mlp_grad_mods, column, both_in, both_grad, sp, n_up
    )
    col_got = pair_permute(col_send, CORE)
    row_send, row_keep = row_grad(core, *after((act, gd), col_keep), sp)
    row_got = pair_permute(row_send, CORE)

    left_send, left, right_send, right = first_halves(at, row_keep, row_got, col_keep, col_got)
    left_got, right_got = pair_permute(left_send, FIRST), pair_permute(right_send, SECOND)
    gmix = after(gmix, left, right)
    grads, hg, attn_sums = attention_backward(
        q, k, v, gmix, mixed, lse, cos, sin, x, gm, attn_mods, query_key_value_matrix, local_len
    )
    left_got, right_got, output = after((left_got, right_got, output), grads)
    left_send, left, right_send, right = second_halves(at, left, left_got, right, right_got)
    left_got, right_got = pair_permute(left_send, SECOND), pair_permute(right_send, FIRST)
    grads = after(grads, left, right, output)

    time_row, late_send, late_keep = late_grads(
        core, grads, xm_attn, attn_sums, late_mods, ada_weight, column, early_parts, sp
    )
    hidden_grad = exchange(hg)
    late_got = pair_permute(late_send, CORE)
    left_got, right_got = after((left_got, right_got), late_keep)
    if lax.axis_size("dp") > 2 * SECOND:
        left, right = sum_over_rest(add(left, left_got)), sum_over_rest(add(right, right_got))
        sides = [(left,), (right,)]
    else:
        sides = [(left, left_got), (right, right_got)]
    near_send, near = near_halves(at, sides)
    near_got = pair_permute(near_send, 1, "sp")
    late_got = after(late_got, near)
    own_quarter, *other_quarters = quarters(at, late_keep, late_got)
    quarter_parts = [own_quarter] + [
        pair_permute(p, bit)
        for p, bit in zip(other_quarters, (SECOND, FIRST, FIRST + SECOND))
    ]
    output = hand_over(after(output, own_quarter))
    near_got, hidden_grad = after((near_got, hidden_grad), output)
    near_got = after(near_got, hidden_grad)
    upper = me // 2
    far_send = add(pick(near, 1 - upper), pick(near_got, 1 - upper))
    far = add(pick(near, upper), pick(near_got, upper))
    far_got = pair_permute(far_send, 2, "sp")
    quarter_parts = after(quarter_parts, far, far_send)
    if lax.axis_size("dp") > 2 * SECOND:
        total = sum(p.astype(f32) for p in quarter_parts).astype(bf16)
        quarter_parts = [sum_over_rest(total)]
    late_near_send, late_near = near_halves(at, [quarter_parts])
    late_near_got = pair_permute(late_near_send, 1, "sp")
    early_own = add(far, after(far_got, late_near))
    early_four = spread(early_own)
    late_near_got = after(late_near_got, early_own)
    late_far_send = add(pick(late_near, 1 - upper), pick(late_near_got, 1 - upper))
    late_far = add(pick(late_near, upper), pick(late_near_got, upper))
    late_far_got = pair_permute(late_far_send, 2, "sp")
    late_own = add(late_far, late_far_got)
    hidden_grad = after(hidden_grad, late_own).astype(f32)
    time_rows = after(time_row, late_own)
    for bit in bits("sp"):
        time_rows = double(time_rows, bit, "sp")
    time_grad = jnp.concatenate([pick(time_rows, me ^ s)[None] for s in range(sp)], axis=0)
    time_grad = time_grad.astype(f32)
    early_half = four_chips(at, after(early_four, late_own, time_rows, hidden_grad), True)
    early_other = pair_permute(early_half, CORE)
    late_four = spread(after(late_own, early_half))
    n_row, n_col = row_keep.shape[1] // 2, col_keep.shape[1] // 2
    row_starts = [x * (n_row + n_col) + i for x in range(2) for i in range(0, n_row, half)]
    col_starts = [x * (n_row + n_col) + n_row + i for x in range(2) for i in range(0, n_col, half)]
    down_grad, up_grad, proj_grad, early_vectors = finish(
        core,
        early_half,
        after(early_other, late_four[0]),
        half,
        (
            (sp, 1, row_starts),
            (1, n_up, col_starts[:n_up]),
            (1, 1, col_starts[n_up : n_up + 1]),
            (1, 1, col_starts[n_up + 1 :]),
        ),
    )
    late_half = four_chips(at, after(late_four, down_grad), False)
    late_other = pair_permute(late_half, CORE)
    qkv_grad, ada_weight_grad, *small = late_finish(
        core, late_half, late_other, early_vectors, half, cond, sp
    )
    ada_bias_grad, attn_gain_grad, mlp_gain_grad, up_bias_grad, down_bias_grad = (
        v.reshape(-1) for v in small
    )
    return (
        output,
        hidden_grad,
        time_grad,
        ada_weight_grad,
        ada_bias_grad,
        attn_gain_grad,
        qkv_grad,
        proj_grad,
        mlp_gain_grad,
        up_grad,
        up_bias_grad,
        down_grad,
        down_bias_grad,
    )


def solution(mesh):
    return jax.shard_map(
        body,
        mesh=mesh,
        in_specs=(P("dp", "sp", None), P("dp", None)) + (P(),) * 10 + (P("dp", "sp", None),),
        out_specs=(
            P("dp", "sp", None),
            P("dp", "sp", None),
            P("dp", None),
            P("sp", None),
            P("sp"),
            P("sp"),
            P("sp", None),
            P("sp", None),
            P("sp"),
            P("sp", None),
            P("sp"),
            P("sp", None),
            P("sp"),
        ),
        check_vma=False,
    )
```
